32 devices in a mesh: groups: 2 (over y), space: 4 (over z), disp: 4 (over x, core).
Axes of the slice: x: 2, y: 2, z: 4, core: 2. Of those that a mesh axis runs over, the one named last changes fastest.
Arguments:
- volume: bfloat16 [8, 16, 32, 256], P(None, 'disp', ('groups', 'space')), parts along dimension 2, may hold values from -6 to 6
- w_first: bfloat16 [3, 3, 3, 8, 8], replicated, may hold values from -0.4375 to 0.4375
- b_first: float32 [8], replicated, may hold values from -1 to 1
- w_second: bfloat16 [3, 3, 3, 8], replicated, may hold values from -0.4375 to 0.4375
- prior_logits: float32 [16, 32, 256], P('disp', ('groups', 'space')), parts along dimension 1, may hold values from -15 to 310
- cotangent: float32 [32, 256], P(('groups', 'space')), parts along dimension 0, may hold values from -24 to 24
Outputs:
- grad_volume: bfloat16 [8, 16, 32, 256], P(None, 'disp', ('groups', 'space')), parts along dimension 2
- grad_w_first: float32 [3, 3, 3, 16, 8], P(None, None, None, 'groups'), parts along dimension 3
- grad_b_first: float32 [16], P('groups'), parts along dimension 0
- grad_w_second: float32 [3, 3, 3, 16], P(None, None, None, 'groups'), parts along dimension 3
- disparity: float32 [32, 256], P(('groups', 'space')), parts along dimension 0
The draws below stay inside these ranges and needn't reach their ends.
There are 2 independent parts, one for each index of `groups`. The reference program is written for one: setup_inputs(seed, part) draws one part's arguments, and reference() takes and returns one part's arrays. A program takes and returns all parts, laid end to end along the dimension named above; an argument that names none is the same for every part. Nothing has to cross between parts.
All inputs are finite; a program needn't handle non-finite values.
Results may differ from the reference program's by a relative error of at most 0.011.
Values may be sent and summed in bfloat16 or wider, within the bound.
No kernel may reach another device: no remote copies, remote signals or barrier semaphores. Data moves between devices by JAX's collectives and lax.ppermute only.
A program may use at most 64 MiB of HBM per device.

```python
import math
import jax
import jax.numpy as jnp
from jax import lax

C = 8
W = 256
DISP = 16
H = 16


def draw_prior_logits(key, part):
    key_list = jax.random.split(key, 1)
    return jnp.clip(3.0 * jax.random.normal(key_list[0], (DISP, H, W), jnp.float32), -15.0, 15.0)


def level_of(key, extent, pieces, smallest, largest):
    level, own = 1.0, jax.random.fold_in(key, 6)
    for axis_at, blocks in pieces:
        heights = jnp.exp(jax.random.uniform(jax.random.fold_in(own, axis_at), (blocks,), jnp.float32, smallest / len(pieces), largest / len(pieces)))
        level = level * jnp.repeat(heights, extent[axis_at] // blocks).reshape([-1 if axis == axis_at else 1 for axis in range(len(extent))])
    return level


def gaussian(own_key, extent, width, reach, pieces=(), dtype=jnp.bfloat16):
    values = jax.random.normal(own_key, extent, jnp.float32) * width
    if len(pieces) > 0:
        values = level_of(own_key, extent, pieces, -0.22, 0.18) * values
    return jnp.clip(values, min=-reach, max=reach).astype(dtype)


def setup_inputs(seed: int = 0, part: int = 0) -> dict:
    streams_of = jax.random.split(jax.random.key(seed), 7)
    own_keys = jax.random.split(jax.random.fold_in(streams_of[6], part), 7)
    volume = gaussian(own_keys[0], (C, DISP, H, W), 1.0, 6.0, ((1, 4), (2, 4)))
    w_first = gaussian(streams_of[1], (3, 3, 3, C, C), (27 * C) ** -0.5, 0.4375)
    b_first = jnp.clip(jax.random.uniform(streams_of[2], (C,), jnp.float32, -1.0, 1.0), -1.0, 1.0)
    w_second = gaussian(streams_of[3], (3, 3, 3, C), (27 * C) ** -0.5, 0.4375)
    prior_logits = draw_prior_logits(jax.random.fold_in(jax.random.fold_in(streams_of[6], part), 71), part)
    cotangent = gaussian(own_keys[5], (H, W), 4.0, 24.0, ((0, 4),), jnp.float32)
    return dict(volume=volume, w_first=w_first, b_first=b_first, w_second=w_second, prior_logits=prior_logits, cotangent=cotangent)


def correlate(source, kernel):
    return lax.conv_general_dilated(source[None], kernel, (1, 1, 1), ((1, 1), (1, 1), (1, 1)), dimension_numbers=('NCDHW', 'DHWOI', 'NCDHW'), precision=lax.Precision.HIGHEST)[0]

def reference(volume, w_first, b_first, w_second, prior_logits, cotangent):
    source = volume.astype(jnp.float32)
    first_kernel = w_first.astype(jnp.float32)
    second_kernel = w_second.astype(jnp.float32)[:, :, :, None, :]
    pre_act = correlate(source, first_kernel) + b_first[:, None, None, None]
    hidden = jax.nn.silu(pre_act).astype(jnp.bfloat16)
    hidden_wide = hidden.astype(jnp.float32)
    logits = correlate(hidden_wide, second_kernel)[0] + prior_logits
    highest = lax.optimization_barrier(jnp.max(logits, axis=0))
    weights_exp = jnp.exp(logits - highest[None])
    summed = lax.optimization_barrier(jnp.sum(weights_exp, axis=0))
    position = ((jnp.arange(DISP).astype(jnp.float32) + 0.5) / DISP)[:, None, None]
    disparity = lax.optimization_barrier(jnp.sum(weights_exp * position, axis=0)) / summed
    probability = weights_exp / summed[None]
    score_grad = (cotangent[None] * probability * (position - disparity[None])).astype(jnp.bfloat16)
    unused_second, second_pull = jax.vjp(correlate, hidden_wide, second_kernel)
    hidden_grad, second_grad = second_pull(score_grad.astype(jnp.float32)[None])
    gate_sigmoid = jax.nn.sigmoid(pre_act)
    pre_grad = (hidden_grad * gate_sigmoid * (1.0 + pre_act * (1.0 - gate_sigmoid))).astype(jnp.bfloat16)
    pre_wide = pre_grad.astype(jnp.float32)
    unused_first, first_pull = jax.vjp(correlate, source, first_kernel)
    volume_grad, first_grad = first_pull(pre_wide)
    grad_scale = 16.0 / math.sqrt(DISP * H * W)
    bias_grad = lax.optimization_barrier(jnp.sum(pre_wide, axis=(1, 2, 3)))
    return (volume_grad.astype(jnp.bfloat16), first_grad * grad_scale, bias_grad * grad_scale, second_grad[:, :, :, 0, :] * grad_scale, disparity)
```

```python
import functools
import math

import jax
import jax.numpy as jnp
from jax import lax
from jax.experimental import pallas as pl
from jax.experimental.pallas import tpu as pltpu
from jax.sharding import PartitionSpec as P

F32 = jnp.float32
BF16 = jnp.bfloat16


def swap_pairs(count, step):
    pairs = []
    for i in range(count):
        j = i ^ 1 if step == 0 else ((i + 1) ^ 1) - 1
        pairs.append((i, j if 0 <= j < count else i))
    return pairs


def partners(value, axis):
    count = lax.axis_size(axis)
    return [lax.ppermute(value, axis, [(i, i ^ s) for i in range(count)]) for s in range(1, count)]


def radix_stages(count):
    stages = []
    bit = 1
    while bit < count:
        if bit * 4 <= count:
            stages.append((bit, 2 * bit, 3 * bit))
            bit *= 4
        else:
            stages.append((bit,))
            bit *= 2
    return stages


def shift_up(x, lane):
    return jnp.where(lane == 0, 0.0, pltpu.roll(x, 1, 1))


def shift_down(x, lane):
    width = x.shape[1]
    return jnp.where(lane == width - 1, 0.0, pltpu.roll(x, width - 1, 1))


def left(x, amount):
    return x if amount == 0 else pltpu.roll(x, x.shape[1] - amount, 1)


def right(x, amount):
    return x if amount == 0 else pltpu.roll(x, amount, 1)


def dot(a, b):
    return lax.dot_general(a, b, (((1,), (0,)), ((), ())), preferred_element_type=F32)


def dot_t(a, b):
    return lax.dot_general(a, b, (((1,), (1,)), ((), ())), preferred_element_type=F32)


def forward_body(
    dims, mid_ref, da_ref, db_ref, ex_ref, exa_ref, exb_ref, base1_ref, bias_ref, base2_ref,
    logits_ref, slope_ref, hid_ref, xs_ref, cot_ref, x_ref, h_ref, prior_ref
):
    planes, rows, chans, width, disp, space = dims
    zi = lax.axis_index("space")
    di = lax.axis_index("disp")
    z_even = zi % 2 == 0
    d_even = di % 2 == 0
    xr = (rows + 8) * chans
    hr = (rows + 6) * chans
    lane = lax.broadcasted_iota(jnp.int32, (hr, width), 1)

    x_ref[2 * xr : (planes + 2) * xr, :] = mid_ref[...].reshape(planes * xr, width)

    def place(at, size, ok, first, one, two):
        @pl.when(ok & first)
        def _():
            x_ref[at : at + size, :] = one[...].reshape(size, width)

        @pl.when(ok & jnp.logical_not(first))
        def _():
            x_ref[at : at + size, :] = two[...].reshape(size, width)

        @pl.when(jnp.logical_not(ok))
        def _():
            x_ref[at : at + size, :] = jnp.zeros((size, width), BF16)

    place(0, 2 * xr, di > 0, d_even, db_ref, da_ref)
    place((planes + 2) * xr, 2 * xr, di < disp - 1, d_even, da_ref, db_ref)

    zero2 = jnp.zeros((2, width), F32)

    def extras(ok, first, one, two, row, at):
        def put(src):
            for p in range(planes):
                prior_ref[p, at : at + 2, :] = zero2 if src is None else src[p * rows + row : p * rows + row + 2, :]
            base = planes * rows + row
            cot_ref[at : at + 2, :] = zero2 if src is None else src[base : base + 2, :]

        pl.when(ok & first)(lambda: put(one))
        pl.when(ok & jnp.logical_not(first))(lambda: put(two))
        pl.when(jnp.logical_not(ok))(lambda: put(None))

    for p in range(planes):
        prior_ref[p, 2 : 2 + rows, :] = ex_ref[p * rows : (p + 1) * rows, :]
    cot_ref[2 : 2 + rows, :] = ex_ref[planes * rows : (planes + 1) * rows, :]
    extras(zi > 0, z_even, exb_ref, exa_ref, rows - 2, 0)
    extras(zi < space - 1, z_even, exa_ref, exb_ref, 0, rows + 2)

    bands = []
    base1 = base1_ref[...]
    for c in range(3):
        piece = base1[c * chans : (c + 1) * chans]
        for r in range(rows + 6):
            bands.append(right(piece, chans * r))
    band1 = jnp.concatenate(bands, axis=0)[:, : 3 * xr].astype(BF16)
    bias = jnp.concatenate([bias_ref[...]] * (rows + 6), axis=0)
    row_at = zi * rows - 3 + lax.broadcasted_iota(jnp.int32, (hr, width), 0) // chans
    row_ok = ((row_at >= 0) & (row_at < space * rows)).astype(F32)
    for p in range(planes + 2):
        y = dot(band1, x_ref[p * xr : (p + 3) * xr, :])
        pre = y[hr : 2 * hr] + shift_up(y[:hr], lane) + shift_down(y[2 * hr :], lane) + bias
        sig = jax.nn.sigmoid(pre)
        plane_at = di * planes - 1 + p
        ok = row_ok * ((plane_at >= 0) & (plane_at < disp * planes)).astype(F32)
        hidden = (pre * sig * ok).astype(BF16)
        h_ref[p * hr : (p + 1) * hr, :] = hidden
        inner = slice(2 * chans, hr - 2 * chans)
        slope_ref[p] = (sig * (1.0 + pre * (1.0 - sig)) * ok)[inner]
        hid_ref[p] = h_ref[p * hr + chans : (p + 1) * hr - chans, :]
        xs_ref[p] = x_ref[(p + 1) * xr + 2 * chans : (p + 2) * xr - 2 * chans, :]
    hid_ref[planes + 2] = jnp.zeros(hid_ref.shape[1:], BF16)
    xs_ref[planes + 2] = jnp.zeros(xs_ref.shape[1:], BF16)

    lr = rows + 4
    lane2 = lax.broadcasted_iota(jnp.int32, (lr, width), 1)
    bands = []
    for c in range(3):
        piece = base2_ref[c : c + 1, :]
        for r in range(lr):
            bands.append(right(piece, chans * r))
    band2 = jnp.concatenate(bands, axis=0)[:, : 3 * hr].astype(BF16)
    for p in range(planes):
        y = dot(band2, h_ref[p * hr : (p + 3) * hr, :])
        logits_ref[p * lr : (p + 1) * lr, :] = (
            y[lr : 2 * lr] + shift_up(y[:lr], lane2) + shift_down(y[2 * lr :], lane2) + prior_ref[p]
        )


def backward_body(dims, *refs):
    planes, rows, chans, width, disp, space = dims
    logit_refs = refs[:disp]
    cot_ref, slope_ref, hid_ref, xs_ref, base3_ref = refs[disp : disp + 5]
    pay_ref, pg_ref, disp_ref, l_ref, s_ref = refs[disp + 5 :]
    di = lax.axis_index("disp")
    lr = rows + 4
    hr = (rows + 2) * chans
    total = planes * disp
    lane = lax.broadcasted_iota(jnp.int32, (lr, width), 1)

    l_ref[0] = jnp.zeros(l_ref.shape[1:], F32)
    l_ref[disp + 1] = jnp.zeros(l_ref.shape[1:], F32)
    for s in range(disp):
        l_ref[(di ^ s) + 1] = logit_refs[s][...]

    def logit(g, p):
        return l_ref[g, p * lr : (p + 1) * lr, :]

    top = logit(1, 0)
    for k in range(1, total):
        top = jnp.maximum(top, logit(1 + k // planes, k % planes))
    summed = jnp.zeros((lr, width), F32)
    moment = jnp.zeros((lr, width), F32)
    for k in range(total):
        e = jnp.exp(logit(1 + k // planes, k % planes) - top)
        summed = summed + e
        moment = moment + e * ((k + 0.5) / total)
    disparity = moment / summed
    disp_ref[...] = disparity[2 : 2 + rows]
    coef = cot_ref[...] / summed
    scores = []
    for k in range(planes + 4):
        at = di * planes - 2 + k
        group = di + (0 if k < 2 else 1 if k < 2 + planes else 2)
        e = jnp.exp(logit(group, (k - 2) % planes) - top)
        ok = ((at >= 0) & (at < total)).astype(F32)
        position = (at.astype(F32) + 0.5) / total
        score = jnp.where(ok > 0.0, coef * e * (position - disparity), 0.0).astype(BF16)
        scores.append(score.astype(F32))
    s_all = jnp.concatenate(scores, axis=0).astype(BF16)

    lane_h = lax.broadcasted_iota(jnp.int32, (hr, width), 1)
    base3 = base3_ref[...]
    rhs_rows = (rows + 4) * chans
    acc1 = None
    acc2 = None
    bias = jnp.zeros((chans, width), F32)
    for p in range(planes + 2):
        bands = []
        for c in range(3):
            piece = base3[c * chans : (c + 1) * chans]
            for r in range(rows + 2):
                bands.append(right(piece, lr * p + r))
        band3 = jnp.concatenate(bands, axis=0)[:, : (planes + 4) * lr].astype(BF16)
        y = dot(band3, s_all)
        hg = y[hr : 2 * hr] + shift_down(y[:hr], lane_h) + shift_up(y[2 * hr :], lane_h)
        pg = (hg * slope_ref[p]).astype(BF16)
        pg_ref[p] = pg
        if p == 0 or p == planes + 1:
            continue
        k = p - 1
        own = pg.astype(F32)[chans : chans * (rows + 1)]
        lane_o = lane_h[: own.shape[0]]
        moved = (shift_down(own, lane_o), own, shift_up(own, lane_o))
        pieces = []
        for r in range(rows):
            bias = bias + own[r * chans : (r + 1) * chans]
            for c in range(3):
                pieces.append(moved[c][r * chans : (r + 1) * chans])
        lhs = jnp.concatenate(pieces, axis=0).astype(BF16)
        rhs = xs_ref[k : k + 4].reshape(4 * rhs_rows, width)
        part = dot_t(lhs, rhs)
        acc1 = part if acc1 is None else acc1 + part
        sc = scores[k + 2]
        lhs = jnp.concatenate([shift_down(sc, lane), sc, shift_up(sc, lane)], axis=0).astype(BF16)
        part = dot_t(lhs, hid_ref[k : k + 4].reshape(4 * rhs_rows, width))
        acc2 = part if acc2 is None else acc2 + part

    out1 = jnp.zeros((3 * chans, 4 * rhs_rows), F32)
    for r in range(rows):
        out1 = out1 + left(acc1[3 * chans * r : 3 * chans * (r + 1)], chans * (r + 1))
    row_in = lax.broadcasted_iota(jnp.int32, acc2.shape, 0) % lr
    out2 = jnp.zeros(acc2.shape, F32)
    for r in range(2, 2 + rows):
        out2 = out2 + jnp.where(row_in == r, left(acc2, chans * (r - 1)), 0.0)
    out2 = jnp.concatenate(
        [jnp.sum(out2[c * lr : (c + 1) * lr], axis=0, keepdims=True) for c in range(3)]
        + [jnp.zeros((5, out2.shape[1]), F32)],
        axis=0,
    )
    out = jnp.concatenate([out1, out2], axis=0)
    lane_p = lax.broadcasted_iota(jnp.int32, (out.shape[0], 128), 1)
    tap = 3 * chans
    packed = jnp.zeros((out.shape[0], 128), F32)
    for a in range(3):
        moved = left(out, a * (rhs_rows - tap))[:, :128]
        packed = jnp.where((lane_p >= a * tap) & (lane_p < (a + 1) * tap), moved, packed)
    bias = jnp.sum(bias, axis=1, keepdims=True)
    sub = lax.broadcasted_iota(jnp.int32, (chans, 128), 0)
    lane_b = lax.broadcasted_iota(jnp.int32, (chans, 128), 1)
    bias = jnp.sum(jnp.where(sub == lane_b, bias, 0.0), axis=0, keepdims=True)
    pay_ref[...] = packed
    pay_ref[3 * chans + 3 : 3 * chans + 4, :] = bias


def volume_grad_body(dims, pg_ref, base4_ref, out_ref):
    planes, rows, chans, width, disp, space = dims
    hr = (rows + 2) * chans
    n = rows * chans
    lane = lax.broadcasted_iota(jnp.int32, (n, width), 1)
    base4 = base4_ref[...]
    bands = []
    for c in range(3):
        piece = base4[c * chans : (c + 1) * chans]
        for r in range(rows):
            bands.append(right(piece, chans * r))
    band4 = jnp.concatenate(bands, axis=0)[:, : 3 * hr].astype(BF16)
    for p in range(planes):
        y = dot(band4, pg_ref[p : p + 3].reshape(3 * hr, width))
        out_ref[p] = (
            y[n : 2 * n] + shift_down(y[:n], lane) + shift_up(y[2 * n :], lane)
        ).astype(BF16)


def finish_body(chans, scale, *refs):
    parts = refs[:-3]
    gw_ref, gb_ref, gs_ref = refs[-3:]
    sums = [r[...] for r in parts]
    while len(sums) > 1:
        sums = [sums[k] + sums[k + 1] for k in range(0, len(sums), 2)]
    total = sums[0] * scale
    for a in range(3):
        for b in range(3):
            at = (a * 3 + b) * chans
            for c in range(3):
                gw_ref[a, b, c] = total[c * chans : (c + 1) * chans, at : at + chans]
            gs_ref[a, b] = total[3 * chans : 3 * chans + 3, at : at + chans]
    gb_ref[...] = total[3 * chans + 3 : 3 * chans + 4, :chans]


def tree_sum(parts):
    while len(parts) > 1:
        parts = [parts[k] + parts[k + 1] for k in range(0, len(parts), 2)]
    return parts[0]


def shards(volume, w_first, b_first, w_second, prior_logits, cotangent):
    chans, planes, rows, width = volume.shape
    disp = lax.axis_size("disp")
    space = lax.axis_size("space")
    dims = (planes, rows, chans, width, disp, space)
    zi = lax.axis_index("space")
    di = lax.axis_index("disp")

    own = jnp.transpose(volume, (1, 2, 0, 3)).reshape(planes, rows * chans, width)
    z_one = lax.ppermute(own, "space", swap_pairs(space, 0))
    z_two = lax.ppermute(own, "space", swap_pairs(space, 1))
    extra = jnp.concatenate([prior_logits.reshape(planes * rows, width), cotangent], axis=0)
    e_one = lax.ppermute(extra, "space", swap_pairs(space, 0))
    e_two = lax.ppermute(extra, "space", swap_pairs(space, 1))
    z_even = zi % 2 == 0
    zero = jnp.zeros((), BF16)
    above = jnp.where(zi > 0, jnp.where(z_even, z_two, z_one), zero)
    below = jnp.where(zi < space - 1, jnp.where(z_even, z_one, z_two), zero)
    mid = jnp.concatenate([above, own, below], axis=1)
    even = (di % 2 == 0).astype(jnp.int32)
    d_one = lax.ppermute(
        lax.dynamic_slice_in_dim(mid, (planes - 2) * even, 2, axis=0), "disp", swap_pairs(disp, 0)
    )
    d_two = lax.ppermute(
        lax.dynamic_slice_in_dim(mid, (planes - 2) * (1 - even), 2, axis=0), "disp", swap_pairs(disp, 1)
    )

    xr = rows + 8
    base1 = jnp.transpose(w_first, (2, 3, 0, 1, 4)).astype(F32)
    base1 = jnp.pad(base1, ((0, 0), (0, 0), (0, 0), (0, xr - 3), (0, 0))).reshape(3 * chans, 3 * xr * chans)
    base1 = jnp.pad(base1, ((0, 0), (0, -base1.shape[1] % 128)))
    base2 = jnp.transpose(w_second, (2, 0, 1, 3)).astype(F32)
    base2 = jnp.pad(base2, ((0, 0), (0, 0), (0, rows + 3), (0, 0))).reshape(3, 3 * (rows + 6) * chans)
    base2 = jnp.pad(base2, ((0, 5), (0, -base2.shape[1] % 128)))
    base3 = jnp.transpose(w_second[::-1, ::-1], (2, 3, 0, 1)).astype(F32)
    base3 = jnp.pad(base3, ((0, 0), (0, 0), (0, 0), (0, rows + 1))).reshape(3 * chans, 3 * (rows + 4))
    base3 = jnp.pad(base3, ((0, 0), (0, 128 - base3.shape[1])))
    base4 = jnp.transpose(w_first[::-1, ::-1], (2, 4, 0, 1, 3)).astype(F32)
    base4 = jnp.pad(base4, ((0, 0), (0, 0), (0, 0), (0, rows - 1), (0, 0))).reshape(
        3 * chans, 3 * (rows + 2) * chans
    )
    base4 = jnp.pad(base4, ((0, 0), (0, -base4.shape[1] % 128)))

    lr = rows + 4
    hr = rows + 6
    logits, slope, hid, xs, cot = pl.pallas_call(
        functools.partial(forward_body, dims),
        out_shape=(
            jax.ShapeDtypeStruct((planes * lr, width), F32),
            jax.ShapeDtypeStruct((planes + 2, (rows + 2) * chans, width), F32),
            jax.ShapeDtypeStruct((planes + 3, (rows + 4) * chans, width), BF16),
            jax.ShapeDtypeStruct((planes + 3, (rows + 4) * chans, width), BF16),
            jax.ShapeDtypeStruct((lr, width), F32),
        ),
        scratch_shapes=[
            pltpu.VMEM(((planes + 4) * xr * chans, width), BF16),
            pltpu.VMEM(((planes + 2) * hr * chans, width), BF16),
            pltpu.VMEM((planes, lr, width), F32),
        ],
        name="forward",
    )(mid, d_one, d_two, extra, e_one, e_two, base1, b_first[:, None], base2)

    pieces = [logits] + partners(logits, "disp")
    pay, pg, disparity = pl.pallas_call(
        functools.partial(backward_body, dims),
        out_shape=(
            jax.ShapeDtypeStruct((3 * chans + 8, 128), F32),
            jax.ShapeDtypeStruct((planes + 2, (rows + 2) * chans, width), BF16),
            jax.ShapeDtypeStruct((rows, width), F32),
        ),
        scratch_shapes=[
            pltpu.VMEM((disp + 2, planes * lr, width), F32),
            pltpu.VMEM(((planes + 4) * lr, width), F32),
        ],
        name="backward",
    )(*pieces, cot, slope, hid, xs, base3)

    stages = [("disp", s) for s in radix_stages(disp)] + [("space", s) for s in radix_stages(space)]
    for n, (axis, steps) in enumerate(stages):
        count = lax.axis_size(axis)
        parts = [pay] + [lax.ppermute(pay, axis, [(i, i ^ s) for i in range(count)]) for s in steps]
        if n < len(stages) - 1:
            pay = tree_sum(parts)

    volume_grad = pl.pallas_call(
        functools.partial(volume_grad_body, dims),
        out_shape=jax.ShapeDtypeStruct((planes, rows * chans, width), BF16),
        name="volume_grad",
    )(pg, base4)
    volume_grad = jnp.transpose(volume_grad.reshape(planes, rows, chans, width), (2, 0, 1, 3))

    scale = 16.0 / math.sqrt(planes * disp * rows * space * width)
    first_sum, bias_sum, second_sum = pl.pallas_call(
        functools.partial(finish_body, chans, scale),
        out_shape=(
            jax.ShapeDtypeStruct((3, 3, 3, chans, chans), F32),
            jax.ShapeDtypeStruct((1, chans), F32),
            jax.ShapeDtypeStruct((3, 3, 3, chans), F32),
        ),
        name="finish",
    )(*parts)
    return (volume_grad, first_sum, bias_sum[0], second_sum, disparity)


def solution(mesh):
    return jax.shard_map(
        shards,
        mesh=mesh,
        in_specs=(
            P(None, "disp", ("groups", "space"), None),
            P(),
            P(),
            P(),
            P("disp", ("groups", "space"), None),
            P(("groups", "space"), None),
        ),
        out_specs=(
            P(None, "disp", ("groups", "space"), None),
            P(None, None, None, "groups", None),
            P("groups"),
            P(None, None, None, "groups"),
            P(("groups", "space"), None),
        ),
        check_vma=False,
    )
```

```python
import functools
import math

import jax
import jax.numpy as jnp
from jax import lax
from jax.experimental import pallas as pl
from jax.experimental.pallas import tpu as pltpu
from jax.sharding import PartitionSpec as P

F32 = jnp.float32
BF16 = jnp.bfloat16


def swap_pairs(count, step):
    pairs = []
    for i in range(count):
        j = i ^ 1 if step == 0 else ((i + 1) ^ 1) - 1
        pairs.append((i, j if 0 <= j < count else i))
    return pairs


def partners(value, axis):
    count = lax.axis_size(axis)
    return [lax.ppermute(value, axis, [(i, i ^ s) for i in range(count)]) for s in range(1, count)]


def radix_stages(count):
    stages = []
    bit = 1
    while bit < count:
        if bit * 4 <= count:
            stages.append((bit, 2 * bit, 3 * bit))
            bit *= 4
        else:
            stages.append((bit,))
            bit *= 2
    return stages


def shift_up(x, lane):
    return jnp.where(lane == 0, 0.0, pltpu.roll(x, 1, 1))


def shift_down(x, lane):
    width = x.shape[1]
    return jnp.where(lane == width - 1, 0.0, pltpu.roll(x, width - 1, 1))


def left(x, amount):
    return x if amount == 0 else pltpu.roll(x, x.shape[1] - amount, 1)


def right(x, amount):
    return x if amount == 0 else pltpu.roll(x, amount, 1)


def call(body, name, outs, *operands, scratch=()):
    operands = [pltpu.with_memory_space_constraint(x, pltpu.VMEM) for x in operands]
    return pl.pallas_call(
        body,
        out_shape=tuple(
            pltpu.VMEM(shape, dtype) if inside else jax.ShapeDtypeStruct(shape, dtype)
            for shape, dtype, inside in outs
        ),
        in_specs=[pl.BlockSpec(memory_space=pltpu.VMEM)] * len(operands),
        out_specs=tuple(pl.BlockSpec(memory_space=pltpu.VMEM) for _ in outs),
        scratch_shapes=list(scratch),
        name=name,
    )(*operands)


def dot(a, b):
    return lax.dot_general(a, b, (((1,), (0,)), ((), ())), preferred_element_type=F32)


def dot_t(a, b):
    return lax.dot_general(a, b, (((1,), (1,)), ((), ())), preferred_element_type=F32)


def forward_body(
    dims, mid_ref, da_ref, db_ref, ex_ref, exa_ref, exb_ref, base1_ref, bias_ref, base2_ref,
    logits_ref, slope_ref, hid_ref, xs_ref, cot_ref, x_ref, h_ref, prior_ref
):
    planes, rows, chans, width, disp, space = dims
    zi = lax.axis_index("space")
    di = lax.axis_index("disp")
    z_even = zi % 2 == 0
    d_even = di % 2 == 0
    xr = (rows + 8) * chans
    hr = (rows + 6) * chans
    lane = lax.broadcasted_iota(jnp.int32, (hr, width), 1)

    x_ref[2 * xr : (planes + 2) * xr, :] = mid_ref[...].reshape(planes * xr, width)

    def place(at, size, ok, first, one, two):
        @pl.when(ok & first)
        def _():
            x_ref[at : at + size, :] = one[...].reshape(size, width)

        @pl.when(ok & jnp.logical_not(first))
        def _():
            x_ref[at : at + size, :] = two[...].reshape(size, width)

        @pl.when(jnp.logical_not(ok))
        def _():
            x_ref[at : at + size, :] = jnp.zeros((size, width), BF16)

    place(0, 2 * xr, di > 0, d_even, db_ref, da_ref)
    place((planes + 2) * xr, 2 * xr, di < disp - 1, d_even, da_ref, db_ref)

    zero2 = jnp.zeros((2, width), F32)

    def extras(ok, first, one, two, row, at):
        def put(src):
            for p in range(planes):
                prior_ref[p, at : at + 2, :] = zero2 if src is None else src[p * rows + row : p * rows + row + 2, :]
            base = planes * rows + row
            cot_ref[at : at + 2, :] = zero2 if src is None else src[base : base + 2, :]

        pl.when(ok & first)(lambda: put(one))
        pl.when(ok & jnp.logical_not(first))(lambda: put(two))
        pl.when(jnp.logical_not(ok))(lambda: put(None))

    for p in range(planes):
        prior_ref[p, 2 : 2 + rows, :] = ex_ref[p * rows : (p + 1) * rows, :]
    cot_ref[2 : 2 + rows, :] = ex_ref[planes * rows : (planes + 1) * rows, :]
    extras(zi > 0, z_even, exb_ref, exa_ref, rows - 2, 0)
    extras(zi < space - 1, z_even, exa_ref, exb_ref, 0, rows + 2)

    bands = []
    base1 = base1_ref[...]
    for c in range(3):
        piece = base1[c * chans : (c + 1) * chans]
        for r in range(rows + 6):
            bands.append(right(piece, chans * r))
    band1 = jnp.concatenate(bands, axis=0)[:, : 3 * xr].astype(BF16)
    diag = lax.broadcasted_iota(jnp.int32, (chans, chans), 0) == lax.broadcasted_iota(
        jnp.int32, (chans, chans), 1
    )
    bias = jnp.sum(jnp.where(diag, bias_ref[...], 0.0), axis=1, keepdims=True)
    bias = jnp.concatenate([jnp.broadcast_to(bias, (chans, width))] * (rows + 6), axis=0)
    row_at = zi * rows - 3 + lax.broadcasted_iota(jnp.int32, (hr, width), 0) // chans
    row_ok = ((row_at >= 0) & (row_at < space * rows)).astype(F32)
    for p in range(planes + 2):
        y = dot(band1, x_ref[p * xr : (p + 3) * xr, :])
        pre = y[hr : 2 * hr] + shift_up(y[:hr], lane) + shift_down(y[2 * hr :], lane) + bias
        sig = jax.nn.sigmoid(pre)
        plane_at = di * planes - 1 + p
        ok = row_ok * ((plane_at >= 0) & (plane_at < disp * planes)).astype(F32)
        hidden = (pre * sig * ok).astype(BF16)
        h_ref[p * hr : (p + 1) * hr, :] = hidden
        inner = slice(2 * chans, hr - 2 * chans)
        slope_ref[p] = (sig * (1.0 + pre * (1.0 - sig)) * ok)[inner]
        hid_ref[p] = h_ref[p * hr + chans : (p + 1) * hr - chans, :]
        xs_ref[p] = x_ref[(p + 1) * xr + 2 * chans : (p + 2) * xr - 2 * chans, :]
    hid_ref[planes + 2] = jnp.zeros(hid_ref.shape[1:], BF16)
    xs_ref[planes + 2] = jnp.zeros(xs_ref.shape[1:], BF16)

    lr = rows + 4
    lane2 = lax.broadcasted_iota(jnp.int32, (lr, width), 1)
    bands = []
    for c in range(3):
        piece = base2_ref[c : c + 1, :]
        for r in range(lr):
            bands.append(right(piece, chans * r))
    band2 = jnp.concatenate(bands, axis=0)[:, : 3 * hr].astype(BF16)
    for p in range(planes):
        y = dot(band2, h_ref[p * hr : (p + 3) * hr, :])
        logits_ref[p * lr : (p + 1) * lr, :] = (
            y[lr : 2 * lr] + shift_up(y[:lr], lane2) + shift_down(y[2 * lr :], lane2) + prior_ref[p]
        )


def backward_body(dims, *refs):
    planes, rows, chans, width, disp, space = dims
    logit_refs = refs[:disp]
    cot_ref, slope_ref, hid_ref, xs_ref, base3_ref = refs[disp : disp + 5]
    pay_ref, pg_ref, disp_ref, l_ref = refs[disp + 5 :]
    di = lax.axis_index("disp")
    lr = rows + 4
    hr = (rows + 2) * chans
    total = planes * disp
    lane = lax.broadcasted_iota(jnp.int32, (lr, width), 1)

    l_ref[0] = jnp.zeros(l_ref.shape[1:], F32)
    l_ref[disp + 1] = jnp.zeros(l_ref.shape[1:], F32)
    for s in range(disp):
        l_ref[(di ^ s) + 1] = logit_refs[s][...]

    def logit(g, p):
        return l_ref[g, p * lr : (p + 1) * lr, :]

    top = logit(1, 0)
    for k in range(1, total):
        top = jnp.maximum(top, logit(1 + k // planes, k % planes))
    summed = jnp.zeros((lr, width), F32)
    moment = jnp.zeros((lr, width), F32)
    for k in range(total):
        e = jnp.exp(logit(1 + k // planes, k % planes) - top)
        summed = summed + e
        moment = moment + e * ((k + 0.5) / total)
    disparity = moment / summed
    disp_ref[...] = disparity[2 : 2 + rows]
    coef = cot_ref[...] / summed
    scores = []
    for k in range(planes + 4):
        at = di * planes - 2 + k
        group = di + (0 if k < 2 else 1 if k < 2 + planes else 2)
        e = jnp.exp(logit(group, (k - 2) % planes) - top)
        ok = ((at >= 0) & (at < total)).astype(F32)
        position = (at.astype(F32) + 0.5) / total
        score = jnp.where(ok > 0.0, coef * e * (position - disparity), 0.0).astype(BF16)
        scores.append(score.astype(F32))
    s_all = jnp.concatenate(scores, axis=0).astype(BF16)

    lane_h = lax.broadcasted_iota(jnp.int32, (hr, width), 1)
    base3 = base3_ref[...]
    rhs_rows = (rows + 4) * chans
    acc1 = None
    acc2 = None
    bias = jnp.zeros((chans, width), F32)
    for p in range(planes + 2):
        bands = []
        for c in range(3):
            piece = base3[c * chans : (c + 1) * chans]
            for r in range(rows + 2):
                bands.append(right(piece, lr * p + r))
        band3 = jnp.concatenate(bands, axis=0)[:, : (planes + 4) * lr].astype(BF16)
        y = dot(band3, s_all)
        hg = y[hr : 2 * hr] + shift_down(y[:hr], lane_h) + shift_up(y[2 * hr :], lane_h)
        pg = (hg * slope_ref[p]).astype(BF16)
        pg_ref[p] = pg
        if p == 0 or p == planes + 1:
            continue
        k = p - 1
        own = pg.astype(F32)[chans : chans * (rows + 1)]
        lane_o = lane_h[: own.shape[0]]
        moved = (shift_down(own, lane_o), own, shift_up(own, lane_o))
        pieces = []
        for r in range(rows):
            bias = bias + own[r * chans : (r + 1) * chans]
            for c in range(3):
                pieces.append(moved[c][r * chans : (r + 1) * chans])
        lhs = jnp.concatenate(pieces, axis=0).astype(BF16)
        rhs = xs_ref[k : k + 4].reshape(4 * rhs_rows, width)
        part = dot_t(lhs, rhs)
        acc1 = part if acc1 is None else acc1 + part
        sc = scores[k + 2]
        lhs = jnp.concatenate([shift_down(sc, lane), sc, shift_up(sc, lane)], axis=0).astype(BF16)
        part = dot_t(lhs, hid_ref[k : k + 4].reshape(4 * rhs_rows, width))
        acc2 = part if acc2 is None else acc2 + part

    out1 = jnp.zeros((3 * chans, 4 * rhs_rows), F32)
    for r in range(rows):
        out1 = out1 + left(acc1[3 * chans * r : 3 * chans * (r + 1)], chans * (r + 1))
    row_in = lax.broadcasted_iota(jnp.int32, acc2.shape, 0) % lr
    out2 = jnp.zeros(acc2.shape, F32)
    for r in range(2, 2 + rows):
        out2 = out2 + jnp.where(row_in == r, left(acc2, chans * (r - 1)), 0.0)
    out2 = jnp.concatenate(
        [jnp.sum(out2[c * lr : (c + 1) * lr], axis=0, keepdims=True) for c in range(3)]
        + [jnp.zeros((5, out2.shape[1]), F32)],
        axis=0,
    )
    out = jnp.concatenate([out1, out2], axis=0)
    lane_p = lax.broadcasted_iota(jnp.int32, (out.shape[0], 128), 1)
    tap = 3 * chans
    packed = jnp.zeros((out.shape[0], 128), F32)
    for a in range(3):
        moved = left(out, a * (rhs_rows - tap))[:, :128]
        packed = jnp.where((lane_p >= a * tap) & (lane_p < (a + 1) * tap), moved, packed)
    bias = jnp.sum(bias, axis=1, keepdims=True)
    sub = lax.broadcasted_iota(jnp.int32, (chans, 128), 0)
    lane_b = lax.broadcasted_iota(jnp.int32, (chans, 128), 1)
    bias = jnp.sum(jnp.where(sub == lane_b, bias, 0.0), axis=0, keepdims=True)
    pay_ref[...] = packed
    pay_ref[3 * chans + 3 : 3 * chans + 4, :] = bias


def volume_grad_body(dims, pg_ref, base4_ref, out_ref):
    planes, rows, chans, width, disp, space = dims
    hr = (rows + 2) * chans
    n = rows * chans
    lane = lax.broadcasted_iota(jnp.int32, (n, width), 1)
    base4 = base4_ref[...]
    bands = []
    for c in range(3):
        piece = base4[c * chans : (c + 1) * chans]
        for r in range(rows):
            bands.append(right(piece, chans * r))
    band4 = jnp.concatenate(bands, axis=0)[:, : 3 * hr].astype(BF16)
    to = lax.broadcasted_iota(jnp.int32, (3 * n, 3 * n), 0)
    at = lax.broadcasted_iota(jnp.int32, (3 * n, 3 * n), 1)
    source = (to // n) * n + (to % rows) * chans + (to % n) // rows
    band4 = dot((at == source).astype(BF16), band4).astype(BF16)
    for p in range(planes):
        y = dot(band4, pg_ref[p : p + 3].reshape(3 * hr, width))
        y = (y[n : 2 * n] + shift_down(y[:n], lane) + shift_up(y[2 * n :], lane)).astype(BF16)
        for i in range(chans):
            out_ref[i, p] = y[i * rows : (i + 1) * rows]


def finish_body(chans, scale, *refs):
    parts = refs[:-3]
    gw_ref, gb_ref, gs_ref = refs[-3:]
    sums = [r[...] for r in parts]
    while len(sums) > 1:
        sums = [sums[k] + sums[k + 1] for k in range(0, len(sums), 2)]
    total = sums[0] * scale
    for a in range(3):
        for b in range(3):
            at = (a * 3 + b) * chans
            for c in range(3):
                gw_ref[a, b, c] = total[c * chans : (c + 1) * chans, at : at + chans]
            gs_ref[a, b] = total[3 * chans : 3 * chans + 3, at : at + chans]
    gb_ref[...] = total[3 * chans + 3 : 3 * chans + 4, :chans]


def tree_sum(parts):
    while len(parts) > 1:
        parts = [parts[k] + parts[k + 1] for k in range(0, len(parts), 2)]
    return parts[0]


def shards(volume, w_first, b_first, w_second, prior_logits, cotangent):
    chans, planes, rows, width = volume.shape
    disp = lax.axis_size("disp")
    space = lax.axis_size("space")
    dims = (planes, rows, chans, width, disp, space)
    zi = lax.axis_index("space")
    di = lax.axis_index("disp")

    own = jnp.transpose(volume, (1, 2, 0, 3)).reshape(planes, rows * chans, width)
    z_one = lax.ppermute(own, "space", swap_pairs(space, 0))
    z_two = lax.ppermute(own, "space", swap_pairs(space, 1))
    extra = jnp.concatenate([prior_logits.reshape(planes * rows, width), cotangent], axis=0)
    e_one = lax.ppermute(extra, "space", swap_pairs(space, 0))
    e_two = lax.ppermute(extra, "space", swap_pairs(space, 1))
    z_even = zi % 2 == 0
    zero = jnp.zeros((), BF16)
    above = jnp.where(zi > 0, jnp.where(z_even, z_two, z_one), zero)
    below = jnp.where(zi < space - 1, jnp.where(z_even, z_one, z_two), zero)
    mid = jnp.concatenate([above, own, below], axis=1)
    even = (di % 2 == 0).astype(jnp.int32)
    d_one = lax.ppermute(
        lax.dynamic_slice_in_dim(mid, (planes - 2) * even, 2, axis=0), "disp", swap_pairs(disp, 0)
    )
    d_two = lax.ppermute(
        lax.dynamic_slice_in_dim(mid, (planes - 2) * (1 - even), 2, axis=0), "disp", swap_pairs(disp, 1)
    )

    xr = rows + 8
    base1 = jnp.transpose(w_first, (2, 3, 0, 1, 4)).astype(F32)
    base1 = jnp.pad(base1, ((0, 0), (0, 0), (0, 0), (0, xr - 3), (0, 0))).reshape(3 * chans, 3 * xr * chans)
    base1 = jnp.pad(base1, ((0, 0), (0, -base1.shape[1] % 128)))
    base2 = jnp.transpose(w_second, (2, 0, 1, 3)).astype(F32)
    base2 = jnp.pad(base2, ((0, 0), (0, 0), (0, rows + 3), (0, 0))).reshape(3, 3 * (rows + 6) * chans)
    base2 = jnp.pad(base2, ((0, 5), (0, -base2.shape[1] % 128)))
    base3 = jnp.transpose(w_second[::-1, ::-1], (2, 3, 0, 1)).astype(F32)
    base3 = jnp.pad(base3, ((0, 0), (0, 0), (0, 0), (0, rows + 1))).reshape(3 * chans, 3 * (rows + 4))
    base3 = jnp.pad(base3, ((0, 0), (0, 128 - base3.shape[1])))
    base4 = jnp.transpose(w_first[::-1, ::-1], (2, 4, 0, 1, 3)).astype(F32)
    base4 = jnp.pad(base4, ((0, 0), (0, 0), (0, 0), (0, rows - 1), (0, 0))).reshape(
        3 * chans, 3 * (rows + 2) * chans
    )
    base4 = jnp.pad(base4, ((0, 0), (0, -base4.shape[1] % 128)))

    lr = rows + 4
    hr = rows + 6
    logits, slope, hid, xs, cot = call(
        functools.partial(forward_body, dims),
        "forward",
        (
            ((planes * lr, width), F32, True),
            ((planes + 2, (rows + 2) * chans, width), F32, True),
            ((planes + 3, (rows + 4) * chans, width), BF16, True),
            ((planes + 3, (rows + 4) * chans, width), BF16, True),
            ((lr, width), F32, True),
        ),
        mid, d_one, d_two, extra, e_one, e_two, base1, b_first[None, :], base2,
        scratch=[
            pltpu.VMEM(((planes + 4) * xr * chans, width), BF16),
            pltpu.VMEM(((planes + 2) * hr * chans, width), BF16),
            pltpu.VMEM((planes, lr, width), F32),
        ],
    )

    pieces = [logits] + partners(logits, "disp")
    pay, pg, disparity = call(
        functools.partial(backward_body, dims),
        "backward",
        (
            ((3 * chans + 8, 128), F32, True),
            ((planes + 2, (rows + 2) * chans, width), BF16, True),
            ((rows, width), F32, False),
        ),
        *pieces, cot, slope, hid, xs, base3,
        scratch=[pltpu.VMEM((disp + 2, planes * lr, width), F32)],
    )

    stages = [("disp", s) for s in radix_stages(disp)] + [("space", s) for s in radix_stages(space)]
    for n, (axis, steps) in enumerate(stages):
        count = lax.axis_size(axis)
        parts = [pay] + [lax.ppermute(pay, axis, [(i, i ^ s) for i in range(count)]) for s in steps]
        if n < len(stages) - 1:
            pay = tree_sum(parts)

    (volume_grad,) = call(
        functools.partial(volume_grad_body, dims),
        "volume_grad",
        (((chans, planes, rows, width), BF16, False),),
        pg, base4,
    )

    scale = 16.0 / math.sqrt(planes * disp * rows * space * width)
    first_sum, bias_sum, second_sum = call(
        functools.partial(finish_body, chans, scale),
        "finish",
        (
            ((3, 3, 3, chans, chans), F32, False),
            ((1, chans), F32, False),
            ((3, 3, 3, chans), F32, False),
        ),
        *parts,
    )
    return (volume_grad, first_sum, bias_sum[0], second_sum, disparity)


def solution(mesh):
    return jax.shard_map(
        shards,
        mesh=mesh,
        in_specs=(
            P(None, "disp", ("groups", "space"), None),
            P(),
            P(),
            P(),
            P("disp", ("groups", "space"), None),
            P(("groups", "space"), None),
        ),
        out_specs=(
            P(None, "disp", ("groups", "space"), None),
            P(None, None, None, "groups", None),
            P("groups"),
            P(None, None, None, "groups"),
            P(("groups", "space"), None),
        ),
        check_vma=False,
    )
```

```python
import functools
import math

import jax
import jax.numpy as jnp
from jax import lax
from jax.experimental import pallas as pl
from jax.experimental.pallas import tpu as pltpu
from jax.sharding import PartitionSpec as P

F32 = jnp.float32
BF16 = jnp.bfloat16


def swap_pairs(count, step):
    pairs = []
    for i in range(count):
        j = i ^ 1 if step == 0 else ((i + 1) ^ 1) - 1
        pairs.append((i, j if 0 <= j < count else i))
    return pairs


def partners(value, axis):
    count = lax.axis_size(axis)
    return [lax.ppermute(value, axis, [(i, i ^ s) for i in range(count)]) for s in range(1, count)]


def radix_stages(count):
    stages = []
    bit = 1
    while bit < count:
        if bit * 4 <= count:
            stages.append((bit, 2 * bit, 3 * bit))
            bit *= 4
        else:
            stages.append((bit,))
            bit *= 2
    return stages


def shift_up(x, lane):
    return jnp.where(lane == 0, 0.0, pltpu.roll(x, 1, 1))


def shift_down(x, lane):
    width = x.shape[1]
    return jnp.where(lane == width - 1, 0.0, pltpu.roll(x, width - 1, 1))


def left(x, amount):
    return x if amount == 0 else pltpu.roll(x, x.shape[1] - amount, 1)


def right(x, amount):
    return x if amount == 0 else pltpu.roll(x, amount, 1)


def call(body, name, outs, *operands, scratch=()):
    operands = [pltpu.with_memory_space_constraint(x, pltpu.VMEM) for x in operands]
    return pl.pallas_call(
        body,
        out_shape=tuple(
            pltpu.VMEM(shape, dtype) if inside else jax.ShapeDtypeStruct(shape, dtype)
            for shape, dtype, inside in outs
        ),
        in_specs=[pl.BlockSpec(memory_space=pltpu.VMEM)] * len(operands),
        out_specs=tuple(pl.BlockSpec(memory_space=pltpu.VMEM) for _ in outs),
        scratch_shapes=list(scratch),
        name=name,
    )(*operands)


def dot(a, b):
    return lax.dot_general(a, b, (((1,), (0,)), ((), ())), preferred_element_type=F32)


def dot_t(a, b):
    return lax.dot_general(a, b, (((1,), (1,)), ((), ())), preferred_element_type=F32)


def pack_body(dims, own_ref, prior_ref, cot_ref, one_ref, two_ref, wide_ref):
    planes, rows, chans, width, disp, space = dims
    even = lax.axis_index("space") % 2 == 0
    n = planes * rows * chans
    k = 2 * (planes + 1)
    own = own_ref[...].reshape(n, width)
    wide_ref[...] = jnp.zeros(wide_ref.shape, F32)
    for out_ref in (one_ref, two_ref):
        out_ref[:n] = own

        def put(at):
            for p in range(planes):
                wide_ref[2 * p : 2 * p + 2] = prior_ref[p, at : at + 2]
            wide_ref[2 * planes : k] = cot_ref[at : at + 2]

        goes_down = even if out_ref is one_ref else jnp.logical_not(even)
        pl.when(goes_down)(functools.partial(put, rows - 2))
        pl.when(jnp.logical_not(goes_down))(functools.partial(put, 0))
        rest = wide_ref[:k]
        for t in range(3):
            term = rest.astype(BF16).astype(F32)
            wide_ref[t * k : (t + 1) * k] = term
            rest = rest - term
        out_ref[n:] = wide_ref[...].astype(BF16)


def forward_body(
    dims, mid_ref, db_ref, da_ref, prior_in_ref, cot_in_ref, za_ref, zb_ref, base1_ref, bias_ref, base2_ref,
    logits_ref, slope_ref, hid_ref, xs_ref, cot_ref, x_ref, h_ref, prior_ref
):
    planes, rows, chans, width, disp, space = dims
    zi = lax.axis_index("space")
    di = lax.axis_index("disp")
    z_even = zi % 2 == 0
    d_even = di % 2 == 0
    xr = (rows + 8) * chans
    hr = (rows + 6) * chans
    lane = lax.broadcasted_iota(jnp.int32, (hr, width), 1)

    x_ref[2 * xr : (planes + 2) * xr, :] = mid_ref[...].reshape(planes * xr, width)

    def place(at, size, ok, first, one, two):
        @pl.when(ok & first)
        def _():
            x_ref[at : at + size, :] = one[...].reshape(size, width)

        @pl.when(ok & jnp.logical_not(first))
        def _():
            x_ref[at : at + size, :] = two[...].reshape(size, width)

        @pl.when(jnp.logical_not(ok))
        def _():
            x_ref[at : at + size, :] = jnp.zeros((size, width), BF16)

    place(0, 2 * xr, di > 0, d_even, db_ref, da_ref)
    place((planes + 2) * xr, 2 * xr, di < disp - 1, d_even, da_ref, db_ref)

    n = planes * rows * chans
    k = 2 * (planes + 1)

    def extras(ok, first, one, two, at):
        def put(src):
            wide = None if src is None else src[n:, :].astype(F32)
            total = jnp.zeros((k, width), F32)
            if wide is not None:
                total = wide[:k] + wide[k : 2 * k] + wide[2 * k : 3 * k]
            for p in range(planes):
                prior_ref[p, at : at + 2, :] = total[2 * p : 2 * p + 2]
            cot_ref[at : at + 2, :] = total[2 * planes : k]

        pl.when(ok & first)(lambda: put(one))
        pl.when(ok & jnp.logical_not(first))(lambda: put(two))
        pl.when(jnp.logical_not(ok))(lambda: put(None))

    for p in range(planes):
        prior_ref[p, 2 : 2 + rows, :] = prior_in_ref[p]
    cot_ref[2 : 2 + rows, :] = cot_in_ref[...]
    extras(zi > 0, z_even, zb_ref, za_ref, 0)
    extras(zi < space - 1, z_even, za_ref, zb_ref, rows + 2)

    bands = []
    base1 = base1_ref[...]
    for c in range(3):
        piece = base1[c * chans : (c + 1) * chans]
        for r in range(rows + 6):
            bands.append(right(piece, chans * r))
    band1 = jnp.concatenate(bands, axis=0)[:, : 3 * xr].astype(BF16)
    diag = lax.broadcasted_iota(jnp.int32, (chans, chans), 0) == lax.broadcasted_iota(
        jnp.int32, (chans, chans), 1
    )
    bias = jnp.sum(jnp.where(diag, bias_ref[...], 0.0), axis=1, keepdims=True)
    bias = jnp.concatenate([jnp.broadcast_to(bias, (chans, width))] * (rows + 6), axis=0)
    row_at = zi * rows - 3 + lax.broadcasted_iota(jnp.int32, (hr, width), 0) // chans
    row_ok = ((row_at >= 0) & (row_at < space * rows)).astype(F32)
    for p in range(planes + 2):
        y = dot(band1, x_ref[p * xr : (p + 3) * xr, :])
        pre = y[hr : 2 * hr] + shift_up(y[:hr], lane) + shift_down(y[2 * hr :], lane) + bias
        sig = jax.nn.sigmoid(pre)
        plane_at = di * planes - 1 + p
        ok = row_ok * ((plane_at >= 0) & (plane_at < disp * planes)).astype(F32)
        hidden = (pre * sig * ok).astype(BF16)
        h_ref[p * hr : (p + 1) * hr, :] = hidden
        inner = slice(2 * chans, hr - 2 * chans)
        slope_ref[p] = (sig * (1.0 + pre * (1.0 - sig)) * ok)[inner]
        hid_ref[p] = h_ref[p * hr + chans : (p + 1) * hr - chans, :]
        xs_ref[p] = x_ref[(p + 1) * xr + 2 * chans : (p + 2) * xr - 2 * chans, :]
    hid_ref[planes + 2] = jnp.zeros(hid_ref.shape[1:], BF16)
    xs_ref[planes + 2] = jnp.zeros(xs_ref.shape[1:], BF16)

    lr = rows + 4
    lane2 = lax.broadcasted_iota(jnp.int32, (lr, width), 1)
    bands = []
    for c in range(3):
        piece = base2_ref[c : c + 1, :]
        for r in range(lr):
            bands.append(right(piece, chans * r))
    band2 = jnp.concatenate(bands, axis=0)[:, : 3 * hr].astype(BF16)
    for p in range(planes):
        y = dot(band2, h_ref[p * hr : (p + 3) * hr, :])
        logits_ref[p * lr : (p + 1) * lr, :] = (
            y[lr : 2 * lr] + shift_up(y[:lr], lane2) + shift_down(y[2 * lr :], lane2) + prior_ref[p]
        )


def backward_body(dims, *refs):
    planes, rows, chans, width, disp, space = dims
    logit_refs = refs[:disp]
    cot_ref, slope_ref, hid_ref, xs_ref, base3_ref = refs[disp : disp + 5]
    pay_ref, pg_ref, disp_ref, l_ref = refs[disp + 5 :]
    di = lax.axis_index("disp")
    lr = rows + 4
    hr = (rows + 2) * chans
    total = planes * disp
    lane = lax.broadcasted_iota(jnp.int32, (lr, width), 1)

    l_ref[0] = jnp.zeros(l_ref.shape[1:], F32)
    l_ref[disp + 1] = jnp.zeros(l_ref.shape[1:], F32)
    for s in range(disp):
        l_ref[(di ^ s) + 1] = logit_refs[-s % disp][...]

    def logit(g, p):
        return l_ref[g, p * lr : (p + 1) * lr, :]

    top = logit(1, 0)
    for k in range(1, total):
        top = jnp.maximum(top, logit(1 + k // planes, k % planes))
    summed = jnp.zeros((lr, width), F32)
    moment = jnp.zeros((lr, width), F32)
    for k in range(total):
        e = jnp.exp(logit(1 + k // planes, k % planes) - top)
        summed = summed + e
        moment = moment + e * ((k + 0.5) / total)
    disparity = moment / summed
    disp_ref[...] = disparity[2 : 2 + rows]
    coef = cot_ref[...] / summed
    scores = []
    for k in range(planes + 4):
        at = di * planes - 2 + k
        group = di + (0 if k < 2 else 1 if k < 2 + planes else 2)
        e = jnp.exp(logit(group, (k - 2) % planes) - top)
        ok = ((at >= 0) & (at < total)).astype(F32)
        position = (at.astype(F32) + 0.5) / total
        score = jnp.where(ok > 0.0, coef * e * (position - disparity), 0.0).astype(BF16)
        scores.append(score.astype(F32))
    s_all = jnp.concatenate(scores, axis=0).astype(BF16)

    lane_h = lax.broadcasted_iota(jnp.int32, (hr, width), 1)
    base3 = base3_ref[...]
    rhs_rows = (rows + 4) * chans
    acc1 = None
    acc2 = None
    bias = jnp.zeros((chans, width), F32)
    for p in range(planes + 2):
        bands = []
        for c in range(3):
            piece = base3[c * chans : (c + 1) * chans]
            for r in range(rows + 2):
                bands.append(right(piece, lr * p + r))
        band3 = jnp.concatenate(bands, axis=0)[:, : (planes + 4) * lr].astype(BF16)
        y = dot(band3, s_all)
        hg = y[hr : 2 * hr] + shift_down(y[:hr], lane_h) + shift_up(y[2 * hr :], lane_h)
        pg = (hg * slope_ref[p]).astype(BF16)
        pg_ref[p] = pg
        if p == 0 or p == planes + 1:
            continue
        k = p - 1
        own = pg.astype(F32)[chans : chans * (rows + 1)]
        lane_o = lane_h[: own.shape[0]]
        moved = (shift_down(own, lane_o), own, shift_up(own, lane_o))
        pieces = []
        for r in range(rows):
            bias = bias + own[r * chans : (r + 1) * chans]
            for c in range(3):
                pieces.append(moved[c][r * chans : (r + 1) * chans])
        lhs = jnp.concatenate(pieces, axis=0).astype(BF16)
        rhs = xs_ref[k : k + 4].reshape(4 * rhs_rows, width)
        part = dot_t(lhs, rhs)
        acc1 = part if acc1 is None else acc1 + part
        sc = scores[k + 2]
        lhs = jnp.concatenate([shift_down(sc, lane), sc, shift_up(sc, lane)], axis=0).astype(BF16)
        part = dot_t(lhs, hid_ref[k : k + 4].reshape(4 * rhs_rows, width))
        acc2 = part if acc2 is None else acc2 + part

    out1 = jnp.zeros((3 * chans, 4 * rhs_rows), F32)
    for r in range(rows):
        out1 = out1 + left(acc1[3 * chans * r : 3 * chans * (r + 1)], chans * (r + 1))
    row_in = lax.broadcasted_iota(jnp.int32, acc2.shape, 0) % lr
    out2 = jnp.zeros(acc2.shape, F32)
    for r in range(2, 2 + rows):
        out2 = out2 + jnp.where(row_in == r, left(acc2, chans * (r - 1)), 0.0)
    out2 = jnp.concatenate(
        [jnp.sum(out2[c * lr : (c + 1) * lr], axis=0, keepdims=True) for c in range(3)]
        + [jnp.zeros((5, out2.shape[1]), F32)],
        axis=0,
    )
    out = jnp.concatenate([out1, out2], axis=0)
    lane_p = lax.broadcasted_iota(jnp.int32, (out.shape[0], 128), 1)
    tap = 3 * chans
    packed = jnp.zeros((out.shape[0], 128), F32)
    for a in range(3):
        moved = left(out, a * (rhs_rows - tap))[:, :128]
        packed = jnp.where((lane_p >= a * tap) & (lane_p < (a + 1) * tap), moved, packed)
    bias = jnp.sum(bias, axis=1, keepdims=True)
    sub = lax.broadcasted_iota(jnp.int32, (chans, 128), 0)
    lane_b = lax.broadcasted_iota(jnp.int32, (chans, 128), 1)
    bias = jnp.sum(jnp.where(sub == lane_b, bias, 0.0), axis=0, keepdims=True)
    pay_ref[...] = packed
    pay_ref[3 * chans + 3 : 3 * chans + 4, :] = bias


def volume_grad_body(dims, pg_ref, base4_ref, out_ref):
    planes, rows, chans, width, disp, space = dims
    hr = (rows + 2) * chans
    n = rows * chans
    lane = lax.broadcasted_iota(jnp.int32, (n, width), 1)
    base4 = base4_ref[...]
    bands = []
    for c in range(3):
        piece = base4[c * chans : (c + 1) * chans]
        for r in range(rows):
            bands.append(right(piece, chans * r))
    band4 = jnp.concatenate(bands, axis=0)[:, : 3 * hr].astype(BF16)
    to = lax.broadcasted_iota(jnp.int32, (3 * n, 3 * n), 0)
    at = lax.broadcasted_iota(jnp.int32, (3 * n, 3 * n), 1)
    source = (to // n) * n + (to % rows) * chans + (to % n) // rows
    band4 = dot((at == source).astype(BF16), band4).astype(BF16)
    for p in range(planes):
        y = dot(band4, pg_ref[p : p + 3].reshape(3 * hr, width))
        y = (y[n : 2 * n] + shift_down(y[:n], lane) + shift_up(y[2 * n :], lane)).astype(BF16)
        for i in range(chans):
            out_ref[i, p] = y[i * rows : (i + 1) * rows]


def finish_body(chans, scale, *refs):
    parts = refs[:-3]
    gw_ref, gb_ref, gs_ref = refs[-3:]
    sums = [r[...] for r in parts]
    while len(sums) > 1:
        sums = [sums[k] + sums[k + 1] for k in range(0, len(sums), 2)]
    total = sums[0] * scale
    for a in range(3):
        for b in range(3):
            at = (a * 3 + b) * chans
            for c in range(3):
                gw_ref[a, b, c] = total[c * chans : (c + 1) * chans, at : at + chans]
            gs_ref[a, b] = total[3 * chans : 3 * chans + 3, at : at + chans]
    gb_ref[...] = total[3 * chans + 3 : 3 * chans + 4, :chans]


def tree_sum(parts):
    while len(parts) > 1:
        parts = [parts[k] + parts[k + 1] for k in range(0, len(parts), 2)]
    return parts[0]


def shards(volume, w_first, b_first, w_second, prior_logits, cotangent):
    chans, planes, rows, width = volume.shape
    disp = lax.axis_size("disp")
    space = lax.axis_size("space")
    dims = (planes, rows, chans, width, disp, space)
    zi = lax.axis_index("space")
    di = lax.axis_index("disp")

    own = jnp.transpose(volume, (1, 2, 0, 3)).reshape(planes, rows * chans, width)
    n = planes * rows * chans
    extra = -(-6 * (planes + 1) // 16) * 16
    send_one, send_two = call(
        functools.partial(pack_body, dims),
        "pack",
        (((n + extra, width), BF16, True), ((n + extra, width), BF16, True)),
        own, prior_logits, cotangent,
        scratch=[pltpu.VMEM((extra, width), F32)],
    )
    z_one = lax.ppermute(send_one, "space", swap_pairs(space, 0))
    z_two = lax.ppermute(send_two, "space", swap_pairs(space, 1))
    z_even = zi % 2 == 0
    zero = jnp.zeros((), BF16)
    block_one = z_one[:n].reshape(own.shape)
    block_two = z_two[:n].reshape(own.shape)
    above = jnp.where(zi > 0, jnp.where(z_even, block_two, block_one), zero)
    below = jnp.where(zi < space - 1, jnp.where(z_even, block_one, block_two), zero)
    mid = jnp.concatenate([above, own, below], axis=1)
    even = (di % 2 == 0).astype(jnp.int32)
    d_one = lax.ppermute(
        lax.dynamic_slice_in_dim(mid, (planes - 2) * even, 2, axis=0), "disp", swap_pairs(disp, 0)
    )
    d_two = lax.ppermute(
        lax.dynamic_slice_in_dim(mid, (planes - 2) * (1 - even), 2, axis=0), "disp", swap_pairs(disp, 1)
    )

    xr = rows + 8
    base1 = jnp.transpose(w_first, (2, 3, 0, 1, 4)).astype(F32)
    base1 = jnp.pad(base1, ((0, 0), (0, 0), (0, 0), (0, xr - 3), (0, 0))).reshape(3 * chans, 3 * xr * chans)
    base1 = jnp.pad(base1, ((0, 0), (0, -base1.shape[1] % 128)))
    base2 = jnp.transpose(w_second, (2, 0, 1, 3)).astype(F32)
    base2 = jnp.pad(base2, ((0, 0), (0, 0), (0, rows + 3), (0, 0))).reshape(3, 3 * (rows + 6) * chans)
    base2 = jnp.pad(base2, ((0, 5), (0, -base2.shape[1] % 128)))
    base3 = jnp.transpose(w_second[::-1, ::-1], (2, 3, 0, 1)).astype(F32)
    base3 = jnp.pad(base3, ((0, 0), (0, 0), (0, 0), (0, rows + 1))).reshape(3 * chans, 3 * (rows + 4))
    base3 = jnp.pad(base3, ((0, 0), (0, 128 - base3.shape[1])))
    base4 = jnp.transpose(w_first[::-1, ::-1], (2, 4, 0, 1, 3)).astype(F32)
    base4 = jnp.pad(base4, ((0, 0), (0, 0), (0, 0), (0, rows - 1), (0, 0))).reshape(
        3 * chans, 3 * (rows + 2) * chans
    )
    base4 = jnp.pad(base4, ((0, 0), (0, -base4.shape[1] % 128)))

    lr = rows + 4
    hr = rows + 6
    logits, slope, hid, xs, cot = call(
        functools.partial(forward_body, dims),
        "forward",
        (
            ((planes * lr, width), F32, True),
            ((planes + 2, (rows + 2) * chans, width), F32, True),
            ((planes + 3, (rows + 4) * chans, width), BF16, True),
            ((planes + 3, (rows + 4) * chans, width), BF16, True),
            ((lr, width), F32, True),
        ),
        mid, d_two, d_one, prior_logits, cotangent, z_one, z_two, base1, b_first[None, :], base2,
        scratch=[
            pltpu.VMEM(((planes + 4) * xr * chans, width), BF16),
            pltpu.VMEM(((planes + 2) * hr * chans, width), BF16),
            pltpu.VMEM((planes, lr, width), F32),
        ],
    )

    pieces = [logits] + partners(logits, "disp")[::-1]
    pay, pg, disparity = call(
        functools.partial(backward_body, dims),
        "backward",
        (
            ((3 * chans + 8, 128), F32, True),
            ((planes + 2, (rows + 2) * chans, width), BF16, True),
            ((rows, width), F32, False),
        ),
        *pieces, cot, slope, hid, xs, base3,
        scratch=[pltpu.VMEM((disp + 2, planes * lr, width), F32)],
    )

    stages = [("disp", s) for s in radix_stages(disp)] + [("space", s) for s in radix_stages(space)]
    for n, (axis, steps) in enumerate(stages):
        count = lax.axis_size(axis)
        parts = [pay] + [lax.ppermute(pay, axis, [(i, i ^ s) for i in range(count)]) for s in steps]
        if n < len(stages) - 1:
            pay = tree_sum(parts)

    (volume_grad,) = call(
        functools.partial(volume_grad_body, dims),
        "volume_grad",
        (((chans, planes, rows, width), BF16, False),),
        pg, base4,
    )

    scale = 16.0 / math.sqrt(planes * disp * rows * space * width)
    first_sum, bias_sum, second_sum = call(
        functools.partial(finish_body, chans, scale),
        "finish",
        (
            ((3, 3, 3, chans, chans), F32, False),
            ((1, chans), F32, False),
            ((3, 3, 3, chans), F32, False),
        ),
        *parts,
    )
    return (volume_grad, first_sum, bias_sum[0], second_sum, disparity)


def solution(mesh):
    return jax.shard_map(
        shards,
        mesh=mesh,
        in_specs=(
            P(None, "disp", ("groups", "space"), None),
            P(),
            P(),
            P(),
            P("disp", ("groups", "space"), None),
            P(("groups", "space"), None),
        ),
        out_specs=(
            P(None, "disp", ("groups", "space"), None),
            P(None, None, None, "groups", None),
            P("groups"),
            P(None, None, None, "groups"),
            P(("groups", "space"), None),
        ),
        check_vma=False,
    )
```

```python
import functools
import math

import jax
import jax.numpy as jnp
from jax import lax
from jax.experimental import pallas as pl
from jax.experimental.pallas import tpu as pltpu
from jax.sharding import PartitionSpec as P

F32 = jnp.float32
BF16 = jnp.bfloat16


def swap_pairs(count, step):
    pairs = []
    for i in range(count):
        j = i ^ 1 if step == 0 else ((i + 1) ^ 1) - 1
        pairs.append((i, j if 0 <= j < count else i))
    return pairs


def radix_stages(count):
    stages = []
    bit = 1
    while bit < count:
        if bit * 4 <= count:
            stages.append((bit, 2 * bit, 3 * bit))
            bit *= 4
        else:
            stages.append((bit,))
            bit *= 2
    return stages


def shift_up(x):
    return pltpu.roll(x, 1, 1)


def shift_down(x):
    return pltpu.roll(x, x.shape[1] - 1, 1)


def left(x, amount):
    return x if amount == 0 else pltpu.roll(x, x.shape[1] - amount, 1)


def right(x, amount):
    return x if amount == 0 else pltpu.roll(x, amount, 1)


def call(body, name, outs, *operands, scratch=()):
    operands = [pltpu.with_memory_space_constraint(x, pltpu.VMEM) for x in operands]
    return pl.pallas_call(
        body,
        out_shape=tuple(
            pltpu.VMEM(shape, dtype) if inside else jax.ShapeDtypeStruct(shape, dtype)
            for shape, dtype, inside in outs
        ),
        in_specs=[pl.BlockSpec(memory_space=pltpu.VMEM)] * len(operands),
        out_specs=tuple(pl.BlockSpec(memory_space=pltpu.VMEM) for _ in outs),
        scratch_shapes=list(scratch),
        name=name,
    )(*operands)


def dot(a, b):
    return lax.dot_general(a, b, (((1,), (0,)), ((), ())), preferred_element_type=F32)


def dot_t(a, b):
    return lax.dot_general(a, b, (((1,), (1,)), ((), ())), preferred_element_type=F32)


def terms(value):
    out = []
    for _ in range(3):
        term = value.astype(BF16).astype(F32)
        out.append(term)
        value = value - term
    return out


def window(x, start, size):
    width = x.shape[1]
    moved = pltpu.roll(x, (width - start) % width, 1)[:, :size]
    column = start + lax.broadcasted_iota(jnp.int32, moved.shape, 1)
    return jnp.where((column >= 0) & (column < width), moved, 0.0)


def split_body(dims, own_ref, prior_ref, *refs):
    planes, rows, chans, width, disp, space, cols, lanes = dims
    out_refs = refs[:disp]
    wide_ref = refs[disp]
    di = lax.axis_index("disp")
    half = 2 * planes
    for h in range(2):
        for p in range(planes):
            at = h * half + 2 * p
            wide_ref[at : at + 2] = prior_ref[p, 2 * h : 2 * h + 2]
    wide = wide_ref[...]
    pieces = [own_ref[...].reshape(planes * rows * chans, width).astype(F32)]
    for h in range(2):
        pieces += terms(wide[h * half : (h + 1) * half])
    whole = jnp.concatenate(pieces, axis=0)
    for s in range(disp):
        start = (di ^ s) * cols - 4
        out_refs[s][...] = window(whole, start, lanes).astype(BF16)


def rows_body(dims, *refs):
    planes, rows, chans, width, disp, space, cols, lanes = dims
    piece_refs = refs[:disp]
    cot_in_ref, one_ref, two_ref, prior_ref, cot_ref, wide_ref = refs[disp:]
    di = lax.axis_index("disp")
    even = lax.axis_index("space") % 2 == 0
    n = planes * rows * chans
    total = n * disp
    half = 2 * planes
    cot = window(jnp.concatenate([cot_in_ref[...]] * 2, axis=0), di * cols - 4, lanes)[:rows]
    cot_ref[...] = jnp.zeros(cot_ref.shape, F32)
    cot_ref[2 : 2 + rows] = cot
    for s in range(disp):
        g = di ^ s
        block = piece_refs[s][:n]
        at = pl.multiple_of(g * n, n)
        one_ref[pl.ds(at, n)] = block
        two_ref[pl.ds(at, n)] = block
        prior = piece_refs[s][n:].astype(F32)
        for h in range(2):
            base = 3 * half * h
            value = prior[base : base + half] + prior[base + half : base + 2 * half] + prior[base + 2 * half : base + 3 * half]
            for p in range(planes):
                prior_ref[g * planes + p, 2 + 2 * h : 4 + 2 * h] = value[2 * p : 2 * p + 2]
    for out_ref, down in ((one_ref, even), (two_ref, jnp.logical_not(even))):

        def put(h):
            for s in range(disp):
                prior = piece_refs[s][n:].astype(F32)
                at = pl.multiple_of((di ^ s) * 3 * half, 8)
                wide_ref[pl.ds(at, 3 * half)] = prior[3 * half * h : 3 * half * (h + 1)]
            for t, term in enumerate(terms(cot_ref[2 + 2 * h : 4 + 2 * h])):
                at = disp * 3 * half + 2 * t
                wide_ref[at : at + 2] = term
            rest = disp * 3 * half + 6
            wide_ref[rest:] = jnp.zeros((wide_ref.shape[0] - rest, lanes), F32)

        pl.when(down)(functools.partial(put, 1))
        pl.when(jnp.logical_not(down))(functools.partial(put, 0))
        out_ref[total:] = wide_ref[...].astype(BF16)


def bands_body(dims, base1_ref, base2_ref, base3_ref, base4_ref, bias_ref, band1_ref, band2_ref, band3_ref, band4_ref, col_ref):
    planes, rows, chans, width, disp, space, cols, lanes = dims

    def band(base, groups, count, step, used):
        pieces = []
        for c in range(3):
            piece = base[c * groups : (c + 1) * groups]
            for r in range(count):
                pieces.append(right(piece, step * r))
        return jnp.concatenate(pieces, axis=0)[:, :used].astype(BF16)

    band1_ref[...] = band(base1_ref[...], chans, rows + 6, chans, band1_ref.shape[1])
    band2_ref[...] = band(base2_ref[...], 1, rows + 4, chans, band2_ref.shape[1])
    band3_ref[...] = band(base3_ref[...], chans, rows + 2, 1, band3_ref.shape[1])
    band4 = band(base4_ref[...], chans, rows, chans, band4_ref.shape[1])
    n = rows * chans
    to = lax.broadcasted_iota(jnp.int32, (3 * n, 3 * n), 0)
    at = lax.broadcasted_iota(jnp.int32, (3 * n, 3 * n), 1)
    source = (to // n) * n + (to % rows) * chans + (to % n) // rows
    band4_ref[...] = dot((at == source).astype(BF16), band4).astype(BF16)
    diag = lax.broadcasted_iota(jnp.int32, (chans, chans), 0) == lax.broadcasted_iota(
        jnp.int32, (chans, chans), 1
    )
    bias = jnp.sum(jnp.where(diag, bias_ref[...], 0.0), axis=1, keepdims=True)
    col_ref[...] = jnp.concatenate([jnp.broadcast_to(bias, (chans, 2 * lanes))] * (rows + 6), axis=0)


def main_body(dims, *refs):
    planes, rows, chans, width, disp, space, cols, lanes = dims
    own_ref, za_ref, zb_ref, prior_in_ref, cot_in_ref, band1_ref, band2_ref, band3_ref, band4_ref, col_ref = refs[:10]
    back_refs = refs[10 : 10 + disp]
    x_ref, h_ref, slope_ref, prior_ref, cot_ref, s_ref, pg_ref, v_ref = refs[10 + disp :]
    zi = lax.axis_index("space")
    di = lax.axis_index("disp")
    z_even = zi % 2 == 0
    count = planes * disp
    n = count * rows * chans
    block = rows * chans
    xr = (rows + 8) * chans
    hr = (rows + 6) * chans
    gr = (rows + 2) * chans
    lr = rows + 4
    sr = 16
    two = 2 * lanes

    x_ref[:xr] = jnp.zeros((xr, lanes), BF16)
    x_ref[(count + 1) * xr :] = jnp.zeros((2 * xr, lanes), BF16)
    h_ref[:hr] = jnp.zeros((hr, lanes), BF16)
    h_ref[(count + 1) * hr :] = jnp.zeros((2 * hr, lanes), BF16)
    s_ref[...] = jnp.zeros(s_ref.shape, BF16)
    pg_ref[:gr] = jnp.zeros((gr, lanes), BF16)
    pg_ref[(count + 1) * gr :] = jnp.zeros((gr, lanes), BF16)
    for k in range(count):
        at = (k + 1) * xr + 4 * chans
        x_ref[at : at + block] = own_ref[k * block : (k + 1) * block]
    prior_ref[...] = prior_in_ref[...]
    cot_ref[...] = cot_in_ref[...]
    half = 2 * planes

    def place(ok, first, one, other, row, at8):
        def put(src):
            for k in range(count):
                at = (k + 1) * xr + row * chans
                if src is None:
                    x_ref[at : at + 4 * chans] = jnp.zeros((4 * chans, lanes), BF16)
                else:
                    x_ref[at : at + 4 * chans] = src[k * block : k * block + 4 * chans]
            if src is None:
                for k in range(count):
                    prior_ref[k, at8 : at8 + 2] = jnp.zeros((2, lanes), F32)
                cot_ref[at8 : at8 + 2] = jnp.zeros((2, lanes), F32)
                return
            extra = src[n:].astype(F32)
            for g in range(disp):
                base = g * 3 * half
                value = extra[base : base + half] + extra[base + half : base + 2 * half] + extra[base + 2 * half : base + 3 * half]
                for p in range(planes):
                    prior_ref[g * planes + p, at8 : at8 + 2] = value[2 * p : 2 * p + 2]
            base = disp * 3 * half
            cot_ref[at8 : at8 + 2] = extra[base : base + 2] + extra[base + 2 : base + 4] + extra[base + 4 : base + 6]

        pl.when(ok & first)(lambda: put(one))
        pl.when(ok & jnp.logical_not(first))(lambda: put(other))
        pl.when(jnp.logical_not(ok))(lambda: put(None))

    place(zi > 0, z_even, zb_ref, za_ref, 0, 0)
    place(zi < space - 1, z_even, za_ref, zb_ref, 4 + rows, 2 + rows)

    def pair(ref, p, size, taken):
        return jnp.concatenate([ref[p * size : p * size + taken], ref[(p + 1) * size : (p + 1) * size + taken]], axis=1)

    lane = lax.broadcasted_iota(jnp.int32, (hr, two), 1) % lanes
    column = di * cols - 4 + lane
    row_at = zi * rows - 3 + lax.broadcasted_iota(jnp.int32, (hr, two), 0) // chans
    inside = ((row_at >= 0) & (row_at < space * rows) & (column >= 0) & (column < width)).astype(F32)
    band1 = band1_ref[...]
    bias = col_ref[...]
    for p in range(0, count, 2):
        y = dot(band1, pair(x_ref, p, xr, 3 * xr))
        pre = y[hr : 2 * hr] + shift_up(y[:hr]) + shift_down(y[2 * hr :]) + bias
        sig = jax.nn.sigmoid(pre)
        hidden = (pre * sig * inside).astype(BF16)
        slope = (sig * (1.0 + pre * (1.0 - sig)) * inside)[2 * chans : hr - 2 * chans]
        for q in range(2):
            part = slice(q * lanes, (q + 1) * lanes)
            h_ref[(p + q + 1) * hr : (p + q + 2) * hr] = hidden[:, part]
            slope_ref[p + q] = slope[:, part]

    band2 = band2_ref[...]
    logits = []
    for p in range(0, count, 2):
        y = dot(band2, pair(h_ref, p, hr, 3 * hr))
        y = y[lr : 2 * lr] + shift_up(y[:lr]) + shift_down(y[2 * lr :])
        logits += [y[:, :lanes] + prior_ref[p], y[:, lanes:] + prior_ref[p + 1]]

    top = logits[0]
    for value in logits[1:]:
        top = jnp.maximum(top, value)
    summed = jnp.zeros((lr, lanes), F32)
    moment = jnp.zeros((lr, lanes), F32)
    weights = []
    for k, value in enumerate(logits):
        e = jnp.exp(value - top)
        weights.append(e)
        summed = summed + e
        moment = moment + e * ((k + 0.5) / count)
    disparity = moment / summed
    coef = cot_ref[...] / summed
    mine = lax.broadcasted_iota(jnp.int32, (lr, lanes), 1)
    mine = (mine >= 4) & (mine < 4 + cols)
    left2 = []
    for k in range(count):
        score = (coef * weights[k] * ((k + 0.5) / count - disparity)).astype(BF16)
        s_ref[(k + 1) * sr : (k + 1) * sr + lr] = score
        score = jnp.where(mine, score.astype(F32), 0.0)
        left2.append(jnp.concatenate([shift_down(score), score, shift_up(score)], axis=0).astype(BF16))

    band3 = band3_ref[...]
    mine = lax.broadcasted_iota(jnp.int32, (block, two), 1) % lanes
    mine = (mine >= 4) & (mine < 4 + cols)
    bias_sum = jnp.zeros((chans, two), F32)
    left1 = []
    for p in range(0, count, 2):
        y = dot(band3, pair(s_ref, p, sr, 3 * sr))
        hg = y[gr : 2 * gr] + shift_down(y[:gr]) + shift_up(y[2 * gr :])
        slope = jnp.concatenate([slope_ref[p], slope_ref[p + 1]], axis=1)
        pg = (hg * slope).astype(BF16)
        for q in range(2):
            pg_ref[(p + q + 1) * gr : (p + q + 2) * gr] = pg[:, q * lanes : (q + 1) * lanes]
        own = jnp.where(mine, pg.astype(F32)[chans : chans + block], 0.0)
        moved = (shift_down(own), own, shift_up(own))
        pieces = []
        for r in range(rows):
            part = slice(r * chans, (r + 1) * chans)
            bias_sum = bias_sum + own[part]
            pieces += [moved[c][part] for c in range(3)]
        left1.append(jnp.concatenate(pieces, axis=0).astype(BF16))

    inner = (rows + 4) * chans
    acc1 = None
    acc2 = None
    for p in range(0, count, 2):
        rhs = []
        for q in range(2):
            at = [(p + q + a) * xr + 2 * chans for a in range(4)]
            rhs.append(jnp.concatenate([x_ref[k : k + inner] for k in at], axis=0))
        part = dot_t(left1[p // 2], jnp.concatenate(rhs, axis=1))
        acc1 = part if acc1 is None else acc1 + part
        lhs = jnp.concatenate([left2[p], left2[p + 1]], axis=1)
        part = dot_t(lhs, pair(h_ref, p, hr, 4 * hr))
        acc2 = part if acc2 is None else acc2 + part

    out1 = jnp.zeros((3 * chans, acc1.shape[1]), F32)
    for r in range(rows):
        out1 = out1 + left(acc1[3 * chans * r : 3 * chans * (r + 1)], chans * (r + 1))
    acc2 = acc2[:, :256]
    row_in = lax.broadcasted_iota(jnp.int32, acc2.shape, 0) % lr
    out2 = jnp.zeros(acc2.shape, F32)
    for r in range(2, 2 + rows):
        out2 = out2 + jnp.where(row_in == r, left(acc2, chans * r), 0.0)
    out2 = jnp.concatenate(
        [jnp.sum(out2[c * lr : (c + 1) * lr], axis=0, keepdims=True) for c in range(3)]
        + [jnp.zeros((5, out2.shape[1]), F32)],
        axis=0,
    )
    tap = 3 * chans

    def packed(out, pitch):
        lane_p = lax.broadcasted_iota(jnp.int32, (out.shape[0], lanes), 1)
        total = jnp.zeros((out.shape[0], lanes), F32)
        for a in range(3):
            moved = left(out, a * (pitch - tap))[:, :lanes]
            total = jnp.where((lane_p >= a * tap) & (lane_p < (a + 1) * tap), moved, total)
        return total

    bias_sum = jnp.sum(bias_sum, axis=1, keepdims=True)
    sub = lax.broadcasted_iota(jnp.int32, (chans, lanes), 0)
    lane_b = lax.broadcasted_iota(jnp.int32, (chans, lanes), 1)
    bias_sum = jnp.sum(jnp.where(sub == lane_b, bias_sum, 0.0), axis=0, keepdims=True)
    second = packed(out2, hr)
    row_in = lax.broadcasted_iota(jnp.int32, second.shape, 0)
    second = jnp.where(row_in == 3, bias_sum, second)
    payload = jnp.concatenate([packed(out1, inner), second], axis=0)
    shown = jnp.concatenate([disparity[2 : 2 + rows]] * 2, axis=0)
    tail = jnp.concatenate(terms(payload) + terms(shown) + [jnp.zeros((8, lanes), F32)], axis=0).astype(BF16)

    band4 = band4_ref[...]
    for p in range(0, count, 2):
        y = dot(band4, pair(pg_ref, p, gr, 3 * gr))
        y = (y[block : 2 * block] + shift_down(y[:block]) + shift_up(y[2 * block :])).astype(BF16)
        for q in range(2):
            v_ref[(p + q) * block : (p + q + 1) * block] = y[:, q * lanes : (q + 1) * lanes]
    size = planes * block
    for s in range(disp):
        back_refs[s][:size] = v_ref[pl.ds(pl.multiple_of((di ^ s) * size, size), size)]
        back_refs[s][size:] = tail


def sum_body(chans, *refs):
    parts = refs[:-1]
    k = 3 * chans + 8
    sums = []
    for r in parts:
        n = r.shape[0] - 3 * k - 32
        value = r[n:].astype(F32)
        sums.append(value[:k] + value[k : 2 * k] + value[2 * k : 3 * k])
    refs[-1][...] = tree_sum(sums)


def join_body(dims, *refs):
    planes, rows, chans, width, disp, space, cols, lanes = dims
    parts = refs[:disp]
    grad_ref, disp_ref = refs[disp:]
    di = lax.axis_index("disp")
    n = planes * rows * chans
    k = 3 * (3 * chans + 8)
    total = None
    for s in range(disp):
        j = di ^ s
        shown = parts[s][n + k :].astype(F32)
        shown = shown[:8] + shown[8:16] + shown[16:24]
        value = jnp.concatenate([parts[s][:n].astype(F32), shown], axis=0)
        lane = lax.broadcasted_iota(jnp.int32, value.shape, 1)
        value = jnp.where((lane >= 4) & (lane < 4 + cols), value, 0.0)
        value = jnp.concatenate([value, jnp.zeros((value.shape[0], width - lanes), F32)], axis=1)
        value = pltpu.roll(value, (j * cols - 4 + width) % width, 1)
        total = value if total is None else total + value
    disp_ref[...] = total[n : n + rows]
    grad = total[:n].astype(BF16)
    for p in range(planes):
        for i in range(chans):
            at = (p * chans + i) * rows
            grad_ref[i, p] = grad[at : at + rows]


def tree_sum(parts):
    while len(parts) > 1:
        parts = [parts[k] + parts[k + 1] for k in range(0, len(parts), 2)]
    return parts[0]


def finish_body(chans, scale, *refs):
    gw_ref, gb_ref, gs_ref = refs[-3:]
    total = tree_sum([r[...] for r in refs[:-3]]) * scale
    for a in range(3):
        for b in range(3):
            at = (a * 3 + b) * chans
            for c in range(3):
                gw_ref[a, b, c] = total[c * chans : (c + 1) * chans, at : at + chans]
            gs_ref[a, b] = total[3 * chans : 3 * chans + 3, at : at + chans]
    gb_ref[...] = total[3 * chans + 3 : 3 * chans + 4, :chans]


def flipped(body, count):
    def run(*refs):
        return body(*refs[:count][::-1], *refs[count:])

    return run


def exchange(sends, axis):
    count = lax.axis_size(axis)
    return [sends[0]] + [
        lax.ppermute(sends[s], axis, [(i, i ^ s) for i in range(count)]) for s in range(1, count)
    ]


def shards(volume, w_first, b_first, w_second, prior_logits, cotangent):
    chans, planes, rows, width = volume.shape
    disp = lax.axis_size("disp")
    space = lax.axis_size("space")
    cols = width // disp
    lanes = -(-(cols + 8) // 128) * 128
    dims = (planes, rows, chans, width, disp, space, cols, lanes)
    count = planes * disp
    n = planes * rows * chans

    own = jnp.transpose(volume, (1, 2, 0, 3)).reshape(planes, rows * chans, width)
    sends = call(
        functools.partial(split_body, dims),
        "split",
        [((n + 12 * planes, lanes), BF16, True)] * disp,
        own, prior_logits,
        scratch=[pltpu.VMEM((4 * planes, width), F32)],
    )
    pieces = exchange(sends, "disp")

    xr = rows + 8
    hr = rows + 6
    base1 = jnp.transpose(w_first, (2, 3, 0, 1, 4)).astype(F32)
    base1 = jnp.pad(base1, ((0, 0), (0, 0), (0, 0), (0, xr - 3), (0, 0))).reshape(3 * chans, 3 * xr * chans)
    base1 = jnp.pad(base1, ((0, 0), (0, -base1.shape[1] % 128)))
    base2 = jnp.transpose(w_second, (2, 0, 1, 3)).astype(F32)
    base2 = jnp.pad(base2, ((0, 0), (0, 0), (0, hr - 3), (0, 0))).reshape(3, 3 * hr * chans)
    base2 = jnp.pad(base2, ((0, 5), (0, -base2.shape[1] % 128)))
    base3 = jnp.transpose(w_second[::-1, ::-1], (2, 3, 0, 1)).astype(F32)
    base3 = jnp.pad(base3, ((0, 0), (0, 0), (0, 0), (0, 16 - 3))).reshape(3 * chans, 3 * 16)
    base3 = jnp.pad(base3, ((0, 0), (0, 128 - base3.shape[1])))
    base4 = jnp.transpose(w_first[::-1, ::-1], (2, 4, 0, 1, 3)).astype(F32)
    base4 = jnp.pad(base4, ((0, 0), (0, 0), (0, 0), (0, rows - 1), (0, 0))).reshape(
        3 * chans, 3 * (rows + 2) * chans
    )
    base4 = jnp.pad(base4, ((0, 0), (0, -base4.shape[1] % 128)))
    bands = call(
        functools.partial(bands_body, dims),
        "bands",
        (
            ((3 * hr * chans, 3 * xr * chans), BF16, True),
            ((3 * (rows + 4), 3 * hr * chans), BF16, True),
            ((3 * (rows + 2) * chans, 3 * 16), BF16, True),
            ((3 * rows * chans, 3 * (rows + 2) * chans), BF16, True),
            ((hr * chans, 2 * lanes), F32, True),
        ),
        base1, base2, base3, base4, b_first[None, :],
    )

    extra = -(-(6 * count + 6) // 16) * 16
    send_one, send_two, prior, cot = call(
        flipped(functools.partial(rows_body, dims), disp),
        "rows",
        (
            ((n * disp + extra, lanes), BF16, True),
            ((n * disp + extra, lanes), BF16, True),
            ((count, rows + 4, lanes), F32, True),
            ((rows + 4, lanes), F32, True),
        ),
        *pieces[::-1], cotangent,
        scratch=[pltpu.VMEM((extra, lanes), F32)],
    )
    z_one = lax.ppermute(send_one, "space", swap_pairs(space, 0))
    z_two = lax.ppermute(send_two, "space", swap_pairs(space, 1))

    tail = 3 * (3 * chans + 8) + 32
    backs = call(
        functools.partial(main_body, dims),
        "main",
        [((n + tail, lanes), BF16, True)] * disp,
        send_one, z_one, z_two, prior, cot, *bands,
        scratch=[
            pltpu.VMEM(((count + 3) * xr * chans, lanes), BF16),
            pltpu.VMEM(((count + 3) * hr * chans, lanes), BF16),
            pltpu.VMEM((count, (rows + 2) * chans, lanes), F32),
            pltpu.VMEM((count, rows + 4, lanes), F32),
            pltpu.VMEM((rows + 4, lanes), F32),
            pltpu.VMEM(((count + 2) * 16, lanes), BF16),
            pltpu.VMEM(((count + 2) * (rows + 2) * chans, lanes), BF16),
            pltpu.VMEM((n * disp, lanes), BF16),
        ],
    )
    backs = exchange(backs, "disp")
    (pay,) = call(
        flipped(functools.partial(sum_body, chans), disp),
        "sum",
        (((3 * chans + 8, lanes), F32, True),),
        *backs[::-1],
    )
    stages = radix_stages(space)
    for k, steps in enumerate(stages):
        parts = [pay] + [lax.ppermute(pay, "space", [(i, i ^ s) for i in range(space)]) for s in steps]
        if k < len(stages) - 1:
            pay = tree_sum(parts)

    volume_grad, disparity = call(
        functools.partial(join_body, dims),
        "join",
        (((chans, planes, rows, width), BF16, False), ((rows, width), F32, False)),
        *backs,
    )

    scale = 16.0 / math.sqrt(planes * disp * rows * space * width)
    first_sum, bias_sum, second_sum = call(
        functools.partial(finish_body, chans, scale),
        "finish",
        (
            ((3, 3, 3, chans, chans), F32, False),
            ((1, chans), F32, False),
            ((3, 3, 3, chans), F32, False),
        ),
        *parts,
    )
    return (volume_grad, first_sum, bias_sum[0], second_sum, disparity)


def solution(mesh):
    return jax.shard_map(
        shards,
        mesh=mesh,
        in_specs=(
            P(None, "disp", ("groups", "space"), None),
            P(),
            P(),
            P(),
            P("disp", ("groups", "space"), None),
            P(("groups", "space"), None),
        ),
        out_specs=(
            P(None, "disp", ("groups", "space"), None),
            P(None, None, None, "groups", None),
            P("groups"),
            P(None, None, None, "groups"),
            P(("groups", "space"), None),
        ),
        check_vma=False,
    )
```

```python
import functools
import math

import jax
import jax.numpy as jnp
from jax import lax
from jax.experimental import pallas as pl
from jax.experimental.pallas import tpu as pltpu
from jax.sharding import PartitionSpec as P

F32 = jnp.float32
BF16 = jnp.bfloat16


def swap_pairs(count, step):
    pairs = []
    for i in range(count):
        j = i ^ 1 if step == 0 else ((i + 1) ^ 1) - 1
        pairs.append((i, j if 0 <= j < count else i))
    return pairs


def radix_stages(count):
    stages = []
    bit = 1
    while bit < count:
        if bit * 4 <= count:
            stages.append((bit, 2 * bit, 3 * bit))
            bit *= 4
        else:
            stages.append((bit,))
            bit *= 2
    return stages


def shift_up(x):
    return pltpu.roll(x, 1, 1)


def shift_down(x):
    return pltpu.roll(x, x.shape[1] - 1, 1)


def left(x, amount):
    return x if amount == 0 else pltpu.roll(x, x.shape[1] - amount, 1)


def right(x, amount):
    return x if amount == 0 else pltpu.roll(x, amount, 1)


def call(body, name, outs, *operands, scratch=()):
    operands = [pltpu.with_memory_space_constraint(x, pltpu.VMEM) for x in operands]
    return pl.pallas_call(
        body,
        out_shape=tuple(
            pltpu.VMEM(shape, dtype) if inside else jax.ShapeDtypeStruct(shape, dtype)
            for shape, dtype, inside in outs
        ),
        in_specs=[pl.BlockSpec(memory_space=pltpu.VMEM)] * len(operands),
        out_specs=tuple(pl.BlockSpec(memory_space=pltpu.VMEM) for _ in outs),
        scratch_shapes=list(scratch),
        name=name,
    )(*operands)


def dot(a, b):
    return lax.dot_general(a, b, (((1,), (0,)), ((), ())), preferred_element_type=F32)


def dot_t(a, b):
    return lax.dot_general(a, b, (((1,), (1,)), ((), ())), preferred_element_type=F32)


def terms(value, count=3):
    out = []
    for _ in range(count):
        term = value.astype(BF16).astype(F32)
        out.append(term)
        value = value - term
    return out


def window(x, start, size):
    width = x.shape[1]
    moved = pltpu.roll(x, (width - start) % width, 1)[:, :size]
    column = start + lax.broadcasted_iota(jnp.int32, moved.shape, 1)
    return jnp.where((column >= 0) & (column < width), moved, 0.0)


def lanes_of(x):
    return lax.broadcasted_iota(jnp.int32, x.shape, 1)


def pack(x):
    n = x.shape[0]
    far = pltpu.roll(x[n // 2 :], 64, 1)
    out = [jnp.where(lanes_of(far) < 64, x[: n // 2], far)]
    for t in range(-(-n // 128)):
        rest = jnp.zeros((8, 128), F32)
        lane = lanes_of(rest)
        for k in range(16):
            at = (t * 16 + k) * 8
            if at < n:
                moved = pltpu.roll(x[at : at + 8], (8 * k + 64) % 128, 1)
                rest = jnp.where((lane >= 8 * k) & (lane < 8 * k + 8), moved, rest)
        out.append(rest)
    return out


def unpack(main, rest, k):
    n = main.shape[0]
    value = main[8 * k : 8 * k + 8] if 8 * k < n else pltpu.roll(main[8 * k - n : 8 * k - n + 8], 64, 1)
    moved = rest[8 * (k // 16) : 8 * (k // 16) + 8]
    moved = pltpu.roll(moved, (64 - 8 * (k % 16)) % 128, 1)
    return jnp.where(lanes_of(value) < 64, value, moved)


def split_body(dims, own_ref, prior_ref, *refs):
    planes, rows, chans, width, disp, space, cols, lanes = dims
    out_refs = refs[:disp]
    wide_ref = refs[disp]
    di = lax.axis_index("disp")
    half = 2 * planes
    for h in range(2):
        for p in range(planes):
            at = h * half + 2 * p
            wide_ref[at : at + 2] = prior_ref[p, 2 * h : 2 * h + 2]
    wide = wide_ref[...]
    n = planes * rows * chans
    pieces = [own_ref[...].reshape(n, width).astype(F32)]
    for h in range(2):
        pieces += terms(wide[h * half : (h + 1) * half])
    whole = jnp.concatenate(pieces, axis=0)
    for s in range(disp):
        start = (di ^ s) * cols - 4
        moved = window(whole, start, lanes)
        out_refs[s][...] = jnp.concatenate(pack(moved[:n]) + pack(moved[n:]), axis=0).astype(BF16)


def rows_body(dims, *refs):
    planes, rows, chans, width, disp, space, cols, lanes = dims
    piece_refs = refs[:disp]
    cot_in_ref, one_ref, two_ref, prior_ref, cot_ref, wide_ref, rest_ref = refs[disp:]
    di = lax.axis_index("disp")
    even = lax.axis_index("space") % 2 == 0
    n = planes * rows * chans
    half = n // 2
    group = 2 * planes
    cot = window(jnp.concatenate([cot_in_ref[...]] * 2, axis=0), di * cols - 4, lanes)[:rows]
    cot_ref[...] = jnp.zeros(cot_ref.shape, F32)
    cot_ref[2 : 2 + rows] = cot
    fine = []
    for s in range(disp):
        g = di ^ s
        block = piece_refs[s][:half]
        at = pl.multiple_of(g * half, half)
        one_ref[pl.ds(at, half)] = block
        two_ref[pl.ds(at, half)] = block
        value = piece_refs[s][half:].astype(F32)
        rest_ref[pl.ds(pl.multiple_of(g * 8, 8), 8)] = value[:8]
        value = value[8:]
        value = [unpack(value[: 3 * group], value[3 * group :], k) for k in range(6)]
        fine.append(value)
        for h in range(2):
            prior = value[3 * h] + value[3 * h + 1] + value[3 * h + 2]
            for p in range(planes):
                prior_ref[g * planes + p, 2 + 2 * h : 4 + 2 * h] = prior[2 * p : 2 * p + 2]
    for out_ref, down in ((one_ref, even), (two_ref, jnp.logical_not(even))):

        def put(h):
            for s in range(disp):
                at = pl.multiple_of((di ^ s) * 3 * group, 8)
                wide_ref[pl.ds(at, 3 * group)] = jnp.concatenate(fine[s][3 * h : 3 * h + 3], axis=0)
            for t, term in enumerate(terms(cot_ref[2 + 2 * h : 4 + 2 * h])):
                at = disp * 3 * group + 2 * t
                wide_ref[at : at + 2] = term
            rest = disp * 3 * group + 6
            wide_ref[rest:] = jnp.zeros((wide_ref.shape[0] - rest, lanes), F32)

        pl.when(down)(functools.partial(put, 1))
        pl.when(jnp.logical_not(down))(functools.partial(put, 0))
        out_ref[disp * half :] = jnp.concatenate([rest_ref[...]] + pack(wide_ref[...]), axis=0).astype(BF16)


def bands_body(dims, base1_ref, base2_ref, base3_ref, base4_ref, bias_ref, band1_ref, band2_ref, band3_ref, band4_ref, col_ref):
    planes, rows, chans, width, disp, space, cols, lanes = dims

    def band(base, groups, count, step, used):
        pieces = []
        for c in range(3):
            piece = base[c * groups : (c + 1) * groups]
            for r in range(count):
                pieces.append(right(piece, step * r))
        return jnp.concatenate(pieces, axis=0)[:, :used].astype(BF16)

    band1_ref[...] = band(base1_ref[...], chans, rows + 6, chans, band1_ref.shape[1])
    band2_ref[...] = band(base2_ref[...], 1, rows + 4, chans, band2_ref.shape[1])
    band3_ref[...] = band(base3_ref[...], chans, rows + 2, 1, band3_ref.shape[1])
    band4 = band(base4_ref[...], chans, rows, chans, band4_ref.shape[1])
    n = rows * chans
    to = lax.broadcasted_iota(jnp.int32, (3 * n, 3 * n), 0)
    at = lax.broadcasted_iota(jnp.int32, (3 * n, 3 * n), 1)
    source = (to // n) * n + (to % rows) * chans + (to % n) // rows
    band4_ref[...] = dot((at == source).astype(BF16), band4).astype(BF16)
    diag = lax.broadcasted_iota(jnp.int32, (chans, chans), 0) == lax.broadcasted_iota(
        jnp.int32, (chans, chans), 1
    )
    bias = jnp.sum(jnp.where(diag, bias_ref[...], 0.0), axis=1, keepdims=True)
    col_ref[...] = jnp.concatenate([jnp.broadcast_to(bias, (chans, 2 * lanes))] * (rows + 6), axis=0)


def main_body(dims, *refs):
    planes, rows, chans, width, disp, space, cols, lanes = dims
    own_ref, za_ref, zb_ref, prior_in_ref, cot_in_ref, band1_ref, band2_ref, band3_ref, band4_ref, col_ref = refs[:10]
    back_refs = refs[10 : 10 + disp]
    x_ref, h_ref, slope_ref, prior_ref, cot_ref, s_ref, pg_ref, v_ref = refs[10 + disp :]
    zi = lax.axis_index("space")
    di = lax.axis_index("disp")
    z_even = zi % 2 == 0
    count = planes * disp
    n = count * rows * chans
    block = rows * chans
    xr = (rows + 8) * chans
    hr = (rows + 6) * chans
    gr = (rows + 2) * chans
    lr = rows + 4
    sr = 16
    two = 2 * lanes

    def place_rows(src, row):
        main = src[: n // 2].astype(F32)
        rest = src[n // 2 : n // 2 + 8 * disp].astype(F32)
        side = planes * block // 2
        for k in range(count):
            g = k // planes
            p = k % planes
            value = [
                unpack(main[g * side : (g + 1) * side], rest[8 * g : 8 * g + 8], p * rows + r) for r in range(rows)
            ]
            at = (k + 1) * xr + row * chans
            x_ref[at : at + block] = jnp.concatenate(value, axis=0).astype(BF16)

    x_ref[:xr] = jnp.zeros((xr, lanes), BF16)
    x_ref[(count + 1) * xr :] = jnp.zeros((2 * xr, lanes), BF16)
    h_ref[:hr] = jnp.zeros((hr, lanes), BF16)
    h_ref[(count + 1) * hr :] = jnp.zeros((2 * hr, lanes), BF16)
    s_ref[...] = jnp.zeros(s_ref.shape, BF16)
    pg_ref[:gr] = jnp.zeros((gr, lanes), BF16)
    pg_ref[(count + 1) * gr :] = jnp.zeros((gr, lanes), BF16)
    place_rows(own_ref, 4)
    prior_ref[...] = prior_in_ref[...]
    cot_ref[...] = cot_in_ref[...]
    half = 2 * planes

    def place(ok, first, one, other, row, at8):
        def put(src):
            if src is None:
                for k in range(count):
                    at = (k + 1) * xr + row * chans
                    x_ref[at : at + 4 * chans] = jnp.zeros((4 * chans, lanes), BF16)
                    prior_ref[k, at8 : at8 + 2] = jnp.zeros((2, lanes), F32)
                cot_ref[at8 : at8 + 2] = jnp.zeros((2, lanes), F32)
                return
            place_rows(src, row)
            extra = src[n // 2 + 8 * disp :].astype(F32)
            used = -(-(3 * half * disp + 6) // 16) * 16
            value = [unpack(extra[: used // 2], extra[used // 2 :], k) for k in range(3 * disp + 1)]
            for g in range(disp):
                prior = value[3 * g] + value[3 * g + 1] + value[3 * g + 2]
                for p in range(planes):
                    prior_ref[g * planes + p, at8 : at8 + 2] = prior[2 * p : 2 * p + 2]
            cot = value[3 * disp]
            cot_ref[at8 : at8 + 2] = cot[:2] + cot[2:4] + cot[4:6]

        pl.when(ok & first)(lambda: put(one))
        pl.when(ok & jnp.logical_not(first))(lambda: put(other))
        pl.when(jnp.logical_not(ok))(lambda: put(None))

    place(zi > 0, z_even, zb_ref, za_ref, 0, 0)
    place(zi < space - 1, z_even, za_ref, zb_ref, 4 + rows, 2 + rows)

    def pair(ref, p, size, taken):
        return jnp.concatenate([ref[p * size : p * size + taken], ref[(p + 1) * size : (p + 1) * size + taken]], axis=1)

    lane = lax.broadcasted_iota(jnp.int32, (hr, two), 1) % lanes
    column = di * cols - 4 + lane
    row_at = zi * rows - 3 + lax.broadcasted_iota(jnp.int32, (hr, two), 0) // chans
    inside = ((row_at >= 0) & (row_at < space * rows) & (column >= 0) & (column < width)).astype(F32)
    band1 = band1_ref[...]
    bias = col_ref[...]
    for p in range(0, count, 2):
        y = dot(band1, pair(x_ref, p, xr, 3 * xr))
        pre = y[hr : 2 * hr] + shift_up(y[:hr]) + shift_down(y[2 * hr :]) + bias
        sig = jax.nn.sigmoid(pre)
        hidden = (pre * sig * inside).astype(BF16)
        slope = (sig * (1.0 + pre * (1.0 - sig)) * inside)[2 * chans : hr - 2 * chans]
        for q in range(2):
            part = slice(q * lanes, (q + 1) * lanes)
            h_ref[(p + q + 1) * hr : (p + q + 2) * hr] = hidden[:, part]
            slope_ref[p + q] = slope[:, part]

    band2 = band2_ref[...]
    logits = []
    for p in range(0, count, 2):
        y = dot(band2, pair(h_ref, p, hr, 3 * hr))
        y = y[lr : 2 * lr] + shift_up(y[:lr]) + shift_down(y[2 * lr :])
        logits += [y[:, :lanes] + prior_ref[p], y[:, lanes:] + prior_ref[p + 1]]

    top = logits[0]
    for value in logits[1:]:
        top = jnp.maximum(top, value)
    summed = jnp.zeros((lr, lanes), F32)
    moment = jnp.zeros((lr, lanes), F32)
    weights = []
    for k, value in enumerate(logits):
        e = jnp.exp(value - top)
        weights.append(e)
        summed = summed + e
        moment = moment + e * ((k + 0.5) / count)
    disparity = moment / summed
    coef = cot_ref[...] / summed
    mine = lax.broadcasted_iota(jnp.int32, (lr, lanes), 1)
    mine = (mine >= 4) & (mine < 4 + cols)
    left2 = []
    for k in range(count):
        score = (coef * weights[k] * ((k + 0.5) / count - disparity)).astype(BF16)
        s_ref[(k + 1) * sr : (k + 1) * sr + lr] = score
        score = jnp.where(mine, score.astype(F32), 0.0)
        left2.append(jnp.concatenate([shift_down(score), score, shift_up(score)], axis=0).astype(BF16))

    band3 = band3_ref[...]
    mine = lax.broadcasted_iota(jnp.int32, (block, two), 1) % lanes
    mine = (mine >= 4) & (mine < 4 + cols)
    bias_sum = jnp.zeros((chans, two), F32)
    left1 = []
    for p in range(0, count, 2):
        y = dot(band3, pair(s_ref, p, sr, 3 * sr))
        hg = y[gr : 2 * gr] + shift_down(y[:gr]) + shift_up(y[2 * gr :])
        slope = jnp.concatenate([slope_ref[p], slope_ref[p + 1]], axis=1)
        pg = (hg * slope).astype(BF16)
        for q in range(2):
            pg_ref[(p + q + 1) * gr : (p + q + 2) * gr] = pg[:, q * lanes : (q + 1) * lanes]
        own = jnp.where(mine, pg.astype(F32)[chans : chans + block], 0.0)
        moved = (shift_down(own), own, shift_up(own))
        pieces = []
        for r in range(rows):
            part = slice(r * chans, (r + 1) * chans)
            bias_sum = bias_sum + own[part]
            pieces += [moved[c][part] for c in range(3)]
        left1.append(jnp.concatenate(pieces, axis=0).astype(BF16))

    inner = (rows + 4) * chans
    acc1 = None
    acc2 = None
    for p in range(0, count, 2):
        rhs = []
        for q in range(2):
            at = [(p + q + a) * xr + 2 * chans for a in range(4)]
            rhs.append(jnp.concatenate([x_ref[k : k + inner] for k in at], axis=0))
        part = dot_t(left1[p // 2], jnp.concatenate(rhs, axis=1))
        acc1 = part if acc1 is None else acc1 + part
        lhs = jnp.concatenate([left2[p], left2[p + 1]], axis=1)
        part = dot_t(lhs, pair(h_ref, p, hr, 4 * hr))
        acc2 = part if acc2 is None else acc2 + part

    out1 = jnp.zeros((3 * chans, acc1.shape[1]), F32)
    for r in range(rows):
        out1 = out1 + left(acc1[3 * chans * r : 3 * chans * (r + 1)], chans * (r + 1))
    acc2 = acc2[:, :256]
    row_in = lax.broadcasted_iota(jnp.int32, acc2.shape, 0) % lr
    out2 = jnp.zeros(acc2.shape, F32)
    for r in range(2, 2 + rows):
        out2 = out2 + jnp.where(row_in == r, left(acc2, chans * r), 0.0)
    out2 = jnp.concatenate(
        [jnp.sum(out2[c * lr : (c + 1) * lr], axis=0, keepdims=True) for c in range(3)]
        + [jnp.zeros((5, out2.shape[1]), F32)],
        axis=0,
    )
    tap = 3 * chans

    def packed(out, pitch):
        lane_p = lax.broadcasted_iota(jnp.int32, (out.shape[0], lanes), 1)
        total = jnp.zeros((out.shape[0], lanes), F32)
        for a in range(3):
            moved = left(out, a * (pitch - tap))[:, :lanes]
            total = jnp.where((lane_p >= a * tap) & (lane_p < (a + 1) * tap), moved, total)
        return total

    bias_sum = jnp.sum(bias_sum, axis=1, keepdims=True)
    sub = lax.broadcasted_iota(jnp.int32, (chans, lanes), 0)
    lane_b = lax.broadcasted_iota(jnp.int32, (chans, lanes), 1)
    bias_sum = jnp.sum(jnp.where(sub == lane_b, bias_sum, 0.0), axis=0, keepdims=True)
    second = packed(out2, hr)
    row_in = lax.broadcasted_iota(jnp.int32, second.shape, 0)
    second = jnp.where(row_in == 3, bias_sum, second)
    payload = jnp.concatenate([packed(out1, inner), second], axis=0)
    shown = jnp.concatenate([disparity[2 : 2 + rows]] * 2, axis=0)
    tail = jnp.concatenate(terms(payload, 2) + terms(shown, 2), axis=0).astype(BF16)

    band4 = band4_ref[...]
    found = [None] * planes
    for p in range(0, count, 2):
        y = dot(band4, pair(pg_ref, p, gr, 3 * gr))
        y = y[block : 2 * block] + shift_down(y[:block]) + shift_up(y[2 * block :])
        for q in range(2):
            moved = y[:, q * lanes : (q + 1) * lanes]
            k = p + q
            found[k % planes] = moved
        if (p + 2) % planes == 0:
            near = jnp.concatenate(found[: planes // 2], axis=0)
            far = jnp.concatenate(found[planes // 2 :], axis=0)
            near = pltpu.roll(near, lanes - 4, 1)
            far = pltpu.roll(far, 60, 1)
            at = (p // planes) * (planes * block // 2)
            v_ref[at : at + planes * block // 2] = jnp.where(lanes_of(near) < 64, near, far).astype(BF16)
    size = planes * block // 2
    for s in range(disp):
        back_refs[s][:size] = v_ref[pl.ds(pl.multiple_of((di ^ s) * size, size), size)]
        back_refs[s][size:] = tail


def sum_body(chans, *refs):
    parts = refs[:-1]
    k = 3 * chans + 8
    sums = []
    for r in parts:
        n = r.shape[0] - 2 * k - 16
        value = r[n:].astype(F32)
        sums.append(value[:k] + value[k : 2 * k])
    refs[-1][...] = tree_sum(sums)


def join_body(dims, *refs):
    planes, rows, chans, width, disp, space, cols, lanes = dims
    parts = refs[:disp]
    grad_ref, disp_ref = refs[disp:]
    di = lax.axis_index("disp")
    n = planes * rows * chans
    k = 2 * (3 * chans + 8)
    total = None
    for s in range(disp):
        j = di ^ s
        shown = parts[s][n // 2 + k :].astype(F32)
        shown = pltpu.roll(shown[:8] + shown[8:], lanes - 4, 1)
        main = parts[s][: n // 2].astype(F32)
        value = jnp.concatenate([main, pltpu.roll(main, 64, 1), shown], axis=0)
        value = jnp.where(lanes_of(value) < cols, value, 0.0)
        value = jnp.concatenate([value, jnp.zeros((value.shape[0], width - lanes), F32)], axis=1)
        value = pltpu.roll(value, j * cols, 1)
        total = value if total is None else total + value
    disp_ref[...] = total[n : n + rows]
    grad = total[:n].astype(BF16)
    for p in range(planes):
        for i in range(chans):
            at = (p * chans + i) * rows
            grad_ref[i, p] = grad[at : at + rows]


def tree_sum(parts):
    while len(parts) > 1:
        parts = [parts[k] + parts[k + 1] for k in range(0, len(parts), 2)]
    return parts[0]


def finish_body(chans, scale, *refs):
    gw_ref, gb_ref, gs_ref = refs[-3:]
    total = tree_sum([r[...] for r in refs[:-3]]) * scale
    for a in range(3):
        for b in range(3):
            at = (a * 3 + b) * chans
            for c in range(3):
                gw_ref[a, b, c] = total[c * chans : (c + 1) * chans, at : at + chans]
            gs_ref[a, b] = total[3 * chans : 3 * chans + 3, at : at + chans]
    gb_ref[...] = total[3 * chans + 3 : 3 * chans + 4, :chans]


def flipped(body, count):
    def run(*refs):
        return body(*refs[:count][::-1], *refs[count:])

    return run


def exchange(sends, axis):
    count = lax.axis_size(axis)
    return [sends[0]] + [
        lax.ppermute(sends[s], axis, [(i, i ^ s) for i in range(count)]) for s in range(1, count)
    ]


def shards(volume, w_first, b_first, w_second, prior_logits, cotangent):
    chans, planes, rows, width = volume.shape
    disp = lax.axis_size("disp")
    space = lax.axis_size("space")
    cols = width // disp
    lanes = -(-(cols + 8) // 128) * 128
    dims = (planes, rows, chans, width, disp, space, cols, lanes)
    count = planes * disp
    n = planes * rows * chans

    own = jnp.transpose(volume, (1, 2, 0, 3)).reshape(planes, rows * chans, width)
    sends = call(
        functools.partial(split_body, dims),
        "split",
        [((n // 2 + 8 + 6 * planes + 8, lanes), BF16, True)] * disp,
        own, prior_logits,
        scratch=[pltpu.VMEM((4 * planes, width), F32)],
    )
    pieces = exchange(sends, "disp")

    xr = rows + 8
    hr = rows + 6
    base1 = jnp.transpose(w_first, (2, 3, 0, 1, 4)).astype(F32)
    base1 = jnp.pad(base1, ((0, 0), (0, 0), (0, 0), (0, xr - 3), (0, 0))).reshape(3 * chans, 3 * xr * chans)
    base1 = jnp.pad(base1, ((0, 0), (0, -base1.shape[1] % 128)))
    base2 = jnp.transpose(w_second, (2, 0, 1, 3)).astype(F32)
    base2 = jnp.pad(base2, ((0, 0), (0, 0), (0, hr - 3), (0, 0))).reshape(3, 3 * hr * chans)
    base2 = jnp.pad(base2, ((0, 5), (0, -base2.shape[1] % 128)))
    base3 = jnp.transpose(w_second[::-1, ::-1], (2, 3, 0, 1)).astype(F32)
    base3 = jnp.pad(base3, ((0, 0), (0, 0), (0, 0), (0, 16 - 3))).reshape(3 * chans, 3 * 16)
    base3 = jnp.pad(base3, ((0, 0), (0, 128 - base3.shape[1])))
    base4 = jnp.transpose(w_first[::-1, ::-1], (2, 4, 0, 1, 3)).astype(F32)
    base4 = jnp.pad(base4, ((0, 0), (0, 0), (0, 0), (0, rows - 1), (0, 0))).reshape(
        3 * chans, 3 * (rows + 2) * chans
    )
    base4 = jnp.pad(base4, ((0, 0), (0, -base4.shape[1] % 128)))
    bands = call(
        functools.partial(bands_body, dims),
        "bands",
        (
            ((3 * hr * chans, 3 * xr * chans), BF16, True),
            ((3 * (rows + 4), 3 * hr * chans), BF16, True),
            ((3 * (rows + 2) * chans, 3 * 16), BF16, True),
            ((3 * rows * chans, 3 * (rows + 2) * chans), BF16, True),
            ((hr * chans, 2 * lanes), F32, True),
        ),
        base1, base2, base3, base4, b_first[None, :],
    )

    extra = -(-(6 * count + 6) // 16) * 16
    sent = (n // 2 + 8) * disp + extra // 2 + 8 * -(-extra // 128)
    send_one, send_two, prior, cot = call(
        flipped(functools.partial(rows_body, dims), disp),
        "rows",
        (
            ((sent, lanes), BF16, True),
            ((sent, lanes), BF16, True),
            ((count, rows + 4, lanes), F32, True),
            ((rows + 4, lanes), F32, True),
        ),
        *pieces[::-1], cotangent,
        scratch=[pltpu.VMEM((extra, lanes), F32), pltpu.VMEM((8 * disp, lanes), F32)],
    )
    z_one = lax.ppermute(send_one, "space", swap_pairs(space, 0))
    z_two = lax.ppermute(send_two, "space", swap_pairs(space, 1))

    tail = 2 * (3 * chans + 8) + 16
    backs = call(
        functools.partial(main_body, dims),
        "main",
        [((n // 2 + tail, lanes), BF16, True)] * disp,
        send_one, z_one, z_two, prior, cot, *bands,
        scratch=[
            pltpu.VMEM(((count + 3) * xr * chans, lanes), BF16),
            pltpu.VMEM(((count + 3) * hr * chans, lanes), BF16),
            pltpu.VMEM((count, (rows + 2) * chans, lanes), F32),
            pltpu.VMEM((count, rows + 4, lanes), F32),
            pltpu.VMEM((rows + 4, lanes), F32),
            pltpu.VMEM(((count + 2) * 16, lanes), BF16),
            pltpu.VMEM(((count + 2) * (rows + 2) * chans, lanes), BF16),
            pltpu.VMEM((n // 2 * disp, lanes), BF16),
        ],
    )
    backs = exchange(backs, "disp")
    (pay,) = call(
        flipped(functools.partial(sum_body, chans), disp),
        "sum",
        (((3 * chans + 8, lanes), F32, True),),
        *backs[::-1],
    )
    stages = radix_stages(space)
    for k, steps in enumerate(stages):
        parts = [pay] + [lax.ppermute(pay, "space", [(i, i ^ s) for i in range(space)]) for s in steps]
        if k < len(stages) - 1:
            pay = tree_sum(parts)

    volume_grad, disparity = call(
        functools.partial(join_body, dims),
        "join",
        (((chans, planes, rows, width), BF16, False), ((rows, width), F32, False)),
        *backs,
    )

    scale = 16.0 / math.sqrt(planes * disp * rows * space * width)
    first_sum, bias_sum, second_sum = call(
        functools.partial(finish_body, chans, scale),
        "finish",
        (
            ((3, 3, 3, chans, chans), F32, False),
            ((1, chans), F32, False),
            ((3, 3, 3, chans), F32, False),
        ),
        *parts,
    )
    return (volume_grad, first_sum, bias_sum[0], second_sum, disparity)


def solution(mesh):
    return jax.shard_map(
        shards,
        mesh=mesh,
        in_specs=(
            P(None, "disp", ("groups", "space"), None),
            P(),
            P(),
            P(),
            P("disp", ("groups", "space"), None),
            P(("groups", "space"), None),
        ),
        out_specs=(
            P(None, "disp", ("groups", "space"), None),
            P(None, None, None, "groups", None),
            P("groups"),
            P(None, None, None, "groups"),
            P(("groups", "space"), None),
        ),
        check_vma=False,
    )
```

```python
import functools
import math

import jax
import jax.numpy as jnp
from jax import lax
from jax.experimental import pallas as pl
from jax.experimental.pallas import tpu as pltpu
from jax.sharding import PartitionSpec as P

F32 = jnp.float32
BF16 = jnp.bfloat16


def swap_pairs(count, step):
    pairs = []
    for i in range(count):
        j = i ^ 1 if step == 0 else ((i + 1) ^ 1) - 1
        pairs.append((i, j if 0 <= j < count else i))
    return pairs


def radix_stages(count):
    stages = []
    bit = 1
    while bit < count:
        if bit * 4 <= count:
            stages.append((bit, 2 * bit, 3 * bit))
            bit *= 4
        else:
            stages.append((bit,))
            bit *= 2
    return stages


def shift_up(x):
    return pltpu.roll(x, 1, 1)


def shift_down(x):
    return pltpu.roll(x, x.shape[1] - 1, 1)


def left(x, amount):
    return x if amount == 0 else pltpu.roll(x, x.shape[1] - amount, 1)


def right(x, amount):
    return x if amount == 0 else pltpu.roll(x, amount, 1)


def call(body, name, outs, *operands, scratch=(), inside=True):
    if inside:
        operands = [pltpu.with_memory_space_constraint(x, pltpu.VMEM) for x in operands]
    return pl.pallas_call(
        body,
        out_shape=tuple(
            pltpu.VMEM(shape, dtype) if inside else jax.ShapeDtypeStruct(shape, dtype)
            for shape, dtype, inside in outs
        ),
        in_specs=[pl.BlockSpec(memory_space=pltpu.VMEM)] * len(operands),
        out_specs=tuple(pl.BlockSpec(memory_space=pltpu.VMEM) for _ in outs),
        scratch_shapes=list(scratch),
        name=name,
    )(*operands)


def dot(a, b):
    return lax.dot_general(a, b, (((1,), (0,)), ((), ())), preferred_element_type=F32)


def dot_t(a, b):
    return lax.dot_general(a, b, (((1,), (1,)), ((), ())), preferred_element_type=F32)


def terms(value, count=3):
    out = []
    for _ in range(count):
        term = value.astype(BF16).astype(F32)
        out.append(term)
        value = value - term
    return out


def window(x, start, size):
    width = x.shape[1]
    moved = pltpu.roll(x, (width - start) % width, 1)[:, :size]
    column = start + lax.broadcasted_iota(jnp.int32, moved.shape, 1)
    return jnp.where((column >= 0) & (column < width), moved, 0.0)


def lanes_of(x):
    return lax.broadcasted_iota(jnp.int32, x.shape, 1)


def pack(x):
    n = x.shape[0]
    far = pltpu.roll(x[n // 2 :], 64, 1)
    out = [jnp.where(lanes_of(far) < 64, x[: n // 2], far)]
    for t in range(-(-n // 128)):
        rest = jnp.zeros((8, 128), F32)
        lane = lanes_of(rest)
        for k in range(16):
            at = (t * 16 + k) * 8
            if at < n:
                moved = pltpu.roll(x[at : at + 8], (8 * k + 64) % 128, 1)
                rest = jnp.where((lane >= 8 * k) & (lane < 8 * k + 8), moved, rest)
        out.append(rest)
    return out


def unpack(main, rest, k):
    n = main.shape[0]
    value = main[8 * k : 8 * k + 8] if 8 * k < n else pltpu.roll(main[8 * k - n : 8 * k - n + 8], 64, 1)
    moved = rest[8 * (k // 16) : 8 * (k // 16) + 8]
    moved = pltpu.roll(moved, (64 - 8 * (k % 16)) % 128, 1)
    return jnp.where(lanes_of(value) < 64, value, moved)


def split_body(dims, volume_ref, prior_ref, *refs):
    planes, rows, chans, width, disp, space, cols, lanes = dims
    out_refs = refs[:disp]
    wide_ref, found_ref = refs[disp : disp + 2]
    own_refs = refs[disp + 2 :]
    di = lax.axis_index("disp")
    group = 2 * planes
    n = planes * rows * chans
    for i in range(chans):
        value = volume_ref[i].astype(F32)
        for p in range(planes):
            for j, ref in enumerate(own_refs):
                ref[pl.ds(p * rows * chans + i, rows, stride=chans)] = value[p][:, j * 128 : (j + 1) * 128]
    for h in range(2):
        for p in range(planes):
            at = h * group + 2 * p
            wide_ref[at : at + 2] = prior_ref[p, 2 * h : 2 * h + 2]
    wide = wide_ref[...]
    pieces = [jnp.concatenate([ref[...] for ref in own_refs], axis=1)]
    for h in range(2):
        pieces += terms(wide[h * group : (h + 1) * group])
    whole = jnp.concatenate(pieces, axis=0)
    for t in range(disp):
        moved = window(whole, t * cols - 4, lanes)
        found_ref[t] = jnp.concatenate(pack(moved[:n]) + pack(moved[n:]), axis=0).astype(BF16)
    for s in range(disp):
        out_refs[s][...] = found_ref[di ^ s]


def rows_body(dims, *refs):
    planes, rows, chans, width, disp, space, cols, lanes = dims
    piece_refs = refs[:disp]
    cot_in_ref, one_ref, two_ref, prior_ref, cot_ref, wide_ref, rest_ref = refs[disp:]
    di = lax.axis_index("disp")
    even = lax.axis_index("space") % 2 == 0
    n = planes * rows * chans
    half = n // 2
    group = 2 * planes
    cot = window(jnp.concatenate([cot_in_ref[...]] * 2, axis=0), di * cols - 4, lanes)[:rows]
    cot_ref[...] = jnp.zeros(cot_ref.shape, F32)
    cot_ref[2 : 2 + rows] = cot
    fine = []
    for s in range(disp):
        g = di ^ s
        block = piece_refs[s][:half]
        at = pl.multiple_of(g * half, half)
        one_ref[pl.ds(at, half)] = block
        two_ref[pl.ds(at, half)] = block
        value = piece_refs[s][half:].astype(F32)
        rest_ref[pl.ds(pl.multiple_of(g * 8, 8), 8)] = value[:8]
        value = value[8:]
        value = [unpack(value[: 3 * group], value[3 * group :], k) for k in range(6)]
        fine.append(value)
        for h in range(2):
            prior = value[3 * h] + value[3 * h + 1] + value[3 * h + 2]
            for p in range(planes):
                prior_ref[g * planes + p, 2 + 2 * h : 4 + 2 * h] = prior[2 * p : 2 * p + 2]
    for out_ref, down in ((one_ref, even), (two_ref, jnp.logical_not(even))):

        def put(h):
            for s in range(disp):
                at = pl.multiple_of((di ^ s) * 3 * group, 8)
                wide_ref[pl.ds(at, 3 * group)] = jnp.concatenate(fine[s][3 * h : 3 * h + 3], axis=0)
            for t, term in enumerate(terms(cot_ref[2 + 2 * h : 4 + 2 * h])):
                at = disp * 3 * group + 2 * t
                wide_ref[at : at + 2] = term
            rest = disp * 3 * group + 6
            wide_ref[rest:] = jnp.zeros((wide_ref.shape[0] - rest, lanes), F32)

        pl.when(down)(functools.partial(put, 1))
        pl.when(jnp.logical_not(down))(functools.partial(put, 0))
        out_ref[disp * half :] = jnp.concatenate([rest_ref[...]] + pack(wide_ref[...]), axis=0).astype(BF16)


def bands_body(dims, base1_ref, base2_ref, base3_ref, base4_ref, bias_ref, band1_ref, band2_ref, band3_ref, band4_ref, col_ref):
    planes, rows, chans, width, disp, space, cols, lanes = dims

    def band(base, groups, count, step, used):
        pieces = []
        for c in range(3):
            piece = base[c * groups : (c + 1) * groups]
            for r in range(count):
                pieces.append(right(piece, step * r))
        return jnp.concatenate(pieces, axis=0)[:, :used].astype(BF16)

    band1_ref[...] = band(base1_ref[...], chans, rows + 2, chans, band1_ref.shape[1])
    band2_ref[...] = band(base2_ref[...], 1, rows + 4, chans, band2_ref.shape[1])
    band3_ref[...] = band(base3_ref[...], chans, rows + 2, 1, band3_ref.shape[1])
    band4 = band(base4_ref[...], chans, rows, chans, band4_ref.shape[1])
    n = rows * chans
    to = lax.broadcasted_iota(jnp.int32, (3 * n, 3 * n), 0)
    at = lax.broadcasted_iota(jnp.int32, (3 * n, 3 * n), 1)
    source = (to // n) * n + (to % rows) * chans + (to % n) // rows
    band4_ref[...] = dot((at == source).astype(BF16), band4).astype(BF16)
    diag = lax.broadcasted_iota(jnp.int32, (chans, chans), 0) == lax.broadcasted_iota(
        jnp.int32, (chans, chans), 1
    )
    bias = jnp.sum(jnp.where(diag, bias_ref[...], 0.0), axis=1, keepdims=True)
    col_ref[...] = jnp.concatenate([jnp.broadcast_to(bias, (chans, 2 * lanes))] * (rows + 6), axis=0)


def main_body(dims, *refs):
    planes, rows, chans, width, disp, space, cols, lanes = dims
    own_ref, za_ref, zb_ref, prior_in_ref, cot_in_ref, band1_ref, band2_ref, band3_ref, band4_ref, col_ref = refs[:10]
    back_refs = refs[10 : 10 + disp]
    x_ref, h_ref, slope_ref, prior_ref, cot_ref, s_ref, pg_ref, v_ref = refs[10 + disp :]
    zi = lax.axis_index("space")
    di = lax.axis_index("disp")
    z_even = zi % 2 == 0
    count = planes * disp
    n = count * rows * chans
    block = rows * chans
    xr = (rows + 8) * chans
    hr = (rows + 6) * chans
    gr = (rows + 2) * chans
    lr = rows + 4
    sr = 16
    two = 2 * lanes

    def place_rows(src, row):
        main = src[: n // 2].astype(F32)
        rest = src[n // 2 : n // 2 + 8 * disp].astype(F32)
        side = planes * block // 2
        for k in range(count):
            g = k // planes
            p = k % planes
            value = [
                unpack(main[g * side : (g + 1) * side], rest[8 * g : 8 * g + 8], p * rows + r) for r in range(rows)
            ]
            at = (k + 1) * xr + row * chans
            x_ref[at : at + block] = jnp.concatenate(value, axis=0).astype(BF16)

    x_ref[:xr] = jnp.zeros((xr, lanes), BF16)
    x_ref[(count + 1) * xr :] = jnp.zeros((2 * xr, lanes), BF16)
    h_ref[:hr] = jnp.zeros((hr, lanes), BF16)
    h_ref[(count + 1) * hr :] = jnp.zeros((2 * hr, lanes), BF16)
    s_ref[...] = jnp.zeros(s_ref.shape, BF16)
    pg_ref[:gr] = jnp.zeros((gr, lanes), BF16)
    pg_ref[(count + 1) * gr :] = jnp.zeros((gr, lanes), BF16)
    place_rows(own_ref, 4)
    prior_ref[...] = prior_in_ref[...]
    cot_ref[...] = cot_in_ref[...]
    half = 2 * planes

    def place(ok, first, one, other, row, at8):
        def put(src):
            if src is None:
                for k in range(count):
                    at = (k + 1) * xr + row * chans
                    x_ref[at : at + 4 * chans] = jnp.zeros((4 * chans, lanes), BF16)
                    prior_ref[k, at8 : at8 + 2] = jnp.zeros((2, lanes), F32)
                cot_ref[at8 : at8 + 2] = jnp.zeros((2, lanes), F32)
                return
            place_rows(src, row)
            extra = src[n // 2 + 8 * disp :].astype(F32)
            used = -(-(3 * half * disp + 6) // 16) * 16
            value = [unpack(extra[: used // 2], extra[used // 2 :], k) for k in range(3 * disp + 1)]
            for g in range(disp):
                prior = value[3 * g] + value[3 * g + 1] + value[3 * g + 2]
                for p in range(planes):
                    prior_ref[g * planes + p, at8 : at8 + 2] = prior[2 * p : 2 * p + 2]
            cot = value[3 * disp]
            cot_ref[at8 : at8 + 2] = cot[:2] + cot[2:4] + cot[4:6]

        pl.when(ok & first)(lambda: put(one))
        pl.when(ok & jnp.logical_not(first))(lambda: put(other))
        pl.when(jnp.logical_not(ok))(lambda: put(None))

    place(zi > 0, z_even, zb_ref, za_ref, 0, 0)
    place(zi < space - 1, z_even, za_ref, zb_ref, 4 + rows, 2 + rows)

    def pair(ref, p, size, taken):
        return jnp.concatenate([ref[p * size : p * size + taken], ref[(p + 1) * size : (p + 1) * size + taken]], axis=1)

    lane = lax.broadcasted_iota(jnp.int32, (hr, two), 1) % lanes
    column = di * cols - 4 + lane
    row_at = zi * rows - 3 + lax.broadcasted_iota(jnp.int32, (hr, two), 0) // chans
    inside = ((row_at >= 0) & (row_at < space * rows) & (column >= 0) & (column < width)).astype(F32)
    band1 = band1_ref[...]
    bias = col_ref[...]
    yr = (rows + 2) * chans
    wr = (rows + 4) * chans
    for p in range(0, count, 2):
        pre = []
        for at in (0, 4 * chans):
            rhs = [
                jnp.concatenate(
                    [x_ref[(p + q + a) * xr + at : (p + q + a) * xr + at + wr] for a in range(3)], axis=0
                )
                for q in range(2)
            ]
            y = dot(band1, jnp.concatenate(rhs, axis=1))
            skip = at // 2
            y = [y[c * yr + skip : (c + 1) * yr] for c in range(3)]
            pre.append(y[1] + shift_up(y[0]) + shift_down(y[2]))
        pre = jnp.concatenate(pre, axis=0) + bias
        sig = 0.5 * jnp.tanh(0.5 * pre) + 0.5
        hidden = (pre * sig * inside).astype(BF16)
        slope = (sig * (1.0 + pre * (1.0 - sig)) * inside)[2 * chans : hr - 2 * chans]
        for q in range(2):
            part = slice(q * lanes, (q + 1) * lanes)
            h_ref[(p + q + 1) * hr : (p + q + 2) * hr] = hidden[:, part]
            slope_ref[p + q] = slope[:, part]

    band2 = band2_ref[...]
    logits = []
    for p in range(0, count, 2):
        y = dot(band2, pair(h_ref, p, hr, 3 * hr))
        y = y[lr : 2 * lr] + shift_up(y[:lr]) + shift_down(y[2 * lr :])
        logits += [y[:, :lanes] + prior_ref[p], y[:, lanes:] + prior_ref[p + 1]]

    top = logits[0]
    for value in logits[1:]:
        top = jnp.maximum(top, value)
    summed = jnp.zeros((lr, lanes), F32)
    moment = jnp.zeros((lr, lanes), F32)
    weights = []
    for k, value in enumerate(logits):
        e = jnp.exp(value - top)
        weights.append(e)
        summed = summed + e
        moment = moment + e * ((k + 0.5) / count)
    disparity = moment / summed
    coef = cot_ref[...] / summed
    mine = lax.broadcasted_iota(jnp.int32, (lr, lanes), 1)
    mine = (mine >= 4) & (mine < 4 + cols)
    left2 = []
    for k in range(count):
        score = (coef * weights[k] * ((k + 0.5) / count - disparity)).astype(BF16)
        s_ref[(k + 1) * sr : (k + 1) * sr + lr] = score
        score = jnp.where(mine, score.astype(F32), 0.0)
        left2.append(jnp.concatenate([shift_down(score), score, shift_up(score)], axis=0).astype(BF16))

    band3 = band3_ref[...]
    mine = lax.broadcasted_iota(jnp.int32, (block, two), 1) % lanes
    mine = (mine >= 4) & (mine < 4 + cols)
    bias_sum = jnp.zeros((chans, two), F32)
    left1 = []
    for p in range(0, count, 2):
        y = dot(band3, pair(s_ref, p, sr, 3 * sr))
        hg = y[gr : 2 * gr] + shift_down(y[:gr]) + shift_up(y[2 * gr :])
        slope = jnp.concatenate([slope_ref[p], slope_ref[p + 1]], axis=1)
        pg = (hg * slope).astype(BF16)
        for q in range(2):
            pg_ref[(p + q + 1) * gr : (p + q + 2) * gr] = pg[:, q * lanes : (q + 1) * lanes]
        own = jnp.where(mine, pg.astype(F32)[chans : chans + block], 0.0)
        moved = (shift_down(own), own, shift_up(own))
        pieces = []
        for r in range(rows):
            part = slice(r * chans, (r + 1) * chans)
            bias_sum = bias_sum + own[part]
            pieces += [moved[c][part] for c in range(3)]
        left1.append(jnp.concatenate(pieces, axis=0).astype(BF16))

    inner = (rows + 4) * chans
    acc1 = None
    acc2 = None
    for p in range(0, count, 2):
        rhs = []
        for q in range(2):
            at = [(p + q + a) * xr + 2 * chans for a in range(3)]
            rhs.append(jnp.concatenate([x_ref[k : k + inner] for k in at], axis=0))
        part = dot_t(left1[p // 2], jnp.concatenate(rhs, axis=1))
        acc1 = part if acc1 is None else acc1 + part
        lhs = jnp.concatenate([left2[p], left2[p + 1]], axis=1)
        part = dot_t(lhs, pair(h_ref, p, hr, 3 * hr))
        acc2 = part if acc2 is None else acc2 + part

    acc1 = jnp.concatenate([acc1, jnp.zeros((acc1.shape[0], -acc1.shape[1] % 128), F32)], axis=1)
    acc2 = jnp.concatenate([acc2, jnp.zeros((acc2.shape[0], -acc2.shape[1] % 128), F32)], axis=1)
    out1 = jnp.zeros((3 * chans, acc1.shape[1]), F32)
    for r in range(rows):
        out1 = out1 + left(acc1[3 * chans * r : 3 * chans * (r + 1)], chans * (r + 1))
    row_in = lax.broadcasted_iota(jnp.int32, acc2.shape, 0) % lr
    out2 = jnp.zeros(acc2.shape, F32)
    for r in range(2, 2 + rows):
        out2 = out2 + jnp.where(row_in == r, left(acc2, chans * r), 0.0)
    out2 = jnp.concatenate(
        [jnp.sum(out2[c * lr : (c + 1) * lr], axis=0, keepdims=True) for c in range(3)]
        + [jnp.zeros((5, out2.shape[1]), F32)],
        axis=0,
    )
    tap = 3 * chans

    def packed(out, pitch):
        lane_p = lax.broadcasted_iota(jnp.int32, (out.shape[0], lanes), 1)
        total = jnp.zeros((out.shape[0], lanes), F32)
        for a in range(3):
            moved = left(out, a * (pitch - tap))[:, :lanes]
            total = jnp.where((lane_p >= a * tap) & (lane_p < (a + 1) * tap), moved, total)
        return total

    bias_sum = jnp.sum(bias_sum, axis=1, keepdims=True)
    sub = lax.broadcasted_iota(jnp.int32, (chans, lanes), 0)
    lane_b = lax.broadcasted_iota(jnp.int32, (chans, lanes), 1)
    bias_sum = jnp.sum(jnp.where(sub == lane_b, bias_sum, 0.0), axis=0, keepdims=True)
    second = packed(out2, hr)
    row_in = lax.broadcasted_iota(jnp.int32, second.shape, 0)
    second = jnp.where(row_in == 3, bias_sum, second)
    payload = jnp.concatenate([packed(out1, inner), second], axis=0)
    shown = jnp.concatenate([disparity[2 : 2 + rows]] * 2, axis=0)
    tail = jnp.concatenate(terms(payload, 2) + terms(shown, 2), axis=0).astype(BF16)

    band4 = band4_ref[...]
    found = [None] * planes
    for p in range(0, count, 2):
        y = dot(band4, pair(pg_ref, p, gr, 3 * gr))
        y = y[block : 2 * block] + shift_down(y[:block]) + shift_up(y[2 * block :])
        for q in range(2):
            moved = y[:, q * lanes : (q + 1) * lanes]
            k = p + q
            found[k % planes] = moved
        if (p + 2) % planes == 0:
            near = jnp.concatenate(found[: planes // 2], axis=0)
            far = jnp.concatenate(found[planes // 2 :], axis=0)
            near = pltpu.roll(near, lanes - 4, 1)
            far = pltpu.roll(far, 60, 1)
            at = (p // planes) * (planes * block // 2)
            v_ref[at : at + planes * block // 2] = jnp.where(lanes_of(near) < 64, near, far).astype(BF16)
    size = planes * block // 2
    for s in range(disp):
        back_refs[s][:size] = v_ref[pl.ds(pl.multiple_of((di ^ s) * size, size), size)]
        back_refs[s][size:] = tail


def sum_body(chans, *refs):
    parts = refs[:-1]
    k = 3 * chans + 8
    sums = []
    for r in parts:
        n = r.shape[0] - 2 * k - 16
        value = r[n:].astype(F32)
        sums.append(value[:k] + value[k : 2 * k])
    refs[-1][...] = tree_sum(sums)


def join_body(dims, *refs):
    planes, rows, chans, width, disp, space, cols, lanes = dims
    parts = refs[:disp]
    grad_ref, disp_ref = refs[disp:]
    di = lax.axis_index("disp")
    n = planes * rows * chans
    k = 2 * (3 * chans + 8)
    total = None
    for s in range(disp):
        j = di ^ s
        shown = parts[s][n // 2 + k :].astype(F32)
        shown = pltpu.roll(shown[:8] + shown[8:], lanes - 4, 1)
        main = parts[s][: n // 2].astype(F32)
        value = jnp.concatenate([main, pltpu.roll(main, 64, 1), shown], axis=0)
        value = jnp.where(lanes_of(value) < cols, value, 0.0)
        value = jnp.concatenate([value, jnp.zeros((value.shape[0], width - lanes), F32)], axis=1)
        value = pltpu.roll(value, j * cols, 1)
        total = value if total is None else total + value
    disp_ref[...] = total[n : n + rows]
    grad = total[:n].astype(BF16)
    for p in range(planes):
        for i in range(chans):
            at = (p * chans + i) * rows
            grad_ref[i, p] = grad[at : at + rows]


def tree_sum(parts):
    while len(parts) > 1:
        parts = [parts[k] + parts[k + 1] for k in range(0, len(parts), 2)]
    return parts[0]


def finish_body(chans, scale, *refs):
    gw_ref, gb_ref, gs_ref = refs[-3:]
    total = tree_sum([r[...] for r in refs[:-3]]) * scale
    for a in range(3):
        for b in range(3):
            at = (a * 3 + b) * chans
            for c in range(3):
                gw_ref[a, b, c] = total[c * chans : (c + 1) * chans, at : at + chans]
            gs_ref[a, b] = total[3 * chans : 3 * chans + 3, at : at + chans]
    gb_ref[...] = total[3 * chans + 3 : 3 * chans + 4, :chans]


def flipped(body, count):
    def run(*refs):
        return body(*refs[:count][::-1], *refs[count:])

    return run


def exchange(sends, axis):
    count = lax.axis_size(axis)
    return [sends[0]] + [
        lax.ppermute(sends[s], axis, [(i, i ^ s) for i in range(count)]) for s in range(1, count)
    ]


def shards(volume, w_first, b_first, w_second, prior_logits, cotangent):
    chans, planes, rows, width = volume.shape
    disp = lax.axis_size("disp")
    space = lax.axis_size("space")
    cols = width // disp
    lanes = -(-(cols + 8) // 128) * 128
    dims = (planes, rows, chans, width, disp, space, cols, lanes)
    count = planes * disp
    n = planes * rows * chans

    piece = n // 2 + 8 + 6 * planes + 8
    sends = call(
        functools.partial(split_body, dims),
        "split",
        [((piece, lanes), BF16, True)] * disp,
        volume, prior_logits,
        inside=False,
        scratch=[
            pltpu.VMEM((4 * planes, width), F32),
            pltpu.VMEM((disp, piece, lanes), BF16),
        ]
        + [pltpu.VMEM((n, 128), F32)] * (width // 128),
    )
    pieces = exchange(sends, "disp")

    xr = rows + 8
    hr = rows + 6
    base1 = jnp.transpose(w_first, (2, 3, 0, 1, 4)).astype(F32)
    base1 = jnp.pad(base1, ((0, 0), (0, 0), (0, 0), (0, rows + 1), (0, 0)))
    base1 = base1.reshape(3 * chans, 3 * (rows + 4) * chans)
    base1 = jnp.pad(base1, ((0, 0), (0, -base1.shape[1] % 128)))
    base2 = jnp.transpose(w_second, (2, 0, 1, 3)).astype(F32)
    base2 = jnp.pad(base2, ((0, 0), (0, 0), (0, hr - 3), (0, 0))).reshape(3, 3 * hr * chans)
    base2 = jnp.pad(base2, ((0, 5), (0, -base2.shape[1] % 128)))
    base3 = jnp.transpose(w_second[::-1, ::-1], (2, 3, 0, 1)).astype(F32)
    base3 = jnp.pad(base3, ((0, 0), (0, 0), (0, 0), (0, 16 - 3))).reshape(3 * chans, 3 * 16)
    base3 = jnp.pad(base3, ((0, 0), (0, 128 - base3.shape[1])))
    base4 = jnp.transpose(w_first[::-1, ::-1], (2, 4, 0, 1, 3)).astype(F32)
    base4 = jnp.pad(base4, ((0, 0), (0, 0), (0, 0), (0, rows - 1), (0, 0))).reshape(
        3 * chans, 3 * (rows + 2) * chans
    )
    base4 = jnp.pad(base4, ((0, 0), (0, -base4.shape[1] % 128)))
    bands = call(
        functools.partial(bands_body, dims),
        "bands",
        (
            ((3 * (rows + 2) * chans, 3 * (rows + 4) * chans), BF16, True),
            ((3 * (rows + 4), 3 * hr * chans), BF16, True),
            ((3 * (rows + 2) * chans, 3 * 16), BF16, True),
            ((3 * rows * chans, 3 * (rows + 2) * chans), BF16, True),
            ((hr * chans, 2 * lanes), F32, True),
        ),
        base1, base2, base3, base4, b_first[None, :],
    )

    extra = -(-(6 * count + 6) // 16) * 16
    sent = (n // 2 + 8) * disp + extra // 2 + 8 * -(-extra // 128)
    send_one, send_two, prior, cot = call(
        flipped(functools.partial(rows_body, dims), disp),
        "rows",
        (
            ((sent, lanes), BF16, True),
            ((sent, lanes), BF16, True),
            ((count, rows + 4, lanes), F32, True),
            ((rows + 4, lanes), F32, True),
        ),
        *pieces[::-1], cotangent,
        scratch=[pltpu.VMEM((extra, lanes), F32), pltpu.VMEM((8 * disp, lanes), F32)],
    )
    z_one = lax.ppermute(send_one, "space", swap_pairs(space, 0))
    z_two = lax.ppermute(send_two, "space", swap_pairs(space, 1))

    tail = 2 * (3 * chans + 8) + 16
    backs = call(
        functools.partial(main_body, dims),
        "main",
        [((n // 2 + tail, lanes), BF16, True)] * disp,
        send_one, z_one, z_two, prior, cot, *bands,
        scratch=[
            pltpu.VMEM(((count + 3) * xr * chans, lanes), BF16),
            pltpu.VMEM(((count + 3) * hr * chans, lanes), BF16),
            pltpu.VMEM((count, (rows + 2) * chans, lanes), F32),
            pltpu.VMEM((count, rows + 4, lanes), F32),
            pltpu.VMEM((rows + 4, lanes), F32),
            pltpu.VMEM(((count + 2) * 16, lanes), BF16),
            pltpu.VMEM(((count + 2) * (rows + 2) * chans, lanes), BF16),
            pltpu.VMEM((n // 2 * disp, lanes), BF16),
        ],
    )
    backs = exchange(backs, "disp")
    (pay,) = call(
        flipped(functools.partial(sum_body, chans), disp),
        "sum",
        (((3 * chans + 8, lanes), F32, True),),
        *backs[::-1],
    )
    stages = radix_stages(space)
    for k, steps in enumerate(stages):
        parts = [pay] + [lax.ppermute(pay, "space", [(i, i ^ s) for i in range(space)]) for s in steps]
        if k < len(stages) - 1:
            pay = tree_sum(parts)

    volume_grad, disparity = call(
        flipped(functools.partial(join_body, dims), disp),
        "join",
        (((chans, planes, rows, width), BF16, False), ((rows, width), F32, False)),
        *backs[::-1],
    )

    scale = 16.0 / math.sqrt(planes * disp * rows * space * width)
    first_sum, bias_sum, second_sum = call(
        functools.partial(finish_body, chans, scale),
        "finish",
        (
            ((3, 3, 3, chans, chans), F32, False),
            ((1, chans), F32, False),
            ((3, 3, 3, chans), F32, False),
        ),
        *parts,
    )
    return (volume_grad, first_sum, bias_sum[0], second_sum, disparity)


def solution(mesh):
    return jax.shard_map(
        shards,
        mesh=mesh,
        in_specs=(
            P(None, "disp", ("groups", "space"), None),
            P(),
            P(),
            P(),
            P("disp", ("groups", "space"), None),
            P(("groups", "space"), None),
        ),
        out_specs=(
            P(None, "disp", ("groups", "space"), None),
            P(None, None, None, "groups", None),
            P("groups"),
            P(None, None, None, "groups"),
            P(("groups", "space"), None),
        ),
        check_vma=False,
    )
```

```python
import functools
import math

import jax
import jax.numpy as jnp
from jax import lax
from jax.experimental import pallas as pl
from jax.experimental.pallas import tpu as pltpu
from jax.sharding import PartitionSpec as P

F32 = jnp.float32
BF16 = jnp.bfloat16


def swap_pairs(count, step):
    pairs = []
    for i in range(count):
        j = i ^ 1 if step == 0 else ((i + 1) ^ 1) - 1
        pairs.append((i, j if 0 <= j < count else i))
    return pairs


def radix_stages(count):
    stages = []
    bit = 1
    while bit < count:
        if bit * 4 <= count:
            stages.append((bit, 2 * bit, 3 * bit))
            bit *= 4
        else:
            stages.append((bit,))
            bit *= 2
    return stages


def shift_up(x):
    return pltpu.roll(x, 1, 1)


def shift_down(x):
    return pltpu.roll(x, x.shape[1] - 1, 1)


def left(x, amount):
    return x if amount == 0 else pltpu.roll(x, x.shape[1] - amount, 1)


def right(x, amount):
    return x if amount == 0 else pltpu.roll(x, amount, 1)


def call(body, name, outs, *operands, scratch=(), inside=True):
    if inside:
        operands = [pltpu.with_memory_space_constraint(x, pltpu.VMEM) for x in operands]
    return pl.pallas_call(
        body,
        out_shape=tuple(
            pltpu.VMEM(shape, dtype) if inside else jax.ShapeDtypeStruct(shape, dtype)
            for shape, dtype, inside in outs
        ),
        in_specs=[pl.BlockSpec(memory_space=pltpu.VMEM)] * len(operands),
        out_specs=tuple(pl.BlockSpec(memory_space=pltpu.VMEM) for _ in outs),
        scratch_shapes=list(scratch),
        name=name,
    )(*operands)


def dot(a, b):
    return lax.dot_general(a, b, (((1,), (0,)), ((), ())), preferred_element_type=F32)


def dot_t(a, b):
    return lax.dot_general(a, b, (((1,), (1,)), ((), ())), preferred_element_type=F32)


def terms(value, count=3):
    out = []
    for _ in range(count):
        term = value.astype(BF16).astype(F32)
        out.append(term)
        value = value - term
    return out


def window(x, start, size):
    width = x.shape[1]
    moved = pltpu.roll(x, (width - start) % width, 1)[:, :size]
    column = start + lax.broadcasted_iota(jnp.int32, moved.shape, 1)
    return jnp.where((column >= 0) & (column < width), moved, 0.0)


def lanes_of(x):
    return lax.broadcasted_iota(jnp.int32, x.shape, 1)


def pack(x):
    n = x.shape[0]
    far = pltpu.roll(x[n // 2 :], 64, 1)
    out = [jnp.where(lanes_of(far) < 64, x[: n // 2], far)]
    for t in range(-(-n // 128)):
        rest = jnp.zeros((8, 128), F32)
        lane = lanes_of(rest)
        for k in range(16):
            at = (t * 16 + k) * 8
            if at < n:
                moved = pltpu.roll(x[at : at + 8], (8 * k + 64) % 128, 1)
                rest = jnp.where((lane >= 8 * k) & (lane < 8 * k + 8), moved, rest)
        out.append(rest)
    return out


def unpack(main, rest, k):
    n = main.shape[0]
    value = main[8 * k : 8 * k + 8] if 8 * k < n else pltpu.roll(main[8 * k - n : 8 * k - n + 8], 64, 1)
    moved = rest[8 * (k // 16) : 8 * (k // 16) + 8]
    moved = pltpu.roll(moved, (64 - 8 * (k % 16)) % 128, 1)
    return jnp.where(lanes_of(value) < 64, value, moved)


def split_body(dims, volume_ref, prior_ref, *refs):
    planes, rows, chans, width, disp, space, cols, lanes = dims
    out_refs = refs[:disp]
    wide_ref, found_ref = refs[disp : disp + 2]
    own_refs = refs[disp + 2 :]
    di = lax.axis_index("disp")
    group = 2 * planes
    n = planes * rows * chans
    for i in range(chans):
        value = volume_ref[i].astype(F32)
        for p in range(planes):
            for j, ref in enumerate(own_refs):
                ref[pl.ds(p * rows * chans + i, rows, stride=chans)] = value[p][:, j * 128 : (j + 1) * 128]
    for h in range(2):
        for p in range(planes):
            at = h * group + 2 * p
            wide_ref[at : at + 2] = prior_ref[p, 2 * h : 2 * h + 2]
    wide = wide_ref[...]
    pieces = [jnp.concatenate([ref[...] for ref in own_refs], axis=1)]
    for h in range(2):
        pieces += terms(wide[h * group : (h + 1) * group])
    whole = jnp.concatenate(pieces, axis=0)
    for t in range(disp):
        moved = window(whole, t * cols - 4, lanes)
        found_ref[t] = jnp.concatenate(pack(moved[:n]) + pack(moved[n:]), axis=0).astype(BF16)
    for s in range(disp):
        out_refs[s][...] = found_ref[di ^ s]


def rows_body(dims, *refs):
    planes, rows, chans, width, disp, space, cols, lanes = dims
    piece_refs = refs[:disp]
    cot_in_ref, one_ref, two_ref, prior_ref, cot_ref, wide_ref, rest_ref = refs[disp:]
    di = lax.axis_index("disp")
    even = lax.axis_index("space") % 2 == 0
    n = planes * rows * chans
    half = n // 2
    group = 2 * planes
    cot = window(jnp.concatenate([cot_in_ref[...]] * 2, axis=0), di * cols - 4, lanes)[:rows]
    cot_ref[...] = jnp.zeros(cot_ref.shape, F32)
    cot_ref[2 : 2 + rows] = cot
    fine = []
    for s in range(disp):
        g = di ^ s
        block = piece_refs[s][:half]
        at = pl.multiple_of(g * half, half)
        one_ref[pl.ds(at, half)] = block
        two_ref[pl.ds(at, half)] = block
        value = piece_refs[s][half:].astype(F32)
        rest_ref[pl.ds(pl.multiple_of(g * 8, 8), 8)] = value[:8]
        value = value[8:]
        value = [unpack(value[: 3 * group], value[3 * group :], k) for k in range(6)]
        fine.append(value)
        for h in range(2):
            prior = value[3 * h] + value[3 * h + 1] + value[3 * h + 2]
            for p in range(planes):
                prior_ref[g * planes + p, 2 + 2 * h : 4 + 2 * h] = prior[2 * p : 2 * p + 2]
    for out_ref, down in ((one_ref, even), (two_ref, jnp.logical_not(even))):

        def put(h):
            for s in range(disp):
                at = pl.multiple_of((di ^ s) * 3 * group, 8)
                wide_ref[pl.ds(at, 3 * group)] = jnp.concatenate(fine[s][3 * h : 3 * h + 3], axis=0)
            for t, term in enumerate(terms(cot_ref[2 + 2 * h : 4 + 2 * h])):
                at = disp * 3 * group + 2 * t
                wide_ref[at : at + 2] = term
            rest = disp * 3 * group + 6
            wide_ref[rest:] = jnp.zeros((wide_ref.shape[0] - rest, lanes), F32)

        pl.when(down)(functools.partial(put, 1))
        pl.when(jnp.logical_not(down))(functools.partial(put, 0))
        out_ref[disp * half :] = jnp.concatenate([rest_ref[...]] + pack(wide_ref[...]), axis=0).astype(BF16)


def bands_body(dims, base1_ref, base2_ref, base3_ref, base4_ref, bias_ref, band1_ref, band2_ref, band3_ref, band4_ref, col_ref):
    planes, rows, chans, width, disp, space, cols, lanes = dims

    def band(base, groups, count, step, used):
        pieces = []
        for c in range(3):
            piece = base[c * groups : (c + 1) * groups]
            for r in range(count):
                pieces.append(right(piece, step * r))
        return jnp.concatenate(pieces, axis=0)[:, :used].astype(BF16)

    band1_ref[...] = band(base1_ref[...], chans, rows + 2, chans, band1_ref.shape[1])
    band2_ref[...] = band(base2_ref[...], 1, rows + 4, chans, band2_ref.shape[1])
    band3_ref[...] = band(base3_ref[...], chans, rows + 2, 1, band3_ref.shape[1])
    band4 = band(base4_ref[...], chans, rows, chans, band4_ref.shape[1])
    n = rows * chans
    to = lax.broadcasted_iota(jnp.int32, (3 * n, 3 * n), 0)
    at = lax.broadcasted_iota(jnp.int32, (3 * n, 3 * n), 1)
    source = (to // n) * n + (to % rows) * chans + (to % n) // rows
    band4_ref[...] = dot((at == source).astype(BF16), band4).astype(BF16)
    diag = lax.broadcasted_iota(jnp.int32, (chans, chans), 0) == lax.broadcasted_iota(
        jnp.int32, (chans, chans), 1
    )
    bias = jnp.sum(jnp.where(diag, bias_ref[...], 0.0), axis=1, keepdims=True)
    col_ref[...] = jnp.concatenate([jnp.broadcast_to(bias, (chans, 2 * lanes))] * (rows + 6), axis=0)


def main_body(dims, *refs):
    planes, rows, chans, width, disp, space, cols, lanes = dims
    own_ref, za_ref, zb_ref, prior_in_ref, cot_in_ref, band1_ref, band2_ref, band3_ref, band4_ref, col_ref = refs[:10]
    back_refs = refs[10 : 10 + disp]
    x_ref, h_ref, slope_ref, prior_ref, cot_ref, s_ref, pg_ref, v_ref = refs[10 + disp :]
    zi = lax.axis_index("space")
    di = lax.axis_index("disp")
    z_even = zi % 2 == 0
    count = planes * disp
    n = count * rows * chans
    block = rows * chans
    xr = (rows + 8) * chans
    hr = (rows + 6) * chans
    gr = (rows + 2) * chans
    lr = rows + 4
    sr = 16
    two = 2 * lanes

    def place_rows(src, row):
        main = src[: n // 2].astype(F32)
        rest = src[n // 2 : n // 2 + 8 * disp].astype(F32)
        side = planes * block // 2
        for k in range(count):
            g = k // planes
            p = k % planes
            value = [
                unpack(main[g * side : (g + 1) * side], rest[8 * g : 8 * g + 8], p * rows + r) for r in range(rows)
            ]
            at = (k + 1) * xr + row * chans
            x_ref[at : at + block] = jnp.concatenate(value, axis=0).astype(BF16)

    x_ref[:xr] = jnp.zeros((xr, lanes), BF16)
    x_ref[(count + 1) * xr :] = jnp.zeros((2 * xr, lanes), BF16)
    h_ref[:hr] = jnp.zeros((hr, lanes), BF16)
    h_ref[(count + 1) * hr :] = jnp.zeros((2 * hr, lanes), BF16)
    s_ref[...] = jnp.zeros(s_ref.shape, BF16)
    pg_ref[:gr] = jnp.zeros((gr, lanes), BF16)
    pg_ref[(count + 1) * gr :] = jnp.zeros((gr, lanes), BF16)
    place_rows(own_ref, 4)
    prior_ref[...] = prior_in_ref[...]
    cot_ref[...] = cot_in_ref[...]
    half = 2 * planes

    def place(ok, first, one, other, row, at8):
        def put(src):
            if src is None:
                for k in range(count):
                    at = (k + 1) * xr + row * chans
                    x_ref[at : at + 4 * chans] = jnp.zeros((4 * chans, lanes), BF16)
                    prior_ref[k, at8 : at8 + 2] = jnp.zeros((2, lanes), F32)
                cot_ref[at8 : at8 + 2] = jnp.zeros((2, lanes), F32)
                return
            place_rows(src, row)
            extra = src[n // 2 + 8 * disp :].astype(F32)
            used = -(-(3 * half * disp + 6) // 16) * 16
            value = [unpack(extra[: used // 2], extra[used // 2 :], k) for k in range(3 * disp + 1)]
            for g in range(disp):
                prior = value[3 * g] + value[3 * g + 1] + value[3 * g + 2]
                for p in range(planes):
                    prior_ref[g * planes + p, at8 : at8 + 2] = prior[2 * p : 2 * p + 2]
            cot = value[3 * disp]
            cot_ref[at8 : at8 + 2] = cot[:2] + cot[2:4] + cot[4:6]

        pl.when(ok & first)(lambda: put(one))
        pl.when(ok & jnp.logical_not(first))(lambda: put(other))
        pl.when(jnp.logical_not(ok))(lambda: put(None))

    place(zi > 0, z_even, zb_ref, za_ref, 0, 0)
    place(zi < space - 1, z_even, za_ref, zb_ref, 4 + rows, 2 + rows)

    def pair(ref, p, size, taken):
        return jnp.concatenate([ref[p * size : p * size + taken], ref[(p + 1) * size : (p + 1) * size + taken]], axis=1)

    lane = lax.broadcasted_iota(jnp.int32, (hr, two), 1) % lanes
    column = di * cols - 4 + lane
    row_at = zi * rows - 3 + lax.broadcasted_iota(jnp.int32, (hr, two), 0) // chans
    inside = ((row_at >= 0) & (row_at < space * rows) & (column >= 0) & (column < width)).astype(F32)
    band1 = band1_ref[...]
    bias = col_ref[...]
    yr = (rows + 2) * chans
    wr = (rows + 4) * chans
    for p in range(0, count, 2):
        pre = []
        for at in (0, 4 * chans):
            rhs = [
                jnp.concatenate(
                    [x_ref[(p + q + a) * xr + at : (p + q + a) * xr + at + wr] for a in range(3)], axis=0
                )
                for q in range(2)
            ]
            y = dot(band1, jnp.concatenate(rhs, axis=1))
            skip = at // 2
            y = [y[c * yr + skip : (c + 1) * yr] for c in range(3)]
            pre.append(y[1] + shift_up(y[0]) + shift_down(y[2]))
        pre = jnp.concatenate(pre, axis=0) + bias
        sig = 0.5 * jnp.tanh(0.5 * pre) + 0.5
        hidden = (pre * sig * inside).astype(BF16)
        slope = (sig * (1.0 + pre * (1.0 - sig)) * inside)[2 * chans : hr - 2 * chans]
        for q in range(2):
            part = slice(q * lanes, (q + 1) * lanes)
            h_ref[(p + q + 1) * hr : (p + q + 2) * hr] = hidden[:, part]
            slope_ref[p + q] = slope[:, part]

    band2 = band2_ref[...]
    logits = []
    for p in range(0, count, 2):
        y = dot(band2, pair(h_ref, p, hr, 3 * hr))
        y = y[lr : 2 * lr] + shift_up(y[:lr]) + shift_down(y[2 * lr :])
        logits += [y[:, :lanes] + prior_ref[p], y[:, lanes:] + prior_ref[p + 1]]

    top = logits[0]
    for value in logits[1:]:
        top = jnp.maximum(top, value)
    summed = jnp.zeros((lr, lanes), F32)
    moment = jnp.zeros((lr, lanes), F32)
    weights = []
    for k, value in enumerate(logits):
        e = jnp.exp(value - top)
        weights.append(e)
        summed = summed + e
        moment = moment + e * ((k + 0.5) / count)
    disparity = moment / summed
    coef = cot_ref[...] / summed
    mine = lax.broadcasted_iota(jnp.int32, (lr, lanes), 1)
    mine = (mine >= 4) & (mine < 4 + cols)
    left2 = []
    for k in range(count):
        score = (coef * weights[k] * ((k + 0.5) / count - disparity)).astype(BF16)
        s_ref[(k + 1) * sr : (k + 1) * sr + lr] = score
        score = jnp.where(mine, score.astype(F32), 0.0)
        left2.append(jnp.concatenate([shift_down(score), score, shift_up(score)], axis=0).astype(BF16))

    band3 = band3_ref[...]
    mine = lax.broadcasted_iota(jnp.int32, (block, two), 1) % lanes
    mine = (mine >= 4) & (mine < 4 + cols)
    bias_sum = jnp.zeros((chans, two), F32)
    left1 = []
    for p in range(0, count, 2):
        y = dot(band3, pair(s_ref, p, sr, 3 * sr))
        hg = y[gr : 2 * gr] + shift_down(y[:gr]) + shift_up(y[2 * gr :])
        slope = jnp.concatenate([slope_ref[p], slope_ref[p + 1]], axis=1)
        pg = (hg * slope).astype(BF16)
        for q in range(2):
            pg_ref[(p + q + 1) * gr : (p + q + 2) * gr] = pg[:, q * lanes : (q + 1) * lanes]
        own = jnp.where(mine, pg.astype(F32)[chans : chans + block], 0.0)
        moved = (shift_down(own), own, shift_up(own))
        pieces = []
        for r in range(rows):
            part = slice(r * chans, (r + 1) * chans)
            bias_sum = bias_sum + own[part]
            pieces += [moved[c][part] for c in range(3)]
        left1.append(jnp.concatenate(pieces, axis=0).astype(BF16))

    inner = (rows + 4) * chans
    acc = None
    for p in range(0, count, 2):
        far = []
        for q in range(2):
            k = p + q
            far.append(
                jnp.concatenate(
                    [x_ref[(k + a) * xr + 2 * chans : (k + a) * xr + 2 * chans + inner] for a in range(3)]
                    + [h_ref[k * hr : (k + 3) * hr]],
                    axis=0,
                )
            )
        side = jnp.concatenate([left2[p], left2[p + 1]], axis=1)
        side = jnp.concatenate([left1[p // 2], side, jnp.zeros((128 - 15 * chans, two), BF16)], axis=0)
        part = dot_t(jnp.concatenate(far, axis=1), side)
        acc = part if acc is None else acc + part

    def turned(at, amount):
        return pltpu.roll(acc[at : at + chans], amount % 128, 1)

    tap = 3 * chans
    blocks = [jnp.zeros((chans, 128), F32), jnp.zeros((chans, 128), F32)]
    lane_p = lax.broadcasted_iota(jnp.int32, (chans, 128), 1)
    for k in range(9):
        a, b = k // 3, k % 3
        to = tap * (k % 5)
        value = sum(turned(a * inner + (r + b + 1) * chans, to - tap * r) for r in range(rows))
        blocks[k // 5] = jnp.where((lane_p >= to) & (lane_p < to + tap), value, blocks[k // 5])
        base = 3 * inner + a * hr
        used = rows * tap
        if k < 8:
            value = sum(turned(base + (r + b) * chans, 96 + k - used - r) for r in range(2, 2 + rows))
            blocks[1] = jnp.where((lane_p >= 96) & (lane_p < 120) & (lane_p % 8 == k), value, blocks[1])
        else:
            for c in range(3):
                value = sum(turned(base + (r + b) * chans, 120 + c - used - lr * c - r) for r in range(2, 2 + rows))
                blocks[0] = jnp.where(lane_p == 120 + c, value, blocks[0])
    bias_sum = jnp.sum(bias_sum, axis=1, keepdims=True)
    blocks[1] = jnp.where(lane_p == 120, bias_sum, blocks[1])
    payload = jnp.concatenate(blocks, axis=0)
    shown = jnp.concatenate([disparity[2 : 2 + rows]] * 2, axis=0)
    tail = jnp.concatenate(terms(payload, 2) + terms(shown, 2), axis=0).astype(BF16)

    band4 = band4_ref[...]
    found = [None] * planes
    for p in range(0, count, 2):
        y = dot(band4, pair(pg_ref, p, gr, 3 * gr))
        y = y[block : 2 * block] + shift_down(y[:block]) + shift_up(y[2 * block :])
        for q in range(2):
            moved = y[:, q * lanes : (q + 1) * lanes]
            k = p + q
            found[k % planes] = moved
        if (p + 2) % planes == 0:
            near = jnp.concatenate(found[: planes // 2], axis=0)
            far = jnp.concatenate(found[planes // 2 :], axis=0)
            near = pltpu.roll(near, lanes - 4, 1)
            far = pltpu.roll(far, 60, 1)
            at = (p // planes) * (planes * block // 2)
            v_ref[at : at + planes * block // 2] = jnp.where(lanes_of(near) < 64, near, far).astype(BF16)
    size = planes * block // 2
    for s in range(disp):
        back_refs[s][:size] = v_ref[pl.ds(pl.multiple_of((di ^ s) * size, size), size)]
        back_refs[s][size:] = tail


def sum_body(chans, *refs):
    parts = refs[:-1]
    k = 2 * chans
    sums = []
    for r in parts:
        n = r.shape[0] - 2 * k - 16
        value = r[n:].astype(F32)
        sums.append(value[:k] + value[k : 2 * k])
    refs[-1][...] = tree_sum(sums)


def join_body(dims, *refs):
    planes, rows, chans, width, disp, space, cols, lanes = dims
    parts = refs[:disp]
    grad_ref, disp_ref = refs[disp:]
    di = lax.axis_index("disp")
    n = planes * rows * chans
    k = 4 * chans
    total = None
    for s in range(disp):
        j = di ^ s
        shown = parts[s][n // 2 + k :].astype(F32)
        shown = pltpu.roll(shown[:8] + shown[8:], lanes - 4, 1)
        main = parts[s][: n // 2].astype(F32)
        value = jnp.concatenate([main, pltpu.roll(main, 64, 1), shown], axis=0)
        value = jnp.where(lanes_of(value) < cols, value, 0.0)
        value = jnp.concatenate([value, jnp.zeros((value.shape[0], width - lanes), F32)], axis=1)
        value = pltpu.roll(value, j * cols, 1)
        total = value if total is None else total + value
    disp_ref[...] = total[n : n + rows]
    grad = total[:n].astype(BF16)
    for p in range(planes):
        for i in range(chans):
            at = (p * chans + i) * rows
            grad_ref[i, p] = grad[at : at + rows]


def tree_sum(parts):
    while len(parts) > 1:
        parts = [parts[k] + parts[k + 1] for k in range(0, len(parts), 2)]
    return parts[0]


def finish_body(chans, scale, *refs):
    gw_ref, gb_ref, gs_ref = refs[-3:]
    total = tree_sum([r[...] for r in refs[:-3]]) * scale
    flat = [jnp.transpose(total[:chans]), jnp.transpose(total[chans:])]
    for k in range(9):
        a, b = k // 3, k % 3
        for c in range(3):
            at = 3 * chans * (k % 5) + chans * c
            gw_ref[a, b, c] = flat[k // 5][at : at + chans]
            at = 96 + k + 8 * c if k < 8 else 120 + c
            gs_ref[a, b, c : c + 1] = flat[1 if k < 8 else 0][at : at + 1]
    gb_ref[...] = flat[1][120:121]


def flipped(body, count):
    def run(*refs):
        return body(*refs[:count][::-1], *refs[count:])

    return run


def exchange(sends, axis):
    count = lax.axis_size(axis)
    return [sends[0]] + [
        lax.ppermute(sends[s], axis, [(i, i ^ s) for i in range(count)]) for s in range(1, count)
    ]


def shards(volume, w_first, b_first, w_second, prior_logits, cotangent):
    chans, planes, rows, width = volume.shape
    disp = lax.axis_size("disp")
    space = lax.axis_size("space")
    cols = width // disp
    lanes = -(-(cols + 8) // 128) * 128
    dims = (planes, rows, chans, width, disp, space, cols, lanes)
    count = planes * disp
    n = planes * rows * chans

    piece = n // 2 + 8 + 6 * planes + 8
    sends = call(
        functools.partial(split_body, dims),
        "split",
        [((piece, lanes), BF16, True)] * disp,
        volume, prior_logits,
        inside=False,
        scratch=[
            pltpu.VMEM((4 * planes, width), F32),
            pltpu.VMEM((disp, piece, lanes), BF16),
        ]
        + [pltpu.VMEM((n, 128), F32)] * (width // 128),
    )
    pieces = exchange(sends, "disp")

    xr = rows + 8
    hr = rows + 6
    base1 = jnp.transpose(w_first, (2, 3, 0, 1, 4)).astype(F32)
    base1 = jnp.pad(base1, ((0, 0), (0, 0), (0, 0), (0, rows + 1), (0, 0)))
    base1 = base1.reshape(3 * chans, 3 * (rows + 4) * chans)
    base1 = jnp.pad(base1, ((0, 0), (0, -base1.shape[1] % 128)))
    base2 = jnp.transpose(w_second, (2, 0, 1, 3)).astype(F32)
    base2 = jnp.pad(base2, ((0, 0), (0, 0), (0, hr - 3), (0, 0))).reshape(3, 3 * hr * chans)
    base2 = jnp.pad(base2, ((0, 5), (0, -base2.shape[1] % 128)))
    base3 = jnp.transpose(w_second[::-1, ::-1], (2, 3, 0, 1)).astype(F32)
    base3 = jnp.pad(base3, ((0, 0), (0, 0), (0, 0), (0, 16 - 3))).reshape(3 * chans, 3 * 16)
    base3 = jnp.pad(base3, ((0, 0), (0, 128 - base3.shape[1])))
    base4 = jnp.transpose(w_first[::-1, ::-1], (2, 4, 0, 1, 3)).astype(F32)
    base4 = jnp.pad(base4, ((0, 0), (0, 0), (0, 0), (0, rows - 1), (0, 0))).reshape(
        3 * chans, 3 * (rows + 2) * chans
    )
    base4 = jnp.pad(base4, ((0, 0), (0, -base4.shape[1] % 128)))
    bands = call(
        functools.partial(bands_body, dims),
        "bands",
        (
            ((3 * (rows + 2) * chans, 3 * (rows + 4) * chans), BF16, True),
            ((3 * (rows + 4), 3 * hr * chans), BF16, True),
            ((3 * (rows + 2) * chans, 3 * 16), BF16, True),
            ((3 * rows * chans, 3 * (rows + 2) * chans), BF16, True),
            ((hr * chans, 2 * lanes), F32, True),
        ),
        base1, base2, base3, base4, b_first[None, :],
    )

    extra = -(-(6 * count + 6) // 16) * 16
    sent = (n // 2 + 8) * disp + extra // 2 + 8 * -(-extra // 128)
    send_one, send_two, prior, cot = call(
        flipped(functools.partial(rows_body, dims), disp),
        "rows",
        (
            ((sent, lanes), BF16, True),
            ((sent, lanes), BF16, True),
            ((count, rows + 4, lanes), F32, True),
            ((rows + 4, lanes), F32, True),
        ),
        *pieces[::-1], cotangent,
        scratch=[pltpu.VMEM((extra, lanes), F32), pltpu.VMEM((8 * disp, lanes), F32)],
    )
    z_one = lax.ppermute(send_one, "space", swap_pairs(space, 0))
    z_two = lax.ppermute(send_two, "space", swap_pairs(space, 1))

    tail = 4 * chans + 16
    backs = call(
        functools.partial(main_body, dims),
        "main",
        [((n // 2 + tail, lanes), BF16, True)] * disp,
        send_one, z_one, z_two, prior, cot, *bands,
        scratch=[
            pltpu.VMEM(((count + 3) * xr * chans, lanes), BF16),
            pltpu.VMEM(((count + 3) * hr * chans, lanes), BF16),
            pltpu.VMEM((count, (rows + 2) * chans, lanes), F32),
            pltpu.VMEM((count, rows + 4, lanes), F32),
            pltpu.VMEM((rows + 4, lanes), F32),
            pltpu.VMEM(((count + 2) * 16, lanes), BF16),
            pltpu.VMEM(((count + 2) * (rows + 2) * chans, lanes), BF16),
            pltpu.VMEM((n // 2 * disp, lanes), BF16),
        ],
    )
    backs = exchange(backs, "disp")
    (pay,) = call(
        flipped(functools.partial(sum_body, chans), disp),
        "sum",
        (((2 * chans, lanes), F32, True),),
        *backs[::-1],
    )
    stages = radix_stages(space)
    for k, steps in enumerate(stages):
        parts = [pay] + [lax.ppermute(pay, "space", [(i, i ^ s) for i in range(space)]) for s in steps]
        if k < len(stages) - 1:
            pay = tree_sum(parts)

    volume_grad, disparity = call(
        flipped(functools.partial(join_body, dims), disp),
        "join",
        (((chans, planes, rows, width), BF16, False), ((rows, width), F32, False)),
        *backs[::-1],
    )

    scale = 16.0 / math.sqrt(planes * disp * rows * space * width)
    first_sum, bias_sum, second_sum = call(
        functools.partial(finish_body, chans, scale),
        "finish",
        (
            ((3, 3, 3, chans, chans), F32, False),
            ((1, chans), F32, False),
            ((3, 3, 3, chans), F32, False),
        ),
        *parts,
    )
    return (volume_grad, first_sum, bias_sum[0], second_sum, disparity)


def solution(mesh):
    return jax.shard_map(
        shards,
        mesh=mesh,
        in_specs=(
            P(None, "disp", ("groups", "space"), None),
            P(),
            P(),
            P(),
            P("disp", ("groups", "space"), None),
            P(("groups", "space"), None),
        ),
        out_specs=(
            P(None, "disp", ("groups", "space"), None),
            P(None, None, None, "groups", None),
            P("groups"),
            P(None, None, None, "groups"),
            P(("groups", "space"), None),
        ),
        check_vma=False,
    )
```

```python
import functools
import math

import jax
import jax.numpy as jnp
from jax import lax
from jax.experimental import pallas as pl
from jax.experimental.pallas import tpu as pltpu
from jax.sharding import PartitionSpec as P

F32 = jnp.float32
BF16 = jnp.bfloat16


def swap_pairs(count, step):
    pairs = []
    for i in range(count):
        j = i ^ 1 if step == 0 else ((i + 1) ^ 1) - 1
        pairs.append((i, j if 0 <= j < count else i))
    return pairs


def radix_stages(count):
    stages = []
    bit = 1
    while bit < count:
        if bit * 4 <= count:
            stages.append((bit, 2 * bit, 3 * bit))
            bit *= 4
        else:
            stages.append((bit,))
            bit *= 2
    return stages


def shift_up(x):
    return pltpu.roll(x, 1, 1)


def shift_down(x):
    return pltpu.roll(x, x.shape[1] - 1, 1)


def left(x, amount):
    return x if amount == 0 else pltpu.roll(x, x.shape[1] - amount, 1)


def right(x, amount):
    return x if amount == 0 else pltpu.roll(x, amount, 1)


def call(body, name, outs, *operands, scratch=(), inside=True):
    if inside:
        operands = [pltpu.with_memory_space_constraint(x, pltpu.VMEM) for x in operands]
    return pl.pallas_call(
        body,
        out_shape=tuple(
            pltpu.VMEM(shape, dtype) if inside else jax.ShapeDtypeStruct(shape, dtype)
            for shape, dtype, inside in outs
        ),
        in_specs=[pl.BlockSpec(memory_space=pltpu.VMEM)] * len(operands),
        out_specs=tuple(pl.BlockSpec(memory_space=pltpu.VMEM) for _ in outs),
        scratch_shapes=list(scratch),
        name=name,
    )(*operands)


def dot(a, b):
    return lax.dot_general(a, b, (((1,), (0,)), ((), ())), preferred_element_type=F32)


def dot_t(a, b):
    return lax.dot_general(a, b, (((1,), (1,)), ((), ())), preferred_element_type=F32)


def terms(value, count=3):
    out = []
    for _ in range(count):
        term = value.astype(BF16).astype(F32)
        out.append(term)
        value = value - term
    return out


def window(x, start, size):
    width = x.shape[1]
    moved = pltpu.roll(x, (width - start) % width, 1)[:, :size]
    column = start + lax.broadcasted_iota(jnp.int32, moved.shape, 1)
    return jnp.where((column >= 0) & (column < width), moved, 0.0)


def lanes_of(x):
    return lax.broadcasted_iota(jnp.int32, x.shape, 1)


def pack(x):
    n = x.shape[0]
    far = pltpu.roll(x[n // 2 :], 64, 1)
    out = [jnp.where(lanes_of(far) < 64, x[: n // 2], far)]
    for t in range(-(-n // 128)):
        rest = jnp.zeros((8, 128), F32)
        lane = lanes_of(rest)
        for k in range(16):
            at = (t * 16 + k) * 8
            if at < n:
                moved = pltpu.roll(x[at : at + 8], (8 * k + 64) % 128, 1)
                rest = jnp.where((lane >= 8 * k) & (lane < 8 * k + 8), moved, rest)
        out.append(rest)
    return out


def unpack(main, rest, k):
    n = main.shape[0]
    value = main[8 * k : 8 * k + 8] if 8 * k < n else pltpu.roll(main[8 * k - n : 8 * k - n + 8], 64, 1)
    moved = rest[8 * (k // 16) : 8 * (k // 16) + 8]
    moved = pltpu.roll(moved, (64 - 8 * (k % 16)) % 128, 1)
    return jnp.where(lanes_of(value) < 64, value, moved)


def split_body(dims, volume_ref, prior_ref, *refs):
    planes, rows, chans, width, disp, space, cols, lanes = dims
    out_refs = refs[:disp]
    wide_ref, found_ref = refs[disp : disp + 2]
    own_refs = refs[disp + 2 :]
    di = lax.axis_index("disp")
    group = 2 * planes
    n = planes * rows * chans
    for i in range(chans):
        value = volume_ref[i].astype(F32)
        for p in range(planes):
            for j, ref in enumerate(own_refs):
                ref[pl.ds(p * rows * chans + i, rows, stride=chans)] = value[p][:, j * 128 : (j + 1) * 128]
    for h in range(2):
        for p in range(planes):
            at = h * group + 2 * p
            wide_ref[at : at + 2] = prior_ref[p, 2 * h : 2 * h + 2]
    wide = wide_ref[...]
    pieces = [jnp.concatenate([ref[...] for ref in own_refs], axis=1)]
    for h in range(2):
        pieces += terms(wide[h * group : (h + 1) * group])
    whole = jnp.concatenate(pieces, axis=0)
    for t in range(disp):
        moved = window(whole, t * cols - 4, lanes)
        found_ref[t] = jnp.concatenate(pack(moved[:n]) + pack(moved[n:]), axis=0).astype(BF16)
    for s in range(disp):
        out_refs[s][...] = found_ref[di ^ s]


def rows_body(dims, *refs):
    planes, rows, chans, width, disp, space, cols, lanes = dims
    piece_refs = refs[:disp]
    cot_in_ref, one_ref, two_ref, wide_ref, rest_ref = refs[disp:]
    di = lax.axis_index("disp")
    even = lax.axis_index("space") % 2 == 0
    n = planes * rows * chans
    half = n // 2
    group = 2 * planes
    cot = window(jnp.concatenate([cot_in_ref[...]] * 2, axis=0), di * cols - 4, lanes)[:rows]
    fine = []
    for s in range(disp):
        g = di ^ s
        block = piece_refs[s][:half]
        at = pl.multiple_of(g * half, half)
        one_ref[pl.ds(at, half)] = block
        two_ref[pl.ds(at, half)] = block
        value = piece_refs[s][half:].astype(F32)
        rest_ref[pl.ds(pl.multiple_of(g * 8, 8), 8)] = value[:8]
        value = value[8:]
        value = [unpack(value[: 3 * group], value[3 * group :], k) for k in range(6)]
        fine.append(value)
    for out_ref, down in ((one_ref, even), (two_ref, jnp.logical_not(even))):

        def put(h):
            for s in range(disp):
                at = pl.multiple_of((di ^ s) * 3 * group, 8)
                wide_ref[pl.ds(at, 3 * group)] = jnp.concatenate(fine[s][3 * h : 3 * h + 3], axis=0)
            for t, term in enumerate(terms(cot[2 * h : 2 * h + 2])):
                at = disp * 3 * group + 2 * t
                wide_ref[at : at + 2] = term
            rest = disp * 3 * group + 6
            wide_ref[rest:] = jnp.zeros((wide_ref.shape[0] - rest, lanes), F32)

        pl.when(down)(functools.partial(put, 1))
        pl.when(jnp.logical_not(down))(functools.partial(put, 0))
        out_ref[disp * half :] = jnp.concatenate([rest_ref[...]] + pack(wide_ref[...]), axis=0).astype(BF16)


def mine_body(dims, *refs):
    planes, rows, chans, width, disp, space, cols, lanes = dims
    piece_refs = refs[:disp]
    cot_in_ref, x_ref, prior_ref, cot_ref = refs[disp:]
    di = lax.axis_index("disp")
    block = rows * chans
    half = planes * block // 2
    group = 2 * planes
    prior_ref[...] = jnp.zeros(prior_ref.shape, F32)
    cot_ref[...] = jnp.zeros(cot_ref.shape, F32)
    cot = jnp.concatenate([cot_in_ref[...]] * 2, axis=0)
    cot_ref[2 : 2 + rows] = window(cot, di * cols - 4, lanes)[:rows]
    x_ref[:block] = jnp.zeros((block, lanes), BF16)
    x_ref[x_ref.shape[0] - block :] = jnp.zeros((block, lanes), BF16)
    for s in range(disp):
        g = di ^ s
        main = piece_refs[s][:half].astype(F32)
        rest = piece_refs[s][half:].astype(F32)
        for p in range(planes):
            value = [unpack(main, rest[:8], p * rows + r) for r in range(rows)]
            at = pl.multiple_of((g * planes + p + 1) * block, block)
            x_ref[pl.ds(at, block)] = jnp.concatenate(value, axis=0).astype(BF16)
        value = [unpack(rest[8 : 8 + 3 * group], rest[8 + 3 * group :], k) for k in range(6)]
        for h in range(2):
            prior = value[3 * h] + value[3 * h + 1] + value[3 * h + 2]
            for p in range(planes):
                prior_ref[g * planes + p, 2 + 2 * h : 4 + 2 * h] = prior[2 * p : 2 * p + 2]


def bands_body(dims, base1_ref, base2_ref, base3_ref, base4_ref, bias_ref, band1_ref, band2_ref, band3_ref, band4_ref, col_ref):
    planes, rows, chans, width, disp, space, cols, lanes = dims

    def band(base, groups, count, step, used):
        pieces = []
        for c in range(3):
            piece = base[c * groups : (c + 1) * groups]
            for r in range(count):
                pieces.append(right(piece, step * r))
        return jnp.concatenate(pieces, axis=0)[:, :used].astype(BF16)

    band1_ref[...] = band(base1_ref[...], chans, rows + 2, chans, band1_ref.shape[1])
    band2_ref[...] = band(base2_ref[...], 1, rows + 4, chans, band2_ref.shape[1])
    band3_ref[...] = band(base3_ref[...], chans, rows + 2, 1, band3_ref.shape[1])
    band4 = band(base4_ref[...], chans, rows, chans, band4_ref.shape[1])
    n = rows * chans
    to = lax.broadcasted_iota(jnp.int32, (3 * n, 3 * n), 0)
    at = lax.broadcasted_iota(jnp.int32, (3 * n, 3 * n), 1)
    source = (to // n) * n + (to % rows) * chans + (to % n) // rows
    band4_ref[...] = dot((at == source).astype(BF16), band4).astype(BF16)
    diag = lax.broadcasted_iota(jnp.int32, (chans, chans), 0) == lax.broadcasted_iota(
        jnp.int32, (chans, chans), 1
    )
    bias = jnp.sum(jnp.where(diag, bias_ref[...], 0.0), axis=1, keepdims=True)
    col_ref[...] = jnp.concatenate([jnp.broadcast_to(bias, (chans, 2 * lanes))] * (rows + 6), axis=0)


def main_body(dims, *refs):
    planes, rows, chans, width, disp, space, cols, lanes = dims
    xo_ref, za_ref, zb_ref, prior_in_ref, cot_in_ref, band1_ref, band2_ref, band3_ref, band4_ref, col_ref = refs[:10]
    back_refs = refs[10 : 10 + disp]
    xu_ref, xd_ref, h_ref, slope_ref, prior_ref, cot_ref, s_ref, pg_ref, v_ref = refs[10 + disp :]
    zi = lax.axis_index("space")
    di = lax.axis_index("disp")
    z_even = zi % 2 == 0
    count = planes * disp
    n = count * rows * chans
    block = rows * chans
    hr = (rows + 6) * chans
    gr = (rows + 2) * chans
    lr = rows + 4
    sr = 16
    two = 2 * lanes

    def place_rows(src, ref):
        main = src[: n // 2].astype(F32)
        rest = src[n // 2 : n // 2 + 8 * disp].astype(F32)
        side = planes * block // 2
        for k in range(count):
            g = k // planes
            p = k % planes
            value = [
                unpack(main[g * side : (g + 1) * side], rest[8 * g : 8 * g + 8], p * rows + r) for r in range(rows)
            ]
            ref[(k + 1) * block : (k + 2) * block] = jnp.concatenate(value, axis=0).astype(BF16)

    for ref in (xu_ref, xd_ref):
        ref[:block] = jnp.zeros((block, lanes), BF16)
        ref[(count + 1) * block :] = jnp.zeros((block, lanes), BF16)
    h_ref[:hr] = jnp.zeros((hr, lanes), BF16)
    h_ref[(count + 1) * hr :] = jnp.zeros((hr, lanes), BF16)
    s_ref[...] = jnp.zeros(s_ref.shape, BF16)
    pg_ref[:gr] = jnp.zeros((gr, lanes), BF16)
    pg_ref[(count + 1) * gr :] = jnp.zeros((gr, lanes), BF16)
    prior_ref[...] = prior_in_ref[...]
    cot_ref[...] = cot_in_ref[...]
    half = 2 * planes

    def place(ok, first, one, other, ref, at8):
        def put(src):
            if src is None:
                ref[...] = jnp.zeros(ref.shape, BF16)
                for k in range(count):
                    prior_ref[k, at8 : at8 + 2] = jnp.zeros((2, lanes), F32)
                cot_ref[at8 : at8 + 2] = jnp.zeros((2, lanes), F32)
                return
            place_rows(src, ref)
            extra = src[n // 2 + 8 * disp :].astype(F32)
            used = -(-(3 * half * disp + 6) // 16) * 16
            value = [unpack(extra[: used // 2], extra[used // 2 :], k) for k in range(3 * disp + 1)]
            for g in range(disp):
                prior = value[3 * g] + value[3 * g + 1] + value[3 * g + 2]
                for p in range(planes):
                    prior_ref[g * planes + p, at8 : at8 + 2] = prior[2 * p : 2 * p + 2]
            cot = value[3 * disp]
            cot_ref[at8 : at8 + 2] = cot[:2] + cot[2:4] + cot[4:6]

        pl.when(ok & first)(lambda: put(one))
        pl.when(ok & jnp.logical_not(first))(lambda: put(other))
        pl.when(jnp.logical_not(ok))(lambda: put(None))

    place(zi > 0, z_even, zb_ref, za_ref, xu_ref, 0)
    place(zi < space - 1, z_even, za_ref, zb_ref, xd_ref, 2 + rows)

    def pair(ref, p, size, taken):
        return jnp.concatenate([ref[p * size : p * size + taken], ref[(p + 1) * size : (p + 1) * size + taken]], axis=1)

    lane = lax.broadcasted_iota(jnp.int32, (hr, two), 1) % lanes
    column = di * cols - 4 + lane
    row_at = zi * rows - 3 + lax.broadcasted_iota(jnp.int32, (hr, two), 0) // chans
    inside = ((row_at >= 0) & (row_at < space * rows) & (column >= 0) & (column < width)).astype(F32)
    band1 = band1_ref[...]
    bias = col_ref[...]
    yr = (rows + 2) * chans
    for p in range(0, count, 2):
        pre = []
        for at, (near, far) in ((0, (xu_ref, xo_ref)), (4 * chans, (xo_ref, xd_ref))):
            rhs = []
            for q in range(2):
                parts = []
                for k in range(p + q, p + q + 3):
                    parts += [near[k * block : (k + 1) * block], far[k * block : (k + 1) * block]]
                rhs.append(jnp.concatenate(parts, axis=0))
            y = dot(band1, jnp.concatenate(rhs, axis=1))
            skip = at // 2
            y = [y[c * yr + skip : (c + 1) * yr] for c in range(3)]
            pre.append(y[1] + shift_up(y[0]) + shift_down(y[2]))
        pre = jnp.concatenate(pre, axis=0) + bias
        sig = 0.5 * jnp.tanh(0.5 * pre) + 0.5
        hidden = (pre * sig * inside).astype(BF16)
        slope = (sig * (1.0 + pre * (1.0 - sig)) * inside)[2 * chans : hr - 2 * chans]
        for q in range(2):
            part = slice(q * lanes, (q + 1) * lanes)
            h_ref[(p + q + 1) * hr : (p + q + 2) * hr] = hidden[:, part]
            slope_ref[p + q] = slope[:, part]

    band2 = band2_ref[...]
    logits = []
    for p in range(0, count, 2):
        y = dot(band2, pair(h_ref, p, hr, 3 * hr))
        y = y[lr : 2 * lr] + shift_up(y[:lr]) + shift_down(y[2 * lr :])
        logits += [y[:, :lanes] + prior_ref[p], y[:, lanes:] + prior_ref[p + 1]]

    top = logits[0]
    for value in logits[1:]:
        top = jnp.maximum(top, value)
    summed = jnp.zeros((lr, lanes), F32)
    moment = jnp.zeros((lr, lanes), F32)
    weights = []
    for k, value in enumerate(logits):
        e = jnp.exp(value - top)
        weights.append(e)
        summed = summed + e
        moment = moment + e * ((k + 0.5) / count)
    disparity = moment / summed
    coef = cot_ref[...] / summed
    mine = lax.broadcasted_iota(jnp.int32, (lr, lanes), 1)
    mine = (mine >= 4) & (mine < 4 + cols)
    left2 = []
    for k in range(count):
        score = (coef * weights[k] * ((k + 0.5) / count - disparity)).astype(BF16)
        s_ref[(k + 1) * sr : (k + 1) * sr + lr] = score
        score = jnp.where(mine, score.astype(F32), 0.0)
        left2.append(jnp.concatenate([shift_down(score), score, shift_up(score)], axis=0).astype(BF16))

    band3 = band3_ref[...]
    mine = lax.broadcasted_iota(jnp.int32, (block, two), 1) % lanes
    mine = (mine >= 4) & (mine < 4 + cols)
    bias_sum = jnp.zeros((chans, two), F32)
    left1 = []
    for p in range(0, count, 2):
        y = dot(band3, pair(s_ref, p, sr, 3 * sr))
        hg = y[gr : 2 * gr] + shift_down(y[:gr]) + shift_up(y[2 * gr :])
        slope = jnp.concatenate([slope_ref[p], slope_ref[p + 1]], axis=1)
        pg = (hg * slope).astype(BF16)
        for q in range(2):
            pg_ref[(p + q + 1) * gr : (p + q + 2) * gr] = pg[:, q * lanes : (q + 1) * lanes]
        own = jnp.where(mine, pg.astype(F32)[chans : chans + block], 0.0)
        moved = (shift_down(own), own, shift_up(own))
        pieces = []
        for r in range(rows):
            part = slice(r * chans, (r + 1) * chans)
            bias_sum = bias_sum + own[part]
            pieces += [moved[c][part] for c in range(3)]
        left1.append(jnp.concatenate(pieces, axis=0).astype(BF16))

    inner = (rows + 4) * chans
    acc = None
    for p in range(0, count, 2):
        far = []
        for q in range(2):
            k = p + q
            parts = []
            for at in range(k * block, (k + 3) * block, block):
                parts += [
                    xu_ref[at + 2 * chans : at + block],
                    xo_ref[at : at + block],
                    xd_ref[at : at + block - 2 * chans],
                ]
            far.append(jnp.concatenate(parts + [h_ref[k * hr : (k + 3) * hr]], axis=0))
        side = jnp.concatenate([left2[p], left2[p + 1]], axis=1)
        side = jnp.concatenate([left1[p // 2], side, jnp.zeros((128 - 15 * chans, two), BF16)], axis=0)
        part = dot_t(jnp.concatenate(far, axis=1), side)
        acc = part if acc is None else acc + part

    def turned(at, amount):
        return pltpu.roll(acc[at : at + chans], amount % 128, 1)

    tap = 3 * chans
    blocks = [jnp.zeros((chans, 128), F32), jnp.zeros((chans, 128), F32)]
    lane_p = lax.broadcasted_iota(jnp.int32, (chans, 128), 1)
    for k in range(9):
        a, b = k // 3, k % 3
        to = tap * (k % 5)
        value = sum(turned(a * inner + (r + b + 1) * chans, to - tap * r) for r in range(rows))
        blocks[k // 5] = jnp.where((lane_p >= to) & (lane_p < to + tap), value, blocks[k // 5])
        base = 3 * inner + a * hr
        used = rows * tap
        if k < 8:
            value = sum(turned(base + (r + b) * chans, 96 + k - used - r) for r in range(2, 2 + rows))
            blocks[1] = jnp.where((lane_p >= 96) & (lane_p < 120) & (lane_p % 8 == k), value, blocks[1])
        else:
            for c in range(3):
                value = sum(turned(base + (r + b) * chans, 120 + c - used - lr * c - r) for r in range(2, 2 + rows))
                blocks[0] = jnp.where(lane_p == 120 + c, value, blocks[0])
    bias_sum = jnp.sum(bias_sum, axis=1, keepdims=True)
    blocks[1] = jnp.where(lane_p == 120, bias_sum, blocks[1])
    payload = jnp.concatenate(blocks, axis=0)
    shown = jnp.concatenate([disparity[2 : 2 + rows]] * 2, axis=0)
    tail = jnp.concatenate(terms(payload, 2) + terms(shown, 2), axis=0).astype(BF16)

    band4 = band4_ref[...]
    found = [None] * planes
    for p in range(0, count, 2):
        y = dot(band4, pair(pg_ref, p, gr, 3 * gr))
        y = y[block : 2 * block] + shift_down(y[:block]) + shift_up(y[2 * block :])
        for q in range(2):
            moved = y[:, q * lanes : (q + 1) * lanes]
            k = p + q
            found[k % planes] = moved
        if (p + 2) % planes == 0:
            near = jnp.concatenate(found[: planes // 2], axis=0)
            far = jnp.concatenate(found[planes // 2 :], axis=0)
            near = pltpu.roll(near, lanes - 4, 1)
            far = pltpu.roll(far, 60, 1)
            at = (p // planes) * (planes * block // 2)
            v_ref[at : at + planes * block // 2] = jnp.where(lanes_of(near) < 64, near, far).astype(BF16)
    size = planes * block // 2
    for s in range(disp):
        back_refs[s][:size] = v_ref[pl.ds(pl.multiple_of((di ^ s) * size, size), size)]
        back_refs[s][size:] = tail


def sum_body(chans, *refs):
    parts = refs[:-1]
    k = 2 * chans
    sums = []
    for r in parts:
        n = r.shape[0] - 2 * k - 16
        value = r[n:].astype(F32)
        sums.append(value[:k] + value[k : 2 * k])
    refs[-1][...] = tree_sum(sums)


def join_body(dims, *refs):
    planes, rows, chans, width, disp, space, cols, lanes = dims
    parts = refs[:disp]
    grad_ref, disp_ref = refs[disp:]
    di = lax.axis_index("disp")
    n = planes * rows * chans
    k = 4 * chans
    total = None
    for s in range(disp):
        j = di ^ s
        shown = parts[s][n // 2 + k :].astype(F32)
        shown = pltpu.roll(shown[:8] + shown[8:], lanes - 4, 1)
        main = parts[s][: n // 2].astype(F32)
        value = jnp.concatenate([main, pltpu.roll(main, 64, 1), shown], axis=0)
        value = jnp.where(lanes_of(value) < cols, value, 0.0)
        value = jnp.concatenate([value, jnp.zeros((value.shape[0], width - lanes), F32)], axis=1)
        value = pltpu.roll(value, j * cols, 1)
        total = value if total is None else total + value
    disp_ref[...] = total[n : n + rows]
    grad = total[:n].astype(BF16)
    for p in range(planes):
        for i in range(chans):
            at = (p * chans + i) * rows
            grad_ref[i, p] = grad[at : at + rows]


def tree_sum(parts):
    while len(parts) > 1:
        parts = [parts[k] + parts[k + 1] for k in range(0, len(parts), 2)]
    return parts[0]


def finish_body(chans, scale, *refs):
    gw_ref, gb_ref, gs_ref = refs[-3:]
    total = tree_sum([r[...] for r in refs[:-3]]) * scale
    flat = [jnp.transpose(total[:chans]), jnp.transpose(total[chans:])]
    for k in range(9):
        a, b = k // 3, k % 3
        for c in range(3):
            at = 3 * chans * (k % 5) + chans * c
            gw_ref[a, b, c] = flat[k // 5][at : at + chans]
            at = 96 + k + 8 * c if k < 8 else 120 + c
            gs_ref[a, b, c : c + 1] = flat[1 if k < 8 else 0][at : at + 1]
    gb_ref[...] = flat[1][120:121]


def flipped(body, count):
    def run(*refs):
        return body(*refs[:count][::-1], *refs[count:])

    return run


def exchange(sends, axis):
    count = lax.axis_size(axis)
    return [sends[0]] + [
        lax.ppermute(sends[s], axis, [(i, i ^ s) for i in range(count)]) for s in range(1, count)
    ]


def shards(volume, w_first, b_first, w_second, prior_logits, cotangent):
    chans, planes, rows, width = volume.shape
    disp = lax.axis_size("disp")
    space = lax.axis_size("space")
    cols = width // disp
    lanes = -(-(cols + 8) // 128) * 128
    dims = (planes, rows, chans, width, disp, space, cols, lanes)
    count = planes * disp
    n = planes * rows * chans

    piece = n // 2 + 8 + 6 * planes + 8
    sends = call(
        functools.partial(split_body, dims),
        "split",
        [((piece, lanes), BF16, True)] * disp,
        volume, prior_logits,
        inside=False,
        scratch=[
            pltpu.VMEM((4 * planes, width), F32),
            pltpu.VMEM((disp, piece, lanes), BF16),
        ]
        + [pltpu.VMEM((n, 128), F32)] * (width // 128),
    )
    pieces = exchange(sends, "disp")

    hr = rows + 6
    base1 = jnp.transpose(w_first, (2, 3, 0, 1, 4)).astype(F32)
    base1 = jnp.pad(base1, ((0, 0), (0, 0), (0, 0), (0, rows + 1), (0, 0)))
    base1 = base1.reshape(3 * chans, 3 * (rows + 4) * chans)
    base1 = jnp.pad(base1, ((0, 0), (0, -base1.shape[1] % 128)))
    base2 = jnp.transpose(w_second, (2, 0, 1, 3)).astype(F32)
    base2 = jnp.pad(base2, ((0, 0), (0, 0), (0, hr - 3), (0, 0))).reshape(3, 3 * hr * chans)
    base2 = jnp.pad(base2, ((0, 5), (0, -base2.shape[1] % 128)))
    base3 = jnp.transpose(w_second[::-1, ::-1], (2, 3, 0, 1)).astype(F32)
    base3 = jnp.pad(base3, ((0, 0), (0, 0), (0, 0), (0, 16 - 3))).reshape(3 * chans, 3 * 16)
    base3 = jnp.pad(base3, ((0, 0), (0, 128 - base3.shape[1])))
    base4 = jnp.transpose(w_first[::-1, ::-1], (2, 4, 0, 1, 3)).astype(F32)
    base4 = jnp.pad(base4, ((0, 0), (0, 0), (0, 0), (0, rows - 1), (0, 0))).reshape(
        3 * chans, 3 * (rows + 2) * chans
    )
    base4 = jnp.pad(base4, ((0, 0), (0, -base4.shape[1] % 128)))
    bands = call(
        functools.partial(bands_body, dims),
        "bands",
        (
            ((3 * (rows + 2) * chans, 3 * (rows + 4) * chans), BF16, True),
            ((3 * (rows + 4), 3 * hr * chans), BF16, True),
            ((3 * (rows + 2) * chans, 3 * 16), BF16, True),
            ((3 * rows * chans, 3 * (rows + 2) * chans), BF16, True),
            ((hr * chans, 2 * lanes), F32, True),
        ),
        base1, base2, base3, base4, b_first[None, :],
    )

    extra = -(-(6 * count + 6) // 16) * 16
    sent = (n // 2 + 8) * disp + extra // 2 + 8 * -(-extra // 128)
    send_one, send_two = call(
        flipped(functools.partial(rows_body, dims), disp),
        "rows",
        (((sent, lanes), BF16, True), ((sent, lanes), BF16, True)),
        *pieces[::-1], cotangent,
        scratch=[pltpu.VMEM((extra, lanes), F32), pltpu.VMEM((8 * disp, lanes), F32)],
    )
    mine = call(
        flipped(functools.partial(mine_body, dims), disp),
        "mine",
        (
            (((count + 2) * rows * chans, lanes), BF16, True),
            ((count, rows + 4, lanes), F32, True),
            ((rows + 4, lanes), F32, True),
        ),
        *pieces[::-1], cotangent,
    )
    z_one = lax.ppermute(send_one, "space", swap_pairs(space, 0))
    z_two = lax.ppermute(send_two, "space", swap_pairs(space, 1))

    tail = 4 * chans + 16
    backs = call(
        functools.partial(main_body, dims),
        "main",
        [((n // 2 + tail, lanes), BF16, True)] * disp,
        mine[0], z_one, z_two, *mine[1:], *bands,
        scratch=[
            pltpu.VMEM(((count + 2) * rows * chans, lanes), BF16),
            pltpu.VMEM(((count + 2) * rows * chans, lanes), BF16),
            pltpu.VMEM(((count + 2) * hr * chans, lanes), BF16),
            pltpu.VMEM((count, (rows + 2) * chans, lanes), F32),
            pltpu.VMEM((count, rows + 4, lanes), F32),
            pltpu.VMEM((rows + 4, lanes), F32),
            pltpu.VMEM(((count + 2) * 16, lanes), BF16),
            pltpu.VMEM(((count + 2) * (rows + 2) * chans, lanes), BF16),
            pltpu.VMEM((n // 2 * disp, lanes), BF16),
        ],
    )
    backs = exchange(backs, "disp")
    (pay,) = call(
        flipped(functools.partial(sum_body, chans), disp),
        "sum",
        (((2 * chans, lanes), F32, True),),
        *backs[::-1],
    )
    stages = radix_stages(space)
    for k, steps in enumerate(stages):
        parts = [pay] + [lax.ppermute(pay, "space", [(i, i ^ s) for i in range(space)]) for s in steps]
        if k < len(stages) - 1:
            pay = tree_sum(parts)

    volume_grad, disparity = call(
        flipped(functools.partial(join_body, dims), disp),
        "join",
        (((chans, planes, rows, width), BF16, False), ((rows, width), F32, False)),
        *backs[::-1],
    )

    scale = 16.0 / math.sqrt(planes * disp * rows * space * width)
    first_sum, bias_sum, second_sum = call(
        functools.partial(finish_body, chans, scale),
        "finish",
        (
            ((3, 3, 3, chans, chans), F32, False),
            ((1, chans), F32, False),
            ((3, 3, 3, chans), F32, False),
        ),
        *parts,
    )
    return (volume_grad, first_sum, bias_sum[0], second_sum, disparity)


def solution(mesh):
    return jax.shard_map(
        shards,
        mesh=mesh,
        in_specs=(
            P(None, "disp", ("groups", "space"), None),
            P(),
            P(),
            P(),
            P("disp", ("groups", "space"), None),
            P(("groups", "space"), None),
        ),
        out_specs=(
            P(None, "disp", ("groups", "space"), None),
            P(None, None, None, "groups", None),
            P("groups"),
            P(None, None, None, "groups"),
            P(("groups", "space"), None),
        ),
        check_vma=False,
    )
```

```python
import functools
import math

import jax
import jax.numpy as jnp
from jax import lax
from jax.experimental import pallas as pl
from jax.experimental.pallas import tpu as pltpu
from jax.sharding import PartitionSpec as P

F32 = jnp.float32
BF16 = jnp.bfloat16


def swap_pairs(count, step):
    pairs = []
    for i in range(count):
        j = i ^ 1 if step == 0 else ((i + 1) ^ 1) - 1
        pairs.append((i, j if 0 <= j < count else i))
    return pairs


def radix_stages(count):
    stages = []
    bit = 1
    while bit < count:
        if bit * 4 <= count:
            stages.append((bit, 2 * bit, 3 * bit))
            bit *= 4
        else:
            stages.append((bit,))
            bit *= 2
    return stages


def shift_up(x):
    return pltpu.roll(x, 1, 1)


def shift_down(x):
    return pltpu.roll(x, x.shape[1] - 1, 1)


def left(x, amount):
    return x if amount == 0 else pltpu.roll(x, x.shape[1] - amount, 1)


def right(x, amount):
    return x if amount == 0 else pltpu.roll(x, amount, 1)


def call(body, name, outs, *operands, scratch=(), inside=True):
    if inside:
        operands = [pltpu.with_memory_space_constraint(x, pltpu.VMEM) for x in operands]
    return pl.pallas_call(
        body,
        out_shape=tuple(
            pltpu.VMEM(shape, dtype) if inside else jax.ShapeDtypeStruct(shape, dtype)
            for shape, dtype, inside in outs
        ),
        in_specs=[pl.BlockSpec(memory_space=pltpu.VMEM)] * len(operands),
        out_specs=tuple(pl.BlockSpec(memory_space=pltpu.VMEM) for _ in outs),
        scratch_shapes=list(scratch),
        name=name,
    )(*operands)


def dot(a, b):
    return lax.dot_general(a, b, (((1,), (0,)), ((), ())), preferred_element_type=F32)


def dot_t(a, b):
    return lax.dot_general(a, b, (((1,), (1,)), ((), ())), preferred_element_type=F32)


def terms(value, count=3):
    out = []
    for _ in range(count):
        term = value.astype(BF16).astype(F32)
        out.append(term)
        value = value - term
    return out


def window(x, start, size):
    width = x.shape[1]
    moved = pltpu.roll(x, (width - start) % width, 1)[:, :size]
    column = start + lax.broadcasted_iota(jnp.int32, moved.shape, 1)
    return jnp.where((column >= 0) & (column < width), moved, 0.0)


def lanes_of(x):
    return lax.broadcasted_iota(jnp.int32, x.shape, 1)


def pack(x):
    n = x.shape[0]
    far = pltpu.roll(x[n // 2 :], 64, 1)
    out = [jnp.where(lanes_of(far) < 64, x[: n // 2], far)]
    for t in range(-(-n // 128)):
        rest = jnp.zeros((8, 128), F32)
        lane = lanes_of(rest)
        for k in range(16):
            at = (t * 16 + k) * 8
            if at < n:
                moved = pltpu.roll(x[at : at + 8], (8 * k + 64) % 128, 1)
                rest = jnp.where((lane >= 8 * k) & (lane < 8 * k + 8), moved, rest)
        out.append(rest)
    return out


def unpack(main, rest, k):
    n = main.shape[0]
    value = main[8 * k : 8 * k + 8] if 8 * k < n else pltpu.roll(main[8 * k - n : 8 * k - n + 8], 64, 1)
    moved = rest[8 * (k // 16) : 8 * (k // 16) + 8]
    moved = pltpu.roll(moved, (64 - 8 * (k % 16)) % 128, 1)
    return jnp.where(lanes_of(value) < 64, value, moved)


def split_body(dims, volume_ref, prior_ref, *refs):
    planes, rows, chans, width, disp, space, cols, lanes = dims
    out_refs = refs[:disp]
    wide_ref, found_ref = refs[disp : disp + 2]
    own_refs = refs[disp + 2 :]
    di = lax.axis_index("disp")
    group = 2 * planes
    n = planes * rows * chans
    for i in range(chans):
        value = volume_ref[i].astype(F32)
        for p in range(planes):
            for j, ref in enumerate(own_refs):
                ref[pl.ds(p * rows * chans + i, rows, stride=chans)] = value[p][:, j * 128 : (j + 1) * 128]
    for h in range(2):
        for p in range(planes):
            at = h * group + 2 * p
            wide_ref[at : at + 2] = prior_ref[p, 2 * h : 2 * h + 2]
    wide = wide_ref[...]
    pieces = [jnp.concatenate([ref[...] for ref in own_refs], axis=1)]
    for h in range(2):
        pieces += terms(wide[h * group : (h + 1) * group])
    whole = jnp.concatenate(pieces, axis=0)
    for t in range(disp):
        moved = window(whole, t * cols - 4, lanes)
        found_ref[t] = jnp.concatenate(pack(moved[:n]) + pack(moved[n:]), axis=0).astype(BF16)
    for s in range(disp):
        out_refs[s][...] = found_ref[di ^ s]


def rows_body(dims, *refs):
    planes, rows, chans, width, disp, space, cols, lanes = dims
    piece_refs = refs[:disp]
    cot_in_ref, one_ref, two_ref, wide_ref = refs[disp:]
    di = lax.axis_index("disp")
    even = lax.axis_index("space") % 2 == 0
    n = planes * rows * chans
    half = n // 2
    group = 2 * planes
    cot = window(jnp.concatenate([cot_in_ref[...]] * 2, axis=0), di * cols - 4, lanes)[:rows]
    fine = []
    rests = []
    for s in range(disp):
        block = piece_refs[s][:half]
        one_ref[s * half : (s + 1) * half] = block
        two_ref[s * half : (s + 1) * half] = block
        value = piece_refs[s][half:].astype(F32)
        rests.append(value[:8])
        value = value[8:]
        fine.append([unpack(value[: 3 * group], value[3 * group :], k) for k in range(6)])
    wide_ref[...] = jnp.zeros(wide_ref.shape, F32)
    ends = []
    for h in range(2):
        for t, term in enumerate(terms(cot[2 * h : 2 * h + 2])):
            wide_ref[h, 2 * t : 2 * t + 2] = term
        parts = [fine[s][3 * h + t] for s in range(disp) for t in range(3)]
        ends.append(jnp.concatenate(rests + pack(jnp.concatenate(parts + [wide_ref[h]], axis=0)), axis=0))
    one_ref[disp * half :] = jnp.where(even, ends[1], ends[0]).astype(BF16)
    two_ref[disp * half :] = jnp.where(even, ends[0], ends[1]).astype(BF16)


def mine_body(dims, *refs):
    planes, rows, chans, width, disp, space, cols, lanes = dims
    piece_refs = refs[:disp]
    cot_in_ref, x_ref, prior_ref, cot_ref = refs[disp:]
    di = lax.axis_index("disp")
    block = rows * chans
    half = planes * block // 2
    group = 2 * planes
    prior_ref[...] = jnp.zeros(prior_ref.shape, F32)
    cot_ref[...] = jnp.zeros(cot_ref.shape, F32)
    cot = jnp.concatenate([cot_in_ref[...]] * 2, axis=0)
    cot_ref[2 : 2 + rows] = window(cot, di * cols - 4, lanes)[:rows]
    x_ref[:block] = jnp.zeros((block, lanes), BF16)
    x_ref[x_ref.shape[0] - block :] = jnp.zeros((block, lanes), BF16)
    for s in range(disp):
        g = di ^ s
        main = piece_refs[s][:half].astype(F32)
        rest = piece_refs[s][half:].astype(F32)
        for p in range(planes):
            value = [unpack(main, rest[:8], p * rows + r) for r in range(rows)]
            at = pl.multiple_of((g * planes + p + 1) * block, block)
            x_ref[pl.ds(at, block)] = jnp.concatenate(value, axis=0).astype(BF16)
        value = [unpack(rest[8 : 8 + 3 * group], rest[8 + 3 * group :], k) for k in range(6)]
        for h in range(2):
            prior = value[3 * h] + value[3 * h + 1] + value[3 * h + 2]
            for p in range(planes):
                prior_ref[g * planes + p, 2 + 2 * h : 4 + 2 * h] = prior[2 * p : 2 * p + 2]


def bands_body(dims, base1_ref, base2_ref, base3_ref, base4_ref, bias_ref, band1_ref, band2_ref, band3_ref, band4_ref, col_ref):
    planes, rows, chans, width, disp, space, cols, lanes = dims

    def band(base, groups, count, step, used):
        pieces = []
        for c in range(3):
            piece = base[c * groups : (c + 1) * groups]
            for r in range(count):
                pieces.append(right(piece, step * r))
        return jnp.concatenate(pieces, axis=0)[:, :used].astype(BF16)

    band1_ref[...] = band(base1_ref[...], chans, rows + 2, chans, band1_ref.shape[1])
    band2_ref[...] = band(base2_ref[...], 1, rows + 4, chans, band2_ref.shape[1])
    band3_ref[...] = band(base3_ref[...], chans, rows + 2, 1, band3_ref.shape[1])
    band4 = band(base4_ref[...], chans, rows, chans, band4_ref.shape[1])
    n = rows * chans
    to = lax.broadcasted_iota(jnp.int32, (3 * n, 3 * n), 0)
    at = lax.broadcasted_iota(jnp.int32, (3 * n, 3 * n), 1)
    source = (to // n) * n + (to % rows) * chans + (to % n) // rows
    band4_ref[...] = dot((at == source).astype(BF16), band4).astype(BF16)
    diag = lax.broadcasted_iota(jnp.int32, (chans, chans), 0) == lax.broadcasted_iota(
        jnp.int32, (chans, chans), 1
    )
    bias = jnp.sum(jnp.where(diag, bias_ref[...], 0.0), axis=1, keepdims=True)
    col_ref[...] = jnp.concatenate([jnp.broadcast_to(bias, (chans, 2 * lanes))] * (rows + 6), axis=0)


def main_body(dims, *refs):
    planes, rows, chans, width, disp, space, cols, lanes = dims
    xo_ref, za_ref, zb_ref, prior_in_ref, cot_in_ref, band1_ref, band2_ref, band3_ref, band4_ref, col_ref = refs[:10]
    back_refs = refs[10 : 10 + disp]
    xu_ref, xd_ref, h_ref, slope_ref, prior_ref, cot_ref, s_ref, pg_ref, v_ref = refs[10 + disp :]
    zi = lax.axis_index("space")
    di = lax.axis_index("disp")
    z_even = zi % 2 == 0
    count = planes * disp
    n = count * rows * chans
    block = rows * chans
    hr = (rows + 6) * chans
    gr = (rows + 2) * chans
    lr = rows + 4
    sr = 16
    two = 2 * lanes

    def place_rows(src, ref):
        main = src[: n // 2].astype(F32)
        rest = src[n // 2 : n // 2 + 8 * disp].astype(F32)
        side = planes * block // 2
        for k in range(count):
            s = k // planes
            p = k % planes
            value = [
                unpack(main[s * side : (s + 1) * side], rest[8 * s : 8 * s + 8], p * rows + r) for r in range(rows)
            ]
            at = pl.multiple_of(((di ^ s) * planes + p + 1) * block, block)
            ref[pl.ds(at, block)] = jnp.concatenate(value, axis=0).astype(BF16)

    for ref in (xu_ref, xd_ref):
        ref[:block] = jnp.zeros((block, lanes), BF16)
        ref[(count + 1) * block :] = jnp.zeros((block, lanes), BF16)
    h_ref[:hr] = jnp.zeros((hr, lanes), BF16)
    h_ref[(count + 1) * hr :] = jnp.zeros((hr, lanes), BF16)
    s_ref[...] = jnp.zeros(s_ref.shape, BF16)
    pg_ref[:gr] = jnp.zeros((gr, lanes), BF16)
    pg_ref[(count + 1) * gr :] = jnp.zeros((gr, lanes), BF16)
    prior_ref[...] = prior_in_ref[...]
    cot_ref[...] = cot_in_ref[...]
    half = 2 * planes

    def place(ok, first, one, other, ref, at8):
        def put(src):
            if src is None:
                ref[...] = jnp.zeros(ref.shape, BF16)
                for k in range(count):
                    prior_ref[k, at8 : at8 + 2] = jnp.zeros((2, lanes), F32)
                cot_ref[at8 : at8 + 2] = jnp.zeros((2, lanes), F32)
                return
            place_rows(src, ref)
            extra = src[n // 2 + 8 * disp :].astype(F32)
            used = -(-(3 * half * disp + 6) // 16) * 16
            value = [unpack(extra[: used // 2], extra[used // 2 :], k) for k in range(3 * disp + 1)]
            for s in range(disp):
                prior = value[3 * s] + value[3 * s + 1] + value[3 * s + 2]
                for p in range(planes):
                    prior_ref[(di ^ s) * planes + p, at8 : at8 + 2] = prior[2 * p : 2 * p + 2]
            cot = value[3 * disp]
            cot_ref[at8 : at8 + 2] = cot[:2] + cot[2:4] + cot[4:6]

        pl.when(ok & first)(lambda: put(one))
        pl.when(ok & jnp.logical_not(first))(lambda: put(other))
        pl.when(jnp.logical_not(ok))(lambda: put(None))

    place(zi > 0, z_even, zb_ref, za_ref, xu_ref, 0)
    place(zi < space - 1, z_even, za_ref, zb_ref, xd_ref, 2 + rows)

    def pair(ref, p, size, taken):
        return jnp.concatenate([ref[p * size : p * size + taken], ref[(p + 1) * size : (p + 1) * size + taken]], axis=1)

    lane = lax.broadcasted_iota(jnp.int32, (hr, two), 1) % lanes
    column = di * cols - 4 + lane
    row_at = zi * rows - 3 + lax.broadcasted_iota(jnp.int32, (hr, two), 0) // chans
    inside = ((row_at >= 0) & (row_at < space * rows) & (column >= 0) & (column < width)).astype(F32)
    band1 = band1_ref[...]
    bias = col_ref[...]
    yr = (rows + 2) * chans
    for p in range(0, count, 2):
        pre = []
        for at, (near, far) in ((0, (xu_ref, xo_ref)), (4 * chans, (xo_ref, xd_ref))):
            rhs = []
            for q in range(2):
                parts = []
                for k in range(p + q, p + q + 3):
                    parts += [near[k * block : (k + 1) * block], far[k * block : (k + 1) * block]]
                rhs.append(jnp.concatenate(parts, axis=0))
            y = dot(band1, jnp.concatenate(rhs, axis=1))
            skip = at // 2
            y = [y[c * yr + skip : (c + 1) * yr] for c in range(3)]
            pre.append(y[1] + shift_up(y[0]) + shift_down(y[2]))
        pre = jnp.concatenate(pre, axis=0) + bias
        sig = 0.5 * jnp.tanh(0.5 * pre) + 0.5
        hidden = (pre * sig * inside).astype(BF16)
        slope = (sig * (1.0 + pre * (1.0 - sig)) * inside)[2 * chans : hr - 2 * chans]
        for q in range(2):
            part = slice(q * lanes, (q + 1) * lanes)
            h_ref[(p + q + 1) * hr : (p + q + 2) * hr] = hidden[:, part]
            slope_ref[p + q] = slope[:, part]

    band2 = band2_ref[...]
    logits = []
    for p in range(0, count, 2):
        y = dot(band2, pair(h_ref, p, hr, 3 * hr))
        y = y[lr : 2 * lr] + shift_up(y[:lr]) + shift_down(y[2 * lr :])
        logits += [y[:, :lanes] + prior_ref[p], y[:, lanes:] + prior_ref[p + 1]]

    top = logits[0]
    for value in logits[1:]:
        top = jnp.maximum(top, value)
    summed = jnp.zeros((lr, lanes), F32)
    moment = jnp.zeros((lr, lanes), F32)
    weights = []
    for k, value in enumerate(logits):
        e = jnp.exp(value - top)
        weights.append(e)
        summed = summed + e
        moment = moment + e * ((k + 0.5) / count)
    disparity = moment / summed
    coef = cot_ref[...] / summed
    mine = lax.broadcasted_iota(jnp.int32, (lr, lanes), 1)
    mine = (mine >= 4) & (mine < 4 + cols)
    left2 = []
    for k in range(count):
        score = (coef * weights[k] * ((k + 0.5) / count - disparity)).astype(BF16)
        s_ref[(k + 1) * sr : (k + 1) * sr + lr] = score
        score = jnp.where(mine, score.astype(F32), 0.0)
        left2.append(jnp.concatenate([shift_down(score), score, shift_up(score)], axis=0).astype(BF16))

    band3 = band3_ref[...]
    mine = lax.broadcasted_iota(jnp.int32, (block, two), 1) % lanes
    mine = (mine >= 4) & (mine < 4 + cols)
    bias_sum = jnp.zeros((chans, two), F32)
    left1 = []
    for p in range(0, count, 2):
        y = dot(band3, pair(s_ref, p, sr, 3 * sr))
        hg = y[gr : 2 * gr] + shift_down(y[:gr]) + shift_up(y[2 * gr :])
        slope = jnp.concatenate([slope_ref[p], slope_ref[p + 1]], axis=1)
        pg = (hg * slope).astype(BF16)
        for q in range(2):
            pg_ref[(p + q + 1) * gr : (p + q + 2) * gr] = pg[:, q * lanes : (q + 1) * lanes]
        own = jnp.where(mine, pg.astype(F32)[chans : chans + block], 0.0)
        moved = (shift_down(own), own, shift_up(own))
        pieces = []
        for r in range(rows):
            part = slice(r * chans, (r + 1) * chans)
            bias_sum = bias_sum + own[part]
            pieces += [moved[c][part] for c in range(3)]
        left1.append(jnp.concatenate(pieces, axis=0).astype(BF16))

    inner = (rows + 4) * chans
    acc = None
    for p in range(0, count, 2):
        far = []
        for q in range(2):
            k = p + q
            parts = []
            for at in range(k * block, (k + 3) * block, block):
                parts += [
                    xu_ref[at + 2 * chans : at + block],
                    xo_ref[at : at + block],
                    xd_ref[at : at + block - 2 * chans],
                ]
            far.append(jnp.concatenate(parts + [h_ref[k * hr : (k + 3) * hr]], axis=0))
        side = jnp.concatenate([left2[p], left2[p + 1]], axis=1)
        side = jnp.concatenate([left1[p // 2], side, jnp.zeros((128 - 15 * chans, two), BF16)], axis=0)
        part = dot_t(jnp.concatenate(far, axis=1), side)
        acc = part if acc is None else acc + part

    def turned(at, amount):
        return pltpu.roll(acc[at : at + chans], amount % 128, 1)

    tap = 3 * chans
    blocks = [jnp.zeros((chans, 128), F32), jnp.zeros((chans, 128), F32)]
    lane_p = lax.broadcasted_iota(jnp.int32, (chans, 128), 1)
    for k in range(9):
        a, b = k // 3, k % 3
        to = tap * (k % 5)
        value = sum(turned(a * inner + (r + b + 1) * chans, to - tap * r) for r in range(rows))
        blocks[k // 5] = jnp.where((lane_p >= to) & (lane_p < to + tap), value, blocks[k // 5])
        base = 3 * inner + a * hr
        used = rows * tap
        if k < 8:
            value = sum(turned(base + (r + b) * chans, 96 + k - used - r) for r in range(2, 2 + rows))
            blocks[1] = jnp.where((lane_p >= 96) & (lane_p < 120) & (lane_p % 8 == k), value, blocks[1])
        else:
            for c in range(3):
                value = sum(turned(base + (r + b) * chans, 120 + c - used - lr * c - r) for r in range(2, 2 + rows))
                blocks[0] = jnp.where(lane_p == 120 + c, value, blocks[0])
    bias_sum = jnp.sum(bias_sum, axis=1, keepdims=True)
    blocks[1] = jnp.where(lane_p == 120, bias_sum, blocks[1])
    payload = jnp.concatenate(blocks, axis=0)
    shown = jnp.concatenate([disparity[2 : 2 + rows]] * 2, axis=0)
    shown = terms(shown, 2)
    shown = jnp.where(lax.broadcasted_iota(jnp.int32, shown[0].shape, 0) < rows, shown[0], shown[1])
    tail = jnp.concatenate(terms(payload, 2) + [shown], axis=0).astype(BF16)

    band4 = band4_ref[...]
    found = [None] * planes
    for p in range(0, count, 2):
        y = dot(band4, pair(pg_ref, p, gr, 3 * gr))
        y = y[block : 2 * block] + shift_down(y[:block]) + shift_up(y[2 * block :])
        for q in range(2):
            moved = y[:, q * lanes : (q + 1) * lanes]
            k = p + q
            found[k % planes] = moved
        if (p + 2) % planes == 0:
            near = jnp.concatenate(found[: planes // 2], axis=0)
            far = jnp.concatenate(found[planes // 2 :], axis=0)
            near = pltpu.roll(near, lanes - 4, 1)
            far = pltpu.roll(far, 60, 1)
            at = (p // planes) * (planes * block // 2)
            v_ref[at : at + planes * block // 2] = jnp.where(lanes_of(near) < 64, near, far).astype(BF16)
    size = planes * block // 2
    for s in range(disp):
        back_refs[s][:size] = v_ref[pl.ds(pl.multiple_of((di ^ s) * size, size), size)]
        back_refs[s][size:] = tail


def sum_body(chans, *refs):
    parts = refs[:-1]
    k = 2 * chans
    sums = []
    for r in parts:
        n = r.shape[0] - 2 * k - 8
        value = r[n:].astype(F32)
        sums.append(value[:k] + value[k : 2 * k])
    refs[-1][...] = tree_sum(sums)


def join_body(dims, *refs):
    planes, rows, chans, width, disp, space, cols, lanes = dims
    parts = refs[:disp]
    grad_ref, disp_ref = refs[disp:]
    di = lax.axis_index("disp")
    n = planes * rows * chans
    k = 4 * chans
    total = None
    for s in range(disp):
        j = di ^ s
        shown = parts[s][n // 2 + k :].astype(F32)
        shown = pltpu.roll(shown + pltpu.roll(shown, rows, 0), lanes - 4, 1)
        main = parts[s][: n // 2].astype(F32)
        value = jnp.concatenate([main, pltpu.roll(main, 64, 1), shown], axis=0)
        value = jnp.where(lanes_of(value) < cols, value, 0.0)
        value = jnp.concatenate([value, jnp.zeros((value.shape[0], width - lanes), F32)], axis=1)
        value = pltpu.roll(value, j * cols, 1)
        total = value if total is None else total + value
    disp_ref[...] = total[n : n + rows]
    grad = total[:n].astype(BF16)
    for p in range(planes):
        for i in range(chans):
            at = (p * chans + i) * rows
            grad_ref[i, p] = grad[at : at + rows]


def tree_sum(parts):
    while len(parts) > 1:
        parts = [parts[k] + parts[k + 1] for k in range(0, len(parts), 2)]
    return parts[0]


def finish_body(chans, scale, *refs):
    gw_ref, gb_ref, gs_ref = refs[-3:]
    total = tree_sum([r[...] for r in refs[:-3]]) * scale
    flat = [jnp.transpose(total[:chans]), jnp.transpose(total[chans:])]
    for k in range(9):
        a, b = k // 3, k % 3
        for c in range(3):
            at = 3 * chans * (k % 5) + chans * c
            gw_ref[a, b, c] = flat[k // 5][at : at + chans]
            at = 96 + k + 8 * c if k < 8 else 120 + c
            gs_ref[a, b, c : c + 1] = flat[1 if k < 8 else 0][at : at + 1]
    gb_ref[...] = flat[1][120:121]


def flipped(body, count):
    def run(*refs):
        return body(*refs[:count][::-1], *refs[count:])

    return run


def exchange(sends, axis):
    count = lax.axis_size(axis)
    return [sends[0]] + [
        lax.ppermute(sends[s], axis, [(i, i ^ s) for i in range(count)]) for s in range(1, count)
    ]


def shards(volume, w_first, b_first, w_second, prior_logits, cotangent):
    chans, planes, rows, width = volume.shape
    disp = lax.axis_size("disp")
    space = lax.axis_size("space")
    cols = width // disp
    lanes = -(-(cols + 8) // 128) * 128
    dims = (planes, rows, chans, width, disp, space, cols, lanes)
    count = planes * disp
    n = planes * rows * chans

    piece = n // 2 + 8 + 6 * planes + 8
    sends = call(
        functools.partial(split_body, dims),
        "split",
        [((piece, lanes), BF16, True)] * disp,
        volume, prior_logits,
        inside=False,
        scratch=[
            pltpu.VMEM((4 * planes, width), F32),
            pltpu.VMEM((disp, piece, lanes), BF16),
        ]
        + [pltpu.VMEM((n, 128), F32)] * (width // 128),
    )
    pieces = exchange(sends, "disp")

    hr = rows + 6
    base1 = jnp.transpose(w_first, (2, 3, 0, 1, 4)).astype(F32)
    base1 = jnp.pad(base1, ((0, 0), (0, 0), (0, 0), (0, rows + 1), (0, 0)))
    base1 = base1.reshape(3 * chans, 3 * (rows + 4) * chans)
    base1 = jnp.pad(base1, ((0, 0), (0, -base1.shape[1] % 128)))
    base2 = jnp.transpose(w_second, (2, 0, 1, 3)).astype(F32)
    base2 = jnp.pad(base2, ((0, 0), (0, 0), (0, hr - 3), (0, 0))).reshape(3, 3 * hr * chans)
    base2 = jnp.pad(base2, ((0, 5), (0, -base2.shape[1] % 128)))
    base3 = jnp.transpose(w_second[::-1, ::-1], (2, 3, 0, 1)).astype(F32)
    base3 = jnp.pad(base3, ((0, 0), (0, 0), (0, 0), (0, 16 - 3))).reshape(3 * chans, 3 * 16)
    base3 = jnp.pad(base3, ((0, 0), (0, 128 - base3.shape[1])))
    base4 = jnp.transpose(w_first[::-1, ::-1], (2, 4, 0, 1, 3)).astype(F32)
    base4 = jnp.pad(base4, ((0, 0), (0, 0), (0, 0), (0, rows - 1), (0, 0))).reshape(
        3 * chans, 3 * (rows + 2) * chans
    )
    base4 = jnp.pad(base4, ((0, 0), (0, -base4.shape[1] % 128)))
    bands = call(
        functools.partial(bands_body, dims),
        "bands",
        (
            ((3 * (rows + 2) * chans, 3 * (rows + 4) * chans), BF16, True),
            ((3 * (rows + 4), 3 * hr * chans), BF16, True),
            ((3 * (rows + 2) * chans, 3 * 16), BF16, True),
            ((3 * rows * chans, 3 * (rows + 2) * chans), BF16, True),
            ((hr * chans, 2 * lanes), F32, True),
        ),
        base1, base2, base3, base4, b_first[None, :],
    )

    extra = -(-(6 * count + 6) // 16) * 16
    sent = (n // 2 + 8) * disp + extra // 2 + 8 * -(-extra // 128)
    send_one, send_two = call(
        flipped(functools.partial(rows_body, dims), disp),
        "rows",
        (((sent, lanes), BF16, True), ((sent, lanes), BF16, True)),
        *pieces[::-1], cotangent,
        scratch=[pltpu.VMEM((2, extra - 6 * count, lanes), F32)],
    )
    mine = call(
        flipped(functools.partial(mine_body, dims), disp),
        "mine",
        (
            (((count + 2) * rows * chans, lanes), BF16, True),
            ((count, rows + 4, lanes), F32, True),
            ((rows + 4, lanes), F32, True),
        ),
        *pieces[::-1], cotangent,
    )
    z_one = lax.ppermute(send_one, "space", swap_pairs(space, 0))
    z_two = lax.ppermute(send_two, "space", swap_pairs(space, 1))

    tail = 4 * chans + 8
    backs = call(
        functools.partial(main_body, dims),
        "main",
        [((n // 2 + tail, lanes), BF16, True)] * disp,
        mine[0], z_one, z_two, *mine[1:], *bands,
        scratch=[
            pltpu.VMEM(((count + 2) * rows * chans, lanes), BF16),
            pltpu.VMEM(((count + 2) * rows * chans, lanes), BF16),
            pltpu.VMEM(((count + 2) * hr * chans, lanes), BF16),
            pltpu.VMEM((count, (rows + 2) * chans, lanes), F32),
            pltpu.VMEM((count, rows + 4, lanes), F32),
            pltpu.VMEM((rows + 4, lanes), F32),
            pltpu.VMEM(((count + 2) * 16, lanes), BF16),
            pltpu.VMEM(((count + 2) * (rows + 2) * chans, lanes), BF16),
            pltpu.VMEM((n // 2 * disp, lanes), BF16),
        ],
    )
    backs = exchange(backs, "disp")
    (pay,) = call(
        flipped(functools.partial(sum_body, chans), disp),
        "sum",
        (((2 * chans, lanes), F32, True),),
        *backs[::-1],
    )
    stages = radix_stages(space)
    for k, steps in enumerate(stages):
        parts = [pay] + [lax.ppermute(pay, "space", [(i, i ^ s) for i in range(space)]) for s in steps]
        if k < len(stages) - 1:
            pay = tree_sum(parts)

    volume_grad, disparity = call(
        flipped(functools.partial(join_body, dims), disp),
        "join",
        (((chans, planes, rows, width), BF16, False), ((rows, width), F32, False)),
        *backs[::-1],
    )

    scale = 16.0 / math.sqrt(planes * disp * rows * space * width)
    first_sum, bias_sum, second_sum = call(
        functools.partial(finish_body, chans, scale),
        "finish",
        (
            ((3, 3, 3, chans, chans), F32, False),
            ((1, chans), F32, False),
            ((3, 3, 3, chans), F32, False),
        ),
        *parts,
    )
    return (volume_grad, first_sum, bias_sum[0], second_sum, disparity)


def solution(mesh):
    return jax.shard_map(
        shards,
        mesh=mesh,
        in_specs=(
            P(None, "disp", ("groups", "space"), None),
            P(),
            P(),
            P(),
            P("disp", ("groups", "space"), None),
            P(("groups", "space"), None),
        ),
        out_specs=(
            P(None, "disp", ("groups", "space"), None),
            P(None, None, None, "groups", None),
            P("groups"),
            P(None, None, None, "groups"),
            P(("groups", "space"), None),
        ),
        check_vma=False,
    )
```

```python
import functools
import math

import jax
import jax.numpy as jnp
from jax import lax
from jax.experimental import pallas as pl
from jax.experimental.pallas import tpu as pltpu
from jax.sharding import PartitionSpec as P

F32 = jnp.float32
BF16 = jnp.bfloat16


def swap_pairs(count, step):
    pairs = []
    for i in range(count):
        j = i ^ 1 if step == 0 else ((i + 1) ^ 1) - 1
        pairs.append((i, j if 0 <= j < count else i))
    return pairs


def radix_stages(count):
    stages = []
    bit = 1
    while bit < count:
        if bit * 4 <= count:
            stages.append((bit, 2 * bit, 3 * bit))
            bit *= 4
        else:
            stages.append((bit,))
            bit *= 2
    return stages


def shift_up(x):
    return pltpu.roll(x, 1, 1)


def shift_down(x):
    return pltpu.roll(x, x.shape[1] - 1, 1)


def left(x, amount):
    return x if amount == 0 else pltpu.roll(x, x.shape[1] - amount, 1)


def right(x, amount):
    return x if amount == 0 else pltpu.roll(x, amount, 1)


def call(body, name, outs, *operands, scratch=(), inside=True):
    if inside:
        operands = [pltpu.with_memory_space_constraint(x, pltpu.VMEM) for x in operands]
    return pl.pallas_call(
        body,
        out_shape=tuple(
            pltpu.VMEM(shape, dtype) if inside else jax.ShapeDtypeStruct(shape, dtype)
            for shape, dtype, inside in outs
        ),
        in_specs=[pl.BlockSpec(memory_space=pltpu.VMEM)] * len(operands),
        out_specs=tuple(pl.BlockSpec(memory_space=pltpu.VMEM) for _ in outs),
        scratch_shapes=list(scratch),
        name=name,
    )(*operands)


def dot(a, b):
    return lax.dot_general(a, b, (((1,), (0,)), ((), ())), preferred_element_type=F32)


def dot_t(a, b):
    return lax.dot_general(a, b, (((1,), (1,)), ((), ())), preferred_element_type=F32)


def terms(value, count=3):
    out = []
    for _ in range(count):
        term = value.astype(BF16).astype(F32)
        out.append(term)
        value = value - term
    return out


def window(x, start, size):
    width = x.shape[1]
    moved = pltpu.roll(x, (width - start) % width, 1)[:, :size]
    if isinstance(start, int) and 0 <= start <= width - 72:
        return moved
    column = start + lax.broadcasted_iota(jnp.int32, moved.shape, 1)
    return jnp.where((column >= 0) & (column < width), moved, 0.0)


def lanes_of(x):
    return lax.broadcasted_iota(jnp.int32, x.shape, 1)


def pack(x):
    n = x.shape[0]
    far = pltpu.roll(x[n // 2 :], 64, 1)
    out = [jnp.where(lanes_of(far) < 64, x[: n // 2], far)]
    for t in range(-(-n // 128)):
        rest = jnp.zeros((8, 128), F32)
        lane = lanes_of(rest)
        for k in range(16):
            at = (t * 16 + k) * 8
            if at < n:
                moved = pltpu.roll(x[at : at + 8], (8 * k + 64) % 128, 1)
                rest = jnp.where((lane >= 8 * k) & (lane < 8 * k + 8), moved, rest)
        out.append(rest)
    return out


def unpack(main, rest, k):
    n = main.shape[0]
    value = main[8 * k : 8 * k + 8] if 8 * k < n else pltpu.roll(main[8 * k - n : 8 * k - n + 8], 64, 1)
    moved = rest[8 * (k // 16) : 8 * (k // 16) + 8]
    moved = pltpu.roll(moved, (64 - 8 * (k % 16)) % 128, 1)
    return jnp.where(lanes_of(value) < 64, value, moved)


def split_body(dims, volume_ref, prior_ref, *refs):
    planes, rows, chans, width, disp, space, cols, lanes = dims
    out_refs = refs[:disp]
    wide_ref, found_ref = refs[disp : disp + 2]
    own_refs = refs[disp + 2 :]
    di = lax.axis_index("disp")
    group = 2 * planes
    n = planes * rows * chans
    for i in range(chans):
        value = volume_ref[i].astype(F32)
        for p in range(planes):
            for j, ref in enumerate(own_refs):
                ref[pl.ds(p * rows * chans + i, rows, stride=chans)] = value[p][:, j * 128 : (j + 1) * 128]
    for h in range(2):
        for p in range(planes):
            at = h * group + 2 * p
            wide_ref[at : at + 2] = prior_ref[p, 2 * h : 2 * h + 2]
    wide = wide_ref[...]
    pieces = [jnp.concatenate([ref[...] for ref in own_refs], axis=1)]
    for h in range(2):
        pieces += terms(wide[h * group : (h + 1) * group])
    whole = jnp.concatenate(pieces, axis=0)
    for t in range(disp):
        moved = window(whole, t * cols - 4, lanes)
        found_ref[t] = jnp.concatenate(pack(moved[:n]) + pack(moved[n:]), axis=0).astype(BF16)
    for s in range(disp):
        out_refs[s][...] = found_ref[di ^ s]


def rows_body(dims, *refs):
    planes, rows, chans, width, disp, space, cols, lanes = dims
    piece_refs = refs[:disp]
    cot_in_ref, one_ref, two_ref, wide_ref = refs[disp:]
    di = lax.axis_index("disp")
    even = lax.axis_index("space") % 2 == 0
    n = planes * rows * chans
    half = n // 2
    group = 2 * planes
    cot = window(jnp.concatenate([cot_in_ref[...]] * 2, axis=0), di * cols - 4, lanes)[:rows]
    fine = []
    rests = []
    for s in range(disp):
        block = piece_refs[s][:half]
        one_ref[s * half : (s + 1) * half] = block
        two_ref[s * half : (s + 1) * half] = block
        value = piece_refs[s][half:].astype(F32)
        rests.append(value[:8])
        value = value[8:]
        fine.append([unpack(value[: 3 * group], value[3 * group :], k) for k in range(6)])
    wide_ref[...] = jnp.zeros(wide_ref.shape, F32)
    ends = []
    for h in range(2):
        for t, term in enumerate(terms(cot[2 * h : 2 * h + 2])):
            wide_ref[h, 2 * t : 2 * t + 2] = term
        parts = [fine[s][3 * h + t] for s in range(disp) for t in range(3)]
        ends.append(jnp.concatenate(rests + pack(jnp.concatenate(parts + [wide_ref[h]], axis=0)), axis=0))
    one_ref[disp * half :] = jnp.where(even, ends[1], ends[0]).astype(BF16)
    two_ref[disp * half :] = jnp.where(even, ends[0], ends[1]).astype(BF16)


def mine_body(dims, *refs):
    planes, rows, chans, width, disp, space, cols, lanes = dims
    piece_refs = refs[:disp]
    cot_in_ref, x_ref, prior_ref, cot_ref = refs[disp:]
    di = lax.axis_index("disp")
    block = rows * chans
    half = planes * block // 2
    group = 2 * planes
    prior_ref[...] = jnp.zeros(prior_ref.shape, F32)
    cot_ref[...] = jnp.zeros(cot_ref.shape, F32)
    cot = jnp.concatenate([cot_in_ref[...]] * 2, axis=0)
    cot_ref[2 : 2 + rows] = window(cot, di * cols - 4, lanes)[:rows]
    x_ref[:block] = jnp.zeros((block, lanes), BF16)
    x_ref[x_ref.shape[0] - block :] = jnp.zeros((block, lanes), BF16)
    for s in range(disp):
        g = di ^ s
        main = piece_refs[s][:half].astype(F32)
        rest = piece_refs[s][half:].astype(F32)
        for p in range(planes):
            value = [unpack(main, rest[:8], p * rows + r) for r in range(rows)]
            at = pl.multiple_of((g * planes + p + 1) * block, block)
            x_ref[pl.ds(at, block)] = jnp.concatenate(value, axis=0).astype(BF16)
        value = [unpack(rest[8 : 8 + 3 * group], rest[8 + 3 * group :], k) for k in range(6)]
        for h in range(2):
            prior = value[3 * h] + value[3 * h + 1] + value[3 * h + 2]
            for p in range(planes):
                prior_ref[g * planes + p, 2 + 2 * h : 4 + 2 * h] = prior[2 * p : 2 * p + 2]


def bands_body(dims, base1_ref, base2_ref, base3_ref, base4_ref, bias_ref, band1_ref, band2_ref, band3_ref, band4_ref, col_ref):
    planes, rows, chans, width, disp, space, cols, lanes = dims

    def band(base, groups, count, step, used):
        pieces = []
        for c in range(3):
            piece = base[c * groups : (c + 1) * groups]
            for r in range(count):
                pieces.append(right(piece, step * r))
        return jnp.concatenate(pieces, axis=0)[:, :used].astype(BF16)

    band1_ref[...] = band(base1_ref[...], chans, rows + 2, chans, band1_ref.shape[1])
    band2_ref[...] = band(base2_ref[...], 1, rows + 4, chans, band2_ref.shape[1])
    band3_ref[...] = band(base3_ref[...], chans, rows + 2, 1, band3_ref.shape[1])
    band4 = band(base4_ref[...], chans, rows, chans, band4_ref.shape[1])
    n = rows * chans
    to = lax.broadcasted_iota(jnp.int32, (3 * n, 3 * n), 0)
    at = lax.broadcasted_iota(jnp.int32, (3 * n, 3 * n), 1)
    source = (to // n) * n + (to % rows) * chans + (to % n) // rows
    band4_ref[...] = dot((at == source).astype(BF16), band4).astype(BF16)
    diag = lax.broadcasted_iota(jnp.int32, (chans, chans), 0) == lax.broadcasted_iota(
        jnp.int32, (chans, chans), 1
    )
    bias = jnp.sum(jnp.where(diag, bias_ref[...], 0.0), axis=1, keepdims=True)
    col_ref[...] = jnp.concatenate([jnp.broadcast_to(bias, (chans, 2 * lanes))] * (rows + 6), axis=0)


def main_body(dims, *refs):
    planes, rows, chans, width, disp, space, cols, lanes = dims
    xo_ref, za_ref, zb_ref, prior_in_ref, cot_in_ref, band1_ref, band2_ref, band3_ref, band4_ref, col_ref = refs[:10]
    back_refs = refs[10 : 10 + disp]
    xu_ref, xd_ref, h_ref, slope_ref, prior_ref, cot_ref, s_ref, pg_ref, v_ref = refs[10 + disp :]
    zi = lax.axis_index("space")
    di = lax.axis_index("disp")
    z_even = zi % 2 == 0
    count = planes * disp
    n = count * rows * chans
    block = rows * chans
    hr = (rows + 6) * chans
    gr = (rows + 2) * chans
    lr = rows + 4
    sr = 16
    two = 2 * lanes

    def place_rows(src, ref):
        main = src[: n // 2].astype(F32)
        rest = src[n // 2 : n // 2 + 8 * disp].astype(F32)
        side = planes * block // 2
        for k in range(count):
            s = k // planes
            p = k % planes
            value = [
                unpack(main[s * side : (s + 1) * side], rest[8 * s : 8 * s + 8], p * rows + r) for r in range(rows)
            ]
            at = pl.multiple_of(((di ^ s) * planes + p + 1) * block, block)
            ref[pl.ds(at, block)] = jnp.concatenate(value, axis=0).astype(BF16)

    for ref in (xu_ref, xd_ref):
        ref[:block] = jnp.zeros((block, lanes), BF16)
        ref[(count + 1) * block :] = jnp.zeros((block, lanes), BF16)
    h_ref[:hr] = jnp.zeros((hr, lanes), BF16)
    h_ref[(count + 1) * hr :] = jnp.zeros((hr, lanes), BF16)
    s_ref[...] = jnp.zeros(s_ref.shape, BF16)
    pg_ref[:gr] = jnp.zeros((gr, lanes), BF16)
    pg_ref[(count + 1) * gr :] = jnp.zeros((gr, lanes), BF16)
    prior_ref[...] = prior_in_ref[...]
    cot_ref[...] = cot_in_ref[...]
    half = 2 * planes

    def place(ok, first, one, other, ref, at8):
        def put(src):
            if src is None:
                ref[...] = jnp.zeros(ref.shape, BF16)
                for k in range(count):
                    prior_ref[k, at8 : at8 + 2] = jnp.zeros((2, lanes), F32)
                cot_ref[at8 : at8 + 2] = jnp.zeros((2, lanes), F32)
                return
            place_rows(src, ref)
            extra = src[n // 2 + 8 * disp :].astype(F32)
            used = -(-(3 * half * disp + 6) // 16) * 16
            value = [unpack(extra[: used // 2], extra[used // 2 :], k) for k in range(3 * disp + 1)]
            for s in range(disp):
                prior = value[3 * s] + value[3 * s + 1] + value[3 * s + 2]
                for p in range(planes):
                    prior_ref[(di ^ s) * planes + p, at8 : at8 + 2] = prior[2 * p : 2 * p + 2]
            cot = value[3 * disp]
            cot_ref[at8 : at8 + 2] = cot[:2] + cot[2:4] + cot[4:6]

        pl.when(ok & first)(lambda: put(one))
        pl.when(ok & jnp.logical_not(first))(lambda: put(other))
        pl.when(jnp.logical_not(ok))(lambda: put(None))

    place(zi > 0, z_even, zb_ref, za_ref, xu_ref, 0)
    place(zi < space - 1, z_even, za_ref, zb_ref, xd_ref, 2 + rows)

    def pair(ref, p, size, taken):
        return jnp.concatenate([ref[p * size : p * size + taken], ref[(p + 1) * size : (p + 1) * size + taken]], axis=1)

    lane = lax.broadcasted_iota(jnp.int32, (hr, two), 1) % lanes
    column = di * cols - 4 + lane
    row_at = zi * rows - 3 + lax.broadcasted_iota(jnp.int32, (hr, two), 0) // chans
    inside = ((row_at >= 0) & (row_at < space * rows) & (column >= 0) & (column < width)).astype(F32)
    band1 = band1_ref[...]
    bias = col_ref[...]
    yr = (rows + 2) * chans
    for p in range(0, count, 2):
        pre = []
        for at, (near, far) in ((0, (xu_ref, xo_ref)), (4 * chans, (xo_ref, xd_ref))):
            rhs = []
            for q in range(2):
                parts = []
                for k in range(p + q, p + q + 3):
                    parts += [near[k * block : (k + 1) * block], far[k * block : (k + 1) * block]]
                rhs.append(jnp.concatenate(parts, axis=0))
            y = dot(band1, jnp.concatenate(rhs, axis=1))
            skip = at // 2
            y = [y[c * yr + skip : (c + 1) * yr] for c in range(3)]
            pre.append(y[1] + shift_up(y[0]) + shift_down(y[2]))
        pre = jnp.concatenate(pre, axis=0) + bias
        sig = 0.5 * jnp.tanh(0.5 * pre) + 0.5
        hidden = (pre * sig * inside).astype(BF16)
        slope = (sig * (1.0 + pre * (1.0 - sig)) * inside)[2 * chans : hr - 2 * chans]
        for q in range(2):
            part = slice(q * lanes, (q + 1) * lanes)
            h_ref[(p + q + 1) * hr : (p + q + 2) * hr] = hidden[:, part]
            slope_ref[p + q] = slope[:, part]

    band2 = band2_ref[...]
    logits = []
    for p in range(0, count, 2):
        y = dot(band2, pair(h_ref, p, hr, 3 * hr))
        y = y[lr : 2 * lr] + shift_up(y[:lr]) + shift_down(y[2 * lr :])
        logits += [y[:, :lanes] + prior_ref[p], y[:, lanes:] + prior_ref[p + 1]]

    top = logits[0]
    for value in logits[1:]:
        top = jnp.maximum(top, value)
    summed = jnp.zeros((lr, lanes), F32)
    moment = jnp.zeros((lr, lanes), F32)
    weights = []
    for k, value in enumerate(logits):
        e = jnp.exp(value - top)
        weights.append(e)
        summed = summed + e
        moment = moment + e * ((k + 0.5) / count)
    disparity = moment / summed
    coef = cot_ref[...] / summed
    mine = lax.broadcasted_iota(jnp.int32, (lr, lanes), 1)
    mine = (mine >= 4) & (mine < 4 + cols)
    left2 = []
    for k in range(count):
        score = (coef * weights[k] * ((k + 0.5) / count - disparity)).astype(BF16)
        s_ref[(k + 1) * sr : (k + 1) * sr + lr] = score
        score = jnp.where(mine, score.astype(F32), 0.0)
        left2.append(jnp.concatenate([shift_down(score), score, shift_up(score)], axis=0).astype(BF16))

    band3 = band3_ref[...]
    mine = lax.broadcasted_iota(jnp.int32, (block, two), 1) % lanes
    mine = (mine >= 4) & (mine < 4 + cols)
    bias_sum = jnp.zeros((chans, two), F32)
    left1 = []
    for p in range(0, count, 2):
        y = dot(band3, pair(s_ref, p, sr, 3 * sr))
        hg = y[gr : 2 * gr] + shift_down(y[:gr]) + shift_up(y[2 * gr :])
        slope = jnp.concatenate([slope_ref[p], slope_ref[p + 1]], axis=1)
        pg = (hg * slope).astype(BF16)
        for q in range(2):
            pg_ref[(p + q + 1) * gr : (p + q + 2) * gr] = pg[:, q * lanes : (q + 1) * lanes]
        own = jnp.where(mine, pg.astype(F32)[chans : chans + block], 0.0)
        moved = (shift_down(own), own, shift_up(own))
        pieces = []
        for r in range(rows):
            part = slice(r * chans, (r + 1) * chans)
            bias_sum = bias_sum + own[part]
            pieces += [moved[c][part] for c in range(3)]
        left1.append(jnp.concatenate(pieces, axis=0).astype(BF16))

    inner = (rows + 4) * chans
    acc = None
    for p in range(0, count, 2):
        far = []
        for q in range(2):
            k = p + q
            parts = []
            for at in range(k * block, (k + 3) * block, block):
                parts += [
                    xu_ref[at + 2 * chans : at + block],
                    xo_ref[at : at + block],
                    xd_ref[at : at + block - 2 * chans],
                ]
            far.append(jnp.concatenate(parts + [h_ref[k * hr : (k + 3) * hr]], axis=0))
        side = jnp.concatenate([left2[p], left2[p + 1]], axis=1)
        side = jnp.concatenate([left1[p // 2], side, jnp.zeros((128 - 15 * chans, two), BF16)], axis=0)
        part = dot_t(jnp.concatenate(far, axis=1), side)
        acc = part if acc is None else acc + part

    def turned(at, amount):
        return pltpu.roll(acc[at : at + chans], amount % 128, 1)

    tap = 3 * chans
    blocks = [jnp.zeros((chans, 128), F32), jnp.zeros((chans, 128), F32)]
    lane_p = lax.broadcasted_iota(jnp.int32, (chans, 128), 1)
    for k in range(9):
        a, b = k // 3, k % 3
        to = tap * (k % 5)
        value = sum(turned(a * inner + (r + b + 1) * chans, to - tap * r) for r in range(rows))
        blocks[k // 5] = jnp.where((lane_p >= to) & (lane_p < to + tap), value, blocks[k // 5])
        base = 3 * inner + a * hr
        used = rows * tap
        if k < 8:
            value = sum(turned(base + (r + b) * chans, 96 + k - used - r) for r in range(2, 2 + rows))
            blocks[1] = jnp.where((lane_p >= 96) & (lane_p < 120) & (lane_p % 8 == k), value, blocks[1])
        else:
            for c in range(3):
                value = sum(turned(base + (r + b) * chans, 120 + c - used - lr * c - r) for r in range(2, 2 + rows))
                blocks[0] = jnp.where(lane_p == 120 + c, value, blocks[0])
    bias_sum = jnp.sum(bias_sum, axis=1, keepdims=True)
    blocks[1] = jnp.where(lane_p == 120, bias_sum, blocks[1])
    payload = jnp.concatenate(blocks, axis=0)
    shown = jnp.concatenate([disparity[2 : 2 + rows]] * 2, axis=0)
    shown = terms(shown, 2)
    shown = jnp.where(lax.broadcasted_iota(jnp.int32, shown[0].shape, 0) < rows, shown[0], shown[1])
    tail = jnp.concatenate(terms(payload, 2) + [shown], axis=0).astype(BF16)

    band4 = band4_ref[...]
    found = [None] * planes
    for p in range(0, count, 2):
        y = dot(band4, pair(pg_ref, p, gr, 3 * gr))
        y = y[block : 2 * block] + shift_down(y[:block]) + shift_up(y[2 * block :])
        for q in range(2):
            moved = y[:, q * lanes : (q + 1) * lanes]
            k = p + q
            found[k % planes] = moved
        if (p + 2) % planes == 0:
            near = jnp.concatenate(found[: planes // 2], axis=0)
            far = jnp.concatenate(found[planes // 2 :], axis=0)
            near = pltpu.roll(near, lanes - 4, 1)
            far = pltpu.roll(far, 60, 1)
            at = (p // planes) * (planes * block // 2)
            v_ref[at : at + planes * block // 2] = jnp.where(lanes_of(near) < 64, near, far).astype(BF16)
    size = planes * block // 2
    for s in range(disp):
        back_refs[s][:size] = v_ref[pl.ds(pl.multiple_of((di ^ s) * size, size), size)]
        back_refs[s][size:] = tail


def sum_body(chans, *refs):
    parts = refs[:-1]
    k = 2 * chans
    sums = []
    for r in parts:
        n = r.shape[0] - 2 * k - 8
        value = r[n:].astype(F32)
        sums.append(value[:k] + value[k : 2 * k])
    refs[-1][...] = tree_sum(sums)


def join_body(dims, *refs):
    planes, rows, chans, width, disp, space, cols, lanes = dims
    parts = refs[:disp]
    grad_ref, disp_ref = refs[disp:]
    di = lax.axis_index("disp")
    n = planes * rows * chans
    k = 4 * chans
    total = None
    for s in range(disp):
        j = di ^ s
        shown = parts[s][n // 2 + k :].astype(F32)
        shown = pltpu.roll(shown + pltpu.roll(shown, rows, 0), lanes - 4, 1)
        main = parts[s][: n // 2].astype(F32)
        value = jnp.concatenate([main, pltpu.roll(main, 64, 1), shown], axis=0)
        value = jnp.where(lanes_of(value) < cols, value, 0.0)
        value = jnp.concatenate([value, jnp.zeros((value.shape[0], width - lanes), F32)], axis=1)
        value = pltpu.roll(value, j * cols, 1)
        total = value if total is None else total + value
    disp_ref[...] = total[n : n + rows]
    grad = total[:n].astype(BF16)
    for p in range(planes):
        for i in range(chans):
            at = (p * chans + i) * rows
            grad_ref[i, p] = grad[at : at + rows]


def tree_sum(parts):
    while len(parts) > 1:
        parts = [parts[k] + parts[k + 1] for k in range(0, len(parts), 2)]
    return parts[0]


def finish_body(chans, scale, *refs):
    gw_ref, gb_ref, gs_ref = refs[-3:]
    total = tree_sum([r[...] for r in refs[:-3]]) * scale
    flat = [jnp.transpose(total[:chans]), jnp.transpose(total[chans:])]
    for k in range(9):
        a, b = k // 3, k % 3
        for c in range(3):
            at = 3 * chans * (k % 5) + chans * c
            gw_ref[a, b, c] = flat[k // 5][at : at + chans]
            at = 96 + k + 8 * c if k < 8 else 120 + c
            gs_ref[a, b, c : c + 1] = flat[1 if k < 8 else 0][at : at + 1]
    gb_ref[...] = flat[1][120:121]


def flipped(body, count):
    def run(*refs):
        return body(*refs[:count][::-1], *refs[count:])

    return run


def exchange(sends, axis):
    count = lax.axis_size(axis)
    return [sends[0]] + [
        lax.ppermute(sends[s], axis, [(i, i ^ s) for i in range(count)]) for s in range(1, count)
    ]


def shards(volume, w_first, b_first, w_second, prior_logits, cotangent):
    chans, planes, rows, width = volume.shape
    disp = lax.axis_size("disp")
    space = lax.axis_size("space")
    cols = width // disp
    lanes = -(-(cols + 8) // 128) * 128
    dims = (planes, rows, chans, width, disp, space, cols, lanes)
    count = planes * disp
    n = planes * rows * chans

    piece = n // 2 + 8 + 6 * planes + 8
    sends = call(
        functools.partial(split_body, dims),
        "split",
        [((piece, lanes), BF16, True)] * disp,
        volume, prior_logits,
        inside=False,
        scratch=[
            pltpu.VMEM((4 * planes, width), F32),
            pltpu.VMEM((disp, piece, lanes), BF16),
        ]
        + [pltpu.VMEM((n, 128), F32)] * (width // 128),
    )
    pieces = exchange(sends, "disp")

    hr = rows + 6
    base1 = jnp.transpose(w_first, (2, 3, 0, 1, 4)).astype(F32)
    base1 = jnp.pad(base1, ((0, 0), (0, 0), (0, 0), (0, rows + 1), (0, 0)))
    base1 = base1.reshape(3 * chans, 3 * (rows + 4) * chans)
    base1 = jnp.pad(base1, ((0, 0), (0, -base1.shape[1] % 128)))
    base2 = jnp.transpose(w_second, (2, 0, 1, 3)).astype(F32)
    base2 = jnp.pad(base2, ((0, 0), (0, 0), (0, hr - 3), (0, 0))).reshape(3, 3 * hr * chans)
    base2 = jnp.pad(base2, ((0, 5), (0, -base2.shape[1] % 128)))
    base3 = jnp.transpose(w_second[::-1, ::-1], (2, 3, 0, 1)).astype(F32)
    base3 = jnp.pad(base3, ((0, 0), (0, 0), (0, 0), (0, 16 - 3))).reshape(3 * chans, 3 * 16)
    base3 = jnp.pad(base3, ((0, 0), (0, 128 - base3.shape[1])))
    base4 = jnp.transpose(w_first[::-1, ::-1], (2, 4, 0, 1, 3)).astype(F32)
    base4 = jnp.pad(base4, ((0, 0), (0, 0), (0, 0), (0, rows - 1), (0, 0))).reshape(
        3 * chans, 3 * (rows + 2) * chans
    )
    base4 = jnp.pad(base4, ((0, 0), (0, -base4.shape[1] % 128)))
    bands = call(
        functools.partial(bands_body, dims),
        "bands",
        (
            ((3 * (rows + 2) * chans, 3 * (rows + 4) * chans), BF16, True),
            ((3 * (rows + 4), 3 * hr * chans), BF16, True),
            ((3 * (rows + 2) * chans, 3 * 16), BF16, True),
            ((3 * rows * chans, 3 * (rows + 2) * chans), BF16, True),
            ((hr * chans, 2 * lanes), F32, True),
        ),
        base1, base2, base3, base4, b_first[None, :],
    )

    extra = -(-(6 * count + 6) // 16) * 16
    sent = (n // 2 + 8) * disp + extra // 2 + 8 * -(-extra // 128)
    send_one, send_two = call(
        flipped(functools.partial(rows_body, dims), disp),
        "rows",
        (((sent, lanes), BF16, True), ((sent, lanes), BF16, True)),
        *pieces[::-1], cotangent,
        scratch=[pltpu.VMEM((2, extra - 6 * count, lanes), F32)],
    )
    mine = call(
        flipped(functools.partial(mine_body, dims), disp),
        "mine",
        (
            (((count + 2) * rows * chans, lanes), BF16, True),
            ((count, rows + 4, lanes), F32, True),
            ((rows + 4, lanes), F32, True),
        ),
        *pieces[::-1], cotangent,
    )
    z_one = lax.ppermute(send_one, "space", swap_pairs(space, 0))
    z_two = lax.ppermute(send_two, "space", swap_pairs(space, 1))

    tail = 4 * chans + 8
    backs = call(
        functools.partial(main_body, dims),
        "main",
        [((n // 2 + tail, lanes), BF16, True)] * disp,
        mine[0], z_one, z_two, *mine[1:], *bands,
        scratch=[
            pltpu.VMEM(((count + 2) * rows * chans, lanes), BF16),
            pltpu.VMEM(((count + 2) * rows * chans, lanes), BF16),
            pltpu.VMEM(((count + 2) * hr * chans, lanes), BF16),
            pltpu.VMEM((count, (rows + 2) * chans, lanes), F32),
            pltpu.VMEM((count, rows + 4, lanes), F32),
            pltpu.VMEM((rows + 4, lanes), F32),
            pltpu.VMEM(((count + 2) * 16, lanes), BF16),
            pltpu.VMEM(((count + 2) * (rows + 2) * chans, lanes), BF16),
            pltpu.VMEM((n // 2 * disp, lanes), BF16),
        ],
    )
    backs = exchange(backs, "disp")
    (pay,) = call(
        flipped(functools.partial(sum_body, chans), disp),
        "sum",
        (((2 * chans, lanes), F32, True),),
        *backs[::-1],
    )
    stages = radix_stages(space)
    for k, steps in enumerate(stages):
        parts = [pay] + [lax.ppermute(pay, "space", [(i, i ^ s) for i in range(space)]) for s in steps]
        if k < len(stages) - 1:
            pay = tree_sum(parts)

    volume_grad, disparity = call(
        flipped(functools.partial(join_body, dims), disp),
        "join",
        (((chans, planes, rows, width), BF16, False), ((rows, width), F32, False)),
        *backs[::-1],
    )

    scale = 16.0 / math.sqrt(planes * disp * rows * space * width)
    first_sum, bias_sum, second_sum = call(
        functools.partial(finish_body, chans, scale),
        "finish",
        (
            ((3, 3, 3, chans, chans), F32, False),
            ((1, chans), F32, False),
            ((3, 3, 3, chans), F32, False),
        ),
        *parts,
    )
    return (volume_grad, first_sum, bias_sum[0], second_sum, disparity)


def solution(mesh):
    return jax.shard_map(
        shards,
        mesh=mesh,
        in_specs=(
            P(None, "disp", ("groups", "space"), None),
            P(),
            P(),
            P(),
            P("disp", ("groups", "space"), None),
            P(("groups", "space"), None),
        ),
        out_specs=(
            P(None, "disp", ("groups", "space"), None),
            P(None, None, None, "groups", None),
            P("groups"),
            P(None, None, None, "groups"),
            P(("groups", "space"), None),
        ),
        check_vma=False,
    )
```
